32 devices in a mesh: groups: 2 (over y), space: 16 (over z, x, core).
Axes of the slice: x: 2, y: 2, z: 4, core: 2. Of those that a mesh axis runs over, the one named last changes fastest.
Arguments:
- coarse_input: bfloat16 [256, 16, 256], P('groups', 'space'), parts along dimension 0, may hold values from -6 to 6
- skip: bfloat16 [128, 32, 1024], P('groups', None, 'space'), parts along dimension 0, may hold values from -6 to 6
- cotangent: bfloat16 [128, 32, 1024], P('groups', 'space'), parts along dimension 0, may hold values from -6 to 6
- w_up: bfloat16 [8, 64, 128], replicated, may hold values from -0.5 to 0.5
- w_conv: bfloat16 [27, 64, 128], replicated, may hold values from -0.109375 to 0.109375
Outputs:
- activation: bfloat16 [128, 32, 1024], P('groups', 'space'), parts along dimension 0
- grad_input: bfloat16 [256, 16, 256], P('groups', 'space'), parts along dimension 0
- grad_skip: bfloat16 [128, 32, 1024], P('groups', None, 'space'), parts along dimension 0
- grad_w_up: float32 [16, 64, 128], P('groups'), parts along dimension 0
- grad_w_conv: float32 [54, 64, 128], P('groups'), parts along dimension 0
The draws below stay inside these ranges and needn't reach their ends.
There are 2 independent parts, one for each index of `groups`. The reference program is written for one: setup_inputs(seed, part) draws one part's arguments, and reference() takes and returns one part's arrays. A program takes and returns all parts, laid end to end along the dimension named above; an argument that names none is the same for every part. Nothing has to cross between parts.
All inputs are finite; a program needn't handle non-finite values.
Results may differ from the reference program's by a relative error of at most 0.012.
Values may be sent and summed in bfloat16 or wider, within the bound.
No kernel may reach another device: no remote copies, remote signals or barrier semaphores. Data moves between devices by JAX's collectives and lax.ppermute only.
A program may use at most 64 MiB of HBM per device.

```python
import math
import jax
import jax.numpy as jnp
from jax import lax

CIN = 128
CUP = 64
CSK = 64
COUT = 64
CCAT = 128
H = 8
W = 128
CDEP = 16
FD = 32


def steps_of(rng, extent, split, low, top_value):
    level = 1.0
    for dim, parts in split:
        draws = jax.random.uniform(jax.random.fold_in(jax.random.fold_in(rng, 6), dim), (parts,), jnp.float32, low / len(split), top_value / len(split))
        level = level * jnp.repeat(jnp.exp(draws), extent[dim] // parts).reshape((-1,) + (1,) * (len(extent) - 1 - dim))
    return level


def normal_values(rng, shape, deviation, most, shards=(), dtype=jnp.bfloat16):
    result = jax.random.normal(rng, shape, jnp.float32) * deviation
    if len(shards) > 0:
        result = steps_of(rng, shape, shards, -0.22, 0.18) * result
    return jnp.clip(result, min=-most, max=most).astype(dtype)


def setup_inputs(seed: int = 0, part: int = 0) -> dict:
    key_list = jax.random.split(jax.random.key(seed), 6)
    part_splits = jax.random.split(jax.random.fold_in(key_list[5], part), 6)
    return {
        "coarse_input": normal_values(part_splits[0], (CIN, CDEP, (H // 2) * (W // 2)), 1.0, 6.0, ((1, 16),)),
        "skip": normal_values(part_splits[1], (CSK, FD, H * W), 1.0, 6.0, ((2, 16),)),
        "cotangent": normal_values(part_splits[2], (COUT, FD, H * W), 1.0, 6.0, ((1, 16),)),
        "w_up": normal_values(key_list[3], (8, CUP, CIN), CIN ** -0.5, 0.5),
        "w_conv": normal_values(key_list[4], (27, COUT, CCAT), (27 * CCAT) ** -0.5, 0.109375),
    }


def upsample_ref(coarse, w_up, height, width):
    channels = coarse.shape[0]
    planes = coarse.shape[1]
    outputs = w_up.shape[1]
    terms = jnp.dot(w_up.reshape(8 * outputs, channels), coarse.reshape(channels, -1), preferred_element_type=jnp.float32)
    terms = terms.reshape(2, 2, 2, outputs, planes, height // 2, width // 2)
    terms = terms.transpose(3, 4, 0, 5, 1, 6, 2)
    return terms.reshape(outputs, 2 * planes, height, width).astype(jnp.bfloat16)

def pad_all(volume):
    return jnp.pad(volume, ((0, 0), (1, 1), (1, 1), (1, 1)))

def reference(coarse_input, skip, cotangent, w_up, w_conv):
    planes = FD
    height = H
    width = W
    upsampled = upsample_ref(coarse_input, w_up, height, width)
    joined = jnp.concatenate([upsampled, skip.reshape(CSK, planes, height, width)], 0)
    joined_pad = pad_all(joined)
    pre = jnp.zeros((COUT, planes * height * width), jnp.float32)
    for depth_tap in range(3):
        for row_tap in range(3):
            for col_tap in range(3):
                window = joined_pad[:, depth_tap:depth_tap + planes, row_tap:row_tap + height, col_tap:col_tap + width].reshape(CCAT, -1)
                pre = pre + jnp.dot(w_conv[9 * depth_tap + 3 * row_tap + col_tap], window, preferred_element_type=jnp.float32)
    gate = jax.nn.sigmoid(pre)
    activation = (pre * gate).astype(jnp.bfloat16)
    grad_pre = (cotangent.reshape(COUT, -1).astype(jnp.float32) * gate * (1.0 + pre * (1.0 - gate))).astype(jnp.bfloat16)
    grad_pad = pad_all(grad_pre.reshape(COUT, planes, height, width))
    grad_joined = jnp.zeros((CCAT, planes * height * width), jnp.float32)
    weight_terms = []
    flat_grad = grad_pre
    for depth_tap in range(3):
        for row_tap in range(3):
            for col_tap in range(3):
                tap = 9 * depth_tap + 3 * row_tap + col_tap
                window = grad_pad[:, 2 - depth_tap:2 - depth_tap + planes, 2 - row_tap:2 - row_tap + height, 2 - col_tap:2 - col_tap + width].reshape(COUT, -1)
                grad_joined = grad_joined + lax.dot_general(w_conv[tap], window, (((0,), (0,)), ((), ())), preferred_element_type=jnp.float32)
                source = joined_pad[:, depth_tap:depth_tap + planes, row_tap:row_tap + height, col_tap:col_tap + width].reshape(CCAT, -1)
                weight_terms.append(lax.dot_general(flat_grad, source, (((1,), (1,)), ((), ())), preferred_element_type=jnp.float32))
    grad_up = grad_joined[:CUP].astype(jnp.bfloat16)
    grad_skip = grad_joined[CUP:].astype(jnp.bfloat16).reshape(CSK, planes, height * width)
    arranged = grad_up.reshape(CUP, planes // 2, 2, height // 2, 2, width // 2, 2).transpose(2, 4, 6, 0, 1, 3, 5).reshape(8 * CUP, -1)
    grad_input = lax.dot_general(w_up.reshape(8 * CUP, CIN), arranged, (((0,), (0,)), ((), ())), preferred_element_type=jnp.float32)
    grad_input = grad_input.astype(jnp.bfloat16).reshape(CIN, planes // 2, -1)
    scale = 1.0 / math.sqrt(FD * H * W)
    grad_w_up = lax.dot_general(arranged, coarse_input.reshape(CIN, -1), (((1,), (1,)), ((), ())), preferred_element_type=jnp.float32)
    grad_w_up = grad_w_up.reshape(8, CUP, CIN) * scale
    grad_w_conv = jnp.stack(weight_terms, 0) * scale
    return (activation.reshape(COUT, planes, height * width), grad_input, grad_skip, grad_w_up, grad_w_conv)
```

```python
import functools
import math

import jax
import jax.numpy as jnp
from jax import lax
from jax.experimental import pallas as pl
from jax.experimental.pallas import tpu as pltpu

W = 128
AXIS = "space"
BF16 = jnp.bfloat16
F32 = jnp.float32
NT = (((1,), (1,)), ((), ()))


def mm(a, b):
    return jnp.dot(a, b, preferred_element_type=F32)


def one_hot(shape, cond):
    rows = lax.broadcasted_iota(jnp.int32, shape, 0)
    cols = lax.broadcasted_iota(jnp.int32, shape, 1)
    return jnp.where(cond(rows, cols), 1.0, 0.0).astype(BF16)


def row_taps(z, channels):
    zero = jnp.zeros((channels, W), F32)
    low = jnp.concatenate([zero, z[:channels, :-W]], axis=1)
    high = jnp.concatenate([z[2 * channels :, W:], zero], axis=1)
    return z[channels : 2 * channels] + low + high


def row_taps_back(z, channels):
    zero = jnp.zeros((channels, W), F32)
    low = jnp.concatenate([z[:channels, W:], zero], axis=1)
    high = jnp.concatenate([zero, z[2 * channels :, :-W]], axis=1)
    return z[channels : 2 * channels] + low + high


def up_kernel(own_ref, before_ref, after_ref, wup_ref, wf_ref, xu_ref, pre_ref, spread_ref):
    def pick(lane_in, col):
        tap, k, parity, lane = (col >> 9, (col >> 8) & 1, (col >> 7) & 1, col & 127)
        return ((lane_in >> 6) == parity) & (2 * (lane_in & 63) + k == lane + tap - 1)

    select = one_hot((128, 1536), pick)
    weights = jnp.concatenate(
        [jnp.concatenate([wup_ref[2 * ij], wup_ref[2 * ij + 1]], axis=1) for ij in range(4)], axis=0
    )
    for part, ref in enumerate((before_ref, own_ref, after_ref)):
        spread = [mm(ref[:, 128 * t : 128 * t + 128], select).astype(BF16) for t in range(2)]
        for tap in range(3):
            columns = []
            for h in range(4):
                at = 512 * tap + 128 * (h & 1)
                piece = spread[h >> 1]
                columns.append(
                    jnp.concatenate([piece[:, at : at + 128], piece[:, at + 256 : at + 384]], axis=0)
                )
            operand = jnp.concatenate(columns, axis=1)
            if part == 1 and tap == 1:
                spread_ref[...] = operand
            up = mm(weights, operand).astype(BF16)
            for i in range(2):
                for j in range(2):
                    at = (2 * part + i) * 192 + tap * 64
                    for h in range(4):
                        xu_ref[at : at + 64, (2 * h + j) * W : (2 * h + j + 1) * W] = up[
                            (2 * i + j) * 64 : (2 * i + j + 1) * 64, h * W : (h + 1) * W
                        ]
    for j in range(4):
        z = mm(wf_ref[...], xu_ref[j * 192 : j * 192 + 576, :])
        pre_ref[j * 64 : (j + 1) * 64, :] = row_taps(z, 64)


def main_kernel(
    scale,
    own_ref,
    before_ref,
    after_ref,
    cot_ref,
    cot_before_ref,
    cot_after_ref,
    xu_ref,
    pre_ref,
    spread_ref,
    wf_ref,
    wi_ref,
    wg_ref,
    act_ref,
    gi_ref,
    skip_ref,
    gw_ref,
    xs_ref,
    gs_ref,
):
    def pick(row, col):
        out = jnp.where(col >= 384, 1, 0)
        rest = col - 384 * out
        tap, lane = (rest >> 7, rest & 127)
        return (((row >> 6) & 1) == out) & ((row >> 7) * 64 + (row & 63) == lane + tap - 1)

    select = one_hot((256, 768), pick)
    for part, ref in enumerate((before_ref, own_ref, after_ref)):
        left = ref[:, 0].reshape(512, 128)
        right = ref[:, 1].reshape(512, 128)
        placed = mm(jnp.concatenate([left, right], axis=1), select).astype(BF16)
        for parity in range(2):
            for tap in range(3):
                at = (2 * part + parity) * 192 + tap * 64
                for h in range(8):
                    xs_ref[at : at + 64, h * W : (h + 1) * W] = placed[
                        h * 64 : (h + 1) * 64, (3 * parity + tap) * W : (3 * parity + tap + 1) * W
                    ]

    shift = one_hot((128, 256), lambda row, col: row == (col & 127) + 1 - 2 * (col >> 7))
    for j in range(4):
        z = mm(wf_ref[...], xs_ref[j * 192 : j * 192 + 576, :])
        pre = pre_ref[j * 64 : (j + 1) * 64, :] + row_taps(z, 64)
        gate = 1.0 / (1.0 + jnp.exp(-pre))
        if j == 0:
            cot = cot_before_ref[...]
        elif j == 3:
            cot = cot_after_ref[...]
        else:
            cot = cot_ref[:, (j - 1) * 1024 : j * 1024]
            act_ref[:, (j - 1) * 1024 : j * 1024] = (pre * gate).astype(BF16)
        grad = (cot.astype(F32) * gate * (1.0 + pre * (1.0 - gate))).astype(BF16)
        gs_ref[j * 192 + 64 : j * 192 + 128, :] = grad
        tall = jnp.concatenate([grad[:, h * W : (h + 1) * W] for h in range(8)], axis=0)
        moved = mm(tall, shift).astype(BF16)
        for tap in (0, 2):
            at = j * 192 + tap * 64
            for h in range(8):
                gs_ref[at : at + 64, h * W : (h + 1) * W] = moved[
                    h * 64 : (h + 1) * 64, (tap >> 1) * W : (tap >> 1) * W + W
                ]

    zero = jnp.zeros((64, W), BF16)
    grads = []
    for j in (1, 2):
        grad = gs_ref[j * 192 + 64 : j * 192 + 128, :]
        low = jnp.concatenate([grad[:, W:], zero], axis=1)
        high = jnp.concatenate([zero, grad[:, :-W]], axis=1)
        grads.append(jnp.concatenate([low, grad, high], axis=0))
    for a in range(3):
        total = None
        for j in (1, 2):
            pieces = []
            for tap in range(3):
                at = (j + a) * 192 + tap * 64
                pieces += [xu_ref[at : at + 64, :], xs_ref[at : at + 64, :]]
            term = lax.dot_general(
                grads[j - 1], jnp.concatenate(pieces, axis=0), NT, preferred_element_type=F32
            )
            total = term if total is None else total + term
        total = total * scale
        for b in range(3):
            for tap in range(3):
                at = (9 * a + 3 * b + tap) * 64
                gw_ref[at : at + 64, :] = total[b * 64 : (b + 1) * 64, tap * W : (tap + 1) * W]

    lower = lax.broadcasted_iota(jnp.int32, (64, W), 1) < 64
    ups = []
    skips = []
    for j in range(2):
        z = mm(wi_ref[...], gs_ref[j * 192 : j * 192 + 576, :])
        grad = row_taps_back(z, 128)
        ups.append(grad[:64].astype(BF16))
        skips.append(grad[64:])
    for h in range(8):
        first = skips[0][:, h * W : (h + 1) * W]
        second = skips[1][:, h * W : (h + 1) * W]
        skip_ref[2 * h] = jnp.where(lower, first, pltpu.roll(second, 64, 1)).astype(BF16)
        skip_ref[2 * h + 1] = jnp.where(lower, pltpu.roll(first, 64, 1), second).astype(BF16)

    tiles = []
    for h in range(4):
        tiles.append(
            jnp.concatenate(
                [ups[i][:, (2 * h + j) * W : (2 * h + j + 1) * W] for i in range(2) for j in range(2)],
                axis=0,
            )
        )
    grad_up = lax.dot_general(
        jnp.concatenate(tiles, axis=1), spread_ref[...], NT, preferred_element_type=F32
    )
    grad_up = grad_up * scale
    for ij in range(4):
        for k in range(2):
            at = (27 + 2 * ij + k) * 64
            gw_ref[at : at + 64, :] = grad_up[ij * 64 : (ij + 1) * 64, k * W : (k + 1) * W]
    gw_ref[35 * 64 :, :] = jnp.zeros((64, W), F32)

    def part_lanes(row, col):
        return ((row >> 7) == ((col >> 6) & 1)) & ((row & 127) == 2 * (col & 63) + (col >> 7))

    apart = one_hot((256, 256), part_lanes)
    halves = [
        mm(jnp.concatenate([tiles[2 * t], tiles[2 * t + 1]], axis=1), apart).astype(BF16) for t in range(2)
    ]
    operand = jnp.concatenate(
        [jnp.concatenate([half[:, k * W : (k + 1) * W] for half in halves], axis=1) for k in range(2)],
        axis=0,
    )
    gi_ref[...] = mm(wg_ref[...], operand).astype(BF16)


PARAMS = pltpu.CompilerParams(vmem_limit_bytes=56 << 20)


def reduce_weights(partial, n):
    me = lax.axis_index(AXIS)

    def swap(value, bit):
        return lax.ppermute(value, AXIS, [(i, i ^ bit) for i in range(n)])

    half, quarter = (1152, 288)
    core = me & 1
    quad = (me >> 1) & 3
    send = lax.dynamic_slice_in_dim(partial, (1 - core) * half, half, 0).astype(BF16)
    mine = lax.dynamic_slice_in_dim(partial, core * half, half, 0)
    summed = mine + swap(send, 1).astype(F32)
    rounded = summed.astype(BF16)
    total = lax.dynamic_slice_in_dim(summed, quad * quarter, quarter, 0)
    for bit in (1, 2, 3):
        piece = lax.dynamic_slice_in_dim(rounded, (quad ^ bit) * quarter, quarter, 0)
        total = total + swap(piece, 2 * bit).astype(F32)
    bit = 8
    while bit < n:
        own = total.astype(BF16)
        total = own.astype(F32) + swap(own, bit).astype(F32)
        bit *= 2
    own = total.astype(BF16)
    gathered = [own] + [swap(own, 2 * bit) for bit in (1, 2, 3)]
    mine = jnp.zeros((half, W), BF16)
    for bit, piece in enumerate(gathered):
        mine = lax.dynamic_update_slice_in_dim(mine, piece, (quad ^ bit) * quarter, 0)
    other = swap(mine, 1)
    first = jnp.where(core == 0, mine, other)
    second = jnp.where(core == 0, other, mine)
    return jnp.concatenate([first, second], axis=0).astype(F32)


def local(coarse_input, skip, cotangent, w_up, w_conv):
    n = lax.axis_size(AXIS)
    cells = cotangent.shape[2]
    planes = cotangent.shape[1]
    up = [(i, i + 1) for i in range(n - 1)]
    down = [(i + 1, i) for i in range(n - 1)]

    positions = skip.shape[2]
    sent = skip.reshape(64, n, 2 * positions).transpose(1, 0, 2)
    held = lax.all_to_all(sent, AXIS, split_axis=0, concat_axis=0, tiled=True)
    if positions != 64:
        held = held.reshape(n, 64, 2, positions).transpose(1, 2, 0, 3).reshape(64, 2, 16, 64)
        held = held.transpose(2, 0, 1, 3).reshape(16, 64, 128)
    coarse = coarse_input.reshape(128, 256)
    coarse_before = lax.ppermute(coarse, AXIS, up)
    coarse_after = lax.ppermute(coarse, AXIS, down)
    cot_before = lax.ppermute(cotangent[:, 1], AXIS, up)
    cot_after = lax.ppermute(cotangent[:, 0], AXIS, down)
    wc = w_conv.reshape(3, 3, 3, 64, 128)
    forward = wc.transpose(1, 3, 0, 2, 4)
    wf_up = forward[..., :64].reshape(192, 576)
    wf_skip = forward[..., 64:].reshape(192, 576)
    wi = wc[::-1].transpose(1, 4, 0, 2, 3).reshape(384, 576)
    wg = w_up.reshape(2, 2, 2, 64, 128).transpose(4, 2, 0, 1, 3).reshape(128, 512)

    vmem = pl.BlockSpec(memory_space=pltpu.VMEM)
    xu, pre, spread = pl.pallas_call(
        up_kernel,
        out_shape=(
            jax.ShapeDtypeStruct((1152, 1024), BF16),
            jax.ShapeDtypeStruct((256, 1024), F32),
            jax.ShapeDtypeStruct((256, 512), BF16),
        ),
        in_specs=[vmem] * 5,
        out_specs=(vmem,) * 3,
        compiler_params=PARAMS,
        name="upsample",
    )(coarse, coarse_before, coarse_after, w_up, wf_up)

    held_before = lax.ppermute(held, AXIS, up)
    held_after = lax.ppermute(held, AXIS, down)
    scale = 1.0 / math.sqrt(n * planes * cells)
    rows = [v.reshape(8, 2, 64, 128) for v in (held, held_before, held_after)]
    act, gi, skip_part, gw = pl.pallas_call(
        functools.partial(main_kernel, scale),
        out_shape=(
            jax.ShapeDtypeStruct((64, 2048), BF16),
            jax.ShapeDtypeStruct((128, 256), BF16),
            jax.ShapeDtypeStruct((16, 64, 128), BF16),
            jax.ShapeDtypeStruct((2304, 128), F32),
        ),
        in_specs=[vmem] * 12,
        out_specs=(vmem,) * 4,
        scratch_shapes=[pltpu.VMEM((1152, 1024), BF16), pltpu.VMEM((768, 1024), BF16)],
        compiler_params=PARAMS,
        name="section",
    )(
        *rows,
        cotangent.reshape(64, 2048),
        cot_before,
        cot_after,
        xu,
        pre,
        spread,
        wf_skip,
        wi,
        wg,
    )
    summed = reduce_weights(gw, n)
    if positions != 64:
        skip_part = skip_part.reshape(16, 64, 2, 64).transpose(1, 2, 0, 3)
        skip_part = skip_part.reshape(64, 2, n, positions).transpose(2, 0, 1, 3)
        skip_part = skip_part.reshape(n, 64, 2 * positions)
    back = lax.all_to_all(skip_part, AXIS, split_axis=0, concat_axis=0, tiled=True)
    grad_skip = back.transpose(1, 0, 2).reshape(64, 2 * n, positions)
    return (
        act.reshape(64, planes, cells),
        gi.reshape(128, 1, 256),
        grad_skip,
        summed[27 * 64 : 35 * 64].reshape(8, 64, 128),
        summed[: 27 * 64].reshape(27, 64, 128),
    )


def solution(mesh):
    spec = jax.sharding.PartitionSpec
    in_specs = (
        spec("groups", "space", None),
        spec("groups", None, "space"),
        spec("groups", "space", None),
        spec(),
        spec(),
    )
    out_specs = (
        spec("groups", "space", None),
        spec("groups", "space", None),
        spec("groups", None, "space"),
        spec("groups", None, None),
        spec("groups", None, None),
    )
    return jax.shard_map(local, mesh=mesh, in_specs=in_specs, out_specs=out_specs, check_vma=False)
```

```python
import functools
import math

import jax
import jax.numpy as jnp
from jax import lax
from jax.experimental import pallas as pl
from jax.experimental.pallas import tpu as pltpu

W = 128
AXIS = "space"
BF16 = jnp.bfloat16
F32 = jnp.float32
NT = (((1,), (1,)), ((), ()))


def mm(a, b):
    return jnp.dot(a, b, preferred_element_type=F32)


def one_hot(shape, cond):
    rows = lax.broadcasted_iota(jnp.int32, shape, 0)
    cols = lax.broadcasted_iota(jnp.int32, shape, 1)
    return jnp.where(cond(rows, cols), 1.0, 0.0).astype(BF16)


def row_taps(z, channels):
    zero = jnp.zeros((channels, W), F32)
    low = jnp.concatenate([zero, z[:channels, :-W]], axis=1)
    high = jnp.concatenate([z[2 * channels :, W:], zero], axis=1)
    return z[channels : 2 * channels] + low + high


def row_taps_back(z, channels):
    zero = jnp.zeros((channels, W), F32)
    low = jnp.concatenate([z[:channels, W:], zero], axis=1)
    high = jnp.concatenate([zero, z[2 * channels :, :-W]], axis=1)
    return z[channels : 2 * channels] + low + high


def spread_columns():
    def pick(lane_in, col):
        tap, k, parity, lane = (col >> 9, (col >> 8) & 1, (col >> 7) & 1, col & 127)
        return ((lane_in >> 6) == parity) & (2 * (lane_in & 63) + k == lane + tap - 1)

    return one_hot((128, 1536), pick)


def up_weights(wup_ref):
    return jnp.concatenate(
        [jnp.concatenate([wup_ref[2 * ij], wup_ref[2 * ij + 1]], axis=1) for ij in range(4)], axis=0
    )


def upsample(coarse_ref, weights, select, xu_ref, base, spread_ref=None):
    spread = [mm(coarse_ref[:, 128 * t : 128 * t + 128], select).astype(BF16) for t in range(2)]
    for tap in range(3):
        columns = []
        for h in range(4):
            at = 512 * tap + 128 * (h & 1)
            piece = spread[h >> 1]
            columns.append(jnp.concatenate([piece[:, at : at + 128], piece[:, at + 256 : at + 384]], axis=0))
        operand = jnp.concatenate(columns, axis=1)
        if spread_ref is not None and tap == 1:
            spread_ref[...] = operand
        up = mm(weights, operand).astype(BF16)
        for i in range(2):
            for j in range(2):
                at = base + i * 192 + tap * 64
                for h in range(4):
                    xu_ref[at : at + 64, (2 * h + j) * W : (2 * h + j + 1) * W] = up[
                        (2 * i + j) * 64 : (2 * i + j + 1) * 64, h * W : (h + 1) * W
                    ]


def prepare_kernel(own_ref, wup_ref, wc_ref, xu_ref, spread_ref, wfu_ref, wfs_ref, wi_ref, wg_ref):
    upsample(own_ref, up_weights(wup_ref), spread_columns(), xu_ref, 0, spread_ref)
    rows = []
    for b in range(3):
        taps = [wc_ref[9 * a + 3 * b + c] for a in range(3) for c in range(3)]
        rows.append(jnp.concatenate(taps + [jnp.zeros((64, 128), BF16)], axis=1))
    full = jnp.concatenate(rows, axis=0)
    for half, ref in enumerate((wfu_ref, wfs_ref)):
        select = one_hot((256, 128), lambda row, col: row == (col & 63) + 64 * half + 128 * (col >> 6))
        for m in range(5):
            part = mm(full[:, 256 * m : 256 * m + 256], select).astype(BF16)
            if m < 4:
                ref[:, 128 * m : 128 * m + 128] = part
            else:
                ref[:, 512:] = part[:, :64]
    for b in range(3):
        taps = [wc_ref[9 * (2 - jj) + 3 * b + c] for jj in range(3) for c in range(3)]
        wi_ref[b * 128 : (b + 1) * 128, :] = jnp.concatenate(taps, axis=0).T
    wg_ref[...] = jnp.concatenate([wup_ref[2 * ij + k] for k in range(2) for ij in range(4)], axis=0).T


def edge_kernel(before_ref, after_ref, wup_ref, xu_ref, wfu_ref, xb_ref, xa_ref, pre_ref):
    weights = up_weights(wup_ref)
    select = spread_columns()
    upsample(before_ref, weights, select, xb_ref, 0)
    upsample(after_ref, weights, select, xa_ref, 0)
    whole = (xb_ref, xu_ref, xa_ref)
    for j in range(4):
        planes = [whole[e >> 1][(e & 1) * 192 : (e & 1) * 192 + 192, :] for e in range(j, j + 3)]
        z = mm(wfu_ref[...], jnp.concatenate(planes, axis=0))
        pre_ref[j * 64 : (j + 1) * 64, :] = row_taps(z, 64)


def main_kernel(
    scale,
    index_ref,
    own_ref,
    before_ref,
    after_ref,
    cot_ref,
    edge_before_ref,
    edge_after_ref,
    wf_ref,
    far_xb_ref,
    far_xu_ref,
    far_xa_ref,
    far_pre_ref,
    far_spread_ref,
    far_wi_ref,
    far_wg_ref,
    act_ref,
    gi_ref,
    skip_ref,
    keep_ref,
    send_ref,
    xs_ref,
    gs_ref,
    gw_ref,
    xu_ref,
    pre_ref,
    spread_ref,
    wi_ref,
    wg_ref,
    sems,
):
    pairs = (
        (far_pre_ref, pre_ref),
        (far_xb_ref, xu_ref.at[0:384]),
        (far_xu_ref, xu_ref.at[384:768]),
        (far_xa_ref, xu_ref.at[768:1152]),
        (far_wi_ref, wi_ref),
        (far_spread_ref, spread_ref),
        (far_wg_ref, wg_ref),
    )
    copies = [pltpu.make_async_copy(src, dst, sems.at[i]) for i, (src, dst) in enumerate(pairs)]
    for copy in copies:
        copy.start()

    def pick(row, col):
        out = jnp.where(col >= 384, 1, 0)
        rest = col - 384 * out
        tap, lane = (rest >> 7, rest & 127)
        return (((row >> 6) & 1) == out) & ((row >> 7) * 64 + (row & 63) == lane + tap - 1)

    select = one_hot((256, 768), pick)
    for part, ref in enumerate((before_ref, own_ref, after_ref)):
        left = ref[:, 0].reshape(512, 128)
        right = ref[:, 1].reshape(512, 128)
        placed = mm(jnp.concatenate([left, right], axis=1), select).astype(BF16)
        for parity in range(2):
            for tap in range(3):
                at = (2 * part + parity) * 192 + tap * 64
                for h in range(8):
                    xs_ref[at : at + 64, h * W : (h + 1) * W] = placed[
                        h * 64 : (h + 1) * 64, (3 * parity + tap) * W : (3 * parity + tap + 1) * W
                    ]

    copies[0].wait()
    shift = one_hot((128, 256), lambda row, col: row == (col & 127) + 1 - 2 * (col >> 7))
    for j in range(4):
        z = mm(wf_ref[...], xs_ref[j * 192 : j * 192 + 576, :])
        pre = pre_ref[j * 64 : (j + 1) * 64, :] + row_taps(z, 64)
        gate = 1.0 / (1.0 + jnp.exp(-pre))
        if j == 0:
            cot = jnp.concatenate([edge_before_ref[:64, 256:], edge_before_ref[64:, 256:]], axis=1)
        elif j == 3:
            cot = jnp.concatenate([edge_after_ref[:64, 256:], edge_after_ref[64:, 256:]], axis=1)
        else:
            cot = cot_ref[:, (j - 1) * 1024 : j * 1024]
            act_ref[:, (j - 1) * 1024 : j * 1024] = (pre * gate).astype(BF16)
        grad = (cot.astype(F32) * gate * (1.0 + pre * (1.0 - gate))).astype(BF16)
        gs_ref[j * 192 + 64 : j * 192 + 128, :] = grad
        tall = jnp.concatenate([grad[:, h * W : (h + 1) * W] for h in range(8)], axis=0)
        moved = mm(tall, shift).astype(BF16)
        for tap in (0, 2):
            at = j * 192 + tap * 64
            for h in range(8):
                gs_ref[at : at + 64, h * W : (h + 1) * W] = moved[
                    h * 64 : (h + 1) * 64, (tap >> 1) * W : (tap >> 1) * W + W
                ]

    zero = jnp.zeros((64, W), BF16)
    grads = []
    for j in (1, 2):
        grad = gs_ref[j * 192 + 64 : j * 192 + 128, :]
        low = jnp.concatenate([grad[:, W:], zero], axis=1)
        high = jnp.concatenate([zero, grad[:, :-W]], axis=1)
        grads.append(jnp.concatenate([low, grad, high], axis=0))
    for copy in copies[1:4]:
        copy.wait()
    for a in range(3):
        total = None
        for j in (1, 2):
            pieces = []
            for tap in range(3):
                at = (j + a) * 192 + tap * 64
                pieces += [xu_ref[at : at + 64, :], xs_ref[at : at + 64, :]]
            term = lax.dot_general(
                grads[j - 1], jnp.concatenate(pieces, axis=0), NT, preferred_element_type=F32
            )
            total = term if total is None else total + term
        total = total * scale
        for b in range(3):
            for tap in range(3):
                at = (9 * a + 3 * b + tap) * 64
                gw_ref[at : at + 64, :] = total[b * 64 : (b + 1) * 64, tap * W : (tap + 1) * W]

    for copy in copies[4:]:
        copy.wait()
    lower = lax.broadcasted_iota(jnp.int32, (64, W), 1) < 64
    ups = []
    skips = []
    for j in range(2):
        z = mm(wi_ref[...], gs_ref[j * 192 : j * 192 + 576, :])
        grad = row_taps_back(z, 128)
        ups.append(grad[:64].astype(BF16))
        skips.append(grad[64:])
    for h in range(8):
        first = skips[0][:, h * W : (h + 1) * W]
        second = skips[1][:, h * W : (h + 1) * W]
        skip_ref[2 * h] = jnp.where(lower, first, pltpu.roll(second, 64, 1)).astype(BF16)
        skip_ref[2 * h + 1] = jnp.where(lower, pltpu.roll(first, 64, 1), second).astype(BF16)

    tiles = []
    for h in range(4):
        tiles.append(
            jnp.concatenate(
                [ups[i][:, (2 * h + j) * W : (2 * h + j + 1) * W] for i in range(2) for j in range(2)],
                axis=0,
            )
        )
    grad_up = lax.dot_general(
        jnp.concatenate(tiles, axis=1), spread_ref[...], NT, preferred_element_type=F32
    )
    grad_up = grad_up * scale
    for ij in range(4):
        for k in range(2):
            at = (27 + 2 * ij + k) * 64
            gw_ref[at : at + 64, :] = grad_up[ij * 64 : (ij + 1) * 64, k * W : (k + 1) * W]
    gw_ref[35 * 64 :, :] = jnp.zeros((64, W), F32)

    def part_lanes(row, col):
        return ((row >> 7) == ((col >> 6) & 1)) & ((row & 127) == 2 * (col & 63) + (col >> 7))

    apart = one_hot((256, 256), part_lanes)
    halves = [
        mm(jnp.concatenate([tiles[2 * t], tiles[2 * t + 1]], axis=1), apart).astype(BF16) for t in range(2)
    ]
    operand = jnp.concatenate(
        [jnp.concatenate([half[:, k * W : (k + 1) * W] for half in halves], axis=1) for k in range(2)],
        axis=0,
    )
    gi_ref[...] = mm(wg_ref[...], operand).astype(BF16)

    core = index_ref[0]
    quad = index_ref[1]
    for k in range(4):
        row = jnp.bitwise_xor(quad, k) * 288
        mine = pl.multiple_of(core * 1152 + row, 32)
        other = pl.multiple_of((1 - core) * 1152 + row, 32)
        keep_ref[k * 288 : (k + 1) * 288, :] = gw_ref[pl.ds(mine, 288), :]
        send_ref[k * 288 : (k + 1) * 288, :] = gw_ref[pl.ds(other, 288), :].astype(BF16)


def finish_kernel(index_ref, mine_ref, other_ref, conv_ref, up_ref):
    core = index_ref[0]
    quad = index_ref[1]
    for side, ref in ((core, mine_ref), (1 - core, other_ref)):
        for k in range(4):
            piece = 4 * side + jnp.bitwise_xor(quad, k)
            rows = slice(k * 288, (k + 1) * 288)

            @pl.when(piece < 6)
            def _():
                conv_ref[pl.ds(piece * 9, 9)] = ref[rows, :].astype(F32).reshape(9, 32, 128)

            @pl.when(piece == 6)
            def _():
                up_ref[0:9] = ref[rows, :].astype(F32).reshape(9, 32, 128)

            @pl.when(piece == 7)
            def _():
                up_ref[9:16] = ref[k * 288 : k * 288 + 224, :].astype(F32).reshape(7, 32, 128)


def room(mebibytes):
    return pltpu.CompilerParams(vmem_limit_bytes=mebibytes << 20)


VMEM = pl.BlockSpec(memory_space=pltpu.VMEM)
SMEM = pl.BlockSpec(memory_space=pltpu.SMEM)
FAR = pl.BlockSpec(memory_space=pl.ANY)


def like(shape, dtype=BF16):
    return jax.ShapeDtypeStruct(shape, dtype)


def reduce_weights(index, keep, send, back, finish_others, n):
    def swap(value, bit):
        return lax.ppermute(value, AXIS, [(i, i ^ bit) for i in range(n)])

    summed = keep + swap(send, 1).astype(F32)
    rounded = summed.astype(BF16)
    total = summed[:288]
    for k in (1, 2, 3):
        total = total + swap(rounded[k * 288 : (k + 1) * 288], 2 * k).astype(F32)
    total, back = lax.optimization_barrier((total, back))
    bit = 8
    while bit < n:
        own = total.astype(BF16)
        total = own.astype(F32) + swap(own, bit).astype(F32)
        bit *= 2
    own = total.astype(BF16)
    pieces = [own] + [swap(own, 2 * k) for k in (1, 2, 3)]
    pieces, others = lax.optimization_barrier((pieces, finish_others(back)))
    mine = jnp.concatenate(pieces, axis=0)
    other = swap(mine, 1)
    conv, up = pl.pallas_call(
        finish_kernel,
        out_shape=(like((54, 32, 128), F32), like((16, 32, 128), F32)),
        in_specs=[SMEM, VMEM, VMEM],
        out_specs=(VMEM, VMEM),
        compiler_params=room(6),
        name="finish",
    )(index, mine, other)
    return conv.reshape(27, 64, 128), up.reshape(8, 64, 128), others


def local(coarse_input, skip, cotangent, w_up, w_conv):
    n = lax.axis_size(AXIS)
    cells = cotangent.shape[2]
    planes = cotangent.shape[1]
    positions = skip.shape[2]
    up = [(i, i + 1) for i in range(n - 1)]
    down = [(i + 1, i) for i in range(n - 1)]
    me = lax.axis_index(AXIS)
    index = jnp.stack([me & 1, (me >> 1) & 3]).astype(jnp.int32)

    sent = skip.reshape(64, n, 2 * positions).transpose(1, 0, 2)
    held = lax.all_to_all(sent, AXIS, split_axis=0, concat_axis=0, tiled=True)
    if positions != 64:
        held = held.reshape(n, 64, 2, positions).transpose(1, 2, 0, 3).reshape(64, 2, 16, 64)
        held = held.transpose(2, 0, 1, 3).reshape(16, 64, 128)

    coarse = coarse_input.reshape(128, 256)
    flat = lax.optimization_barrier(cotangent.reshape(64, 2048))

    def edge(plane):
        halves = [flat[:, 1024 * plane + 512 * i : 1024 * plane + 512 * (i + 1)] for i in range(2)]
        return jnp.concatenate([coarse, jnp.concatenate(halves, axis=0)], axis=1)

    edge_before = lax.ppermute(edge(1), AXIS, up)
    edge_after = lax.ppermute(edge(0), AXIS, down)
    xu, spread, wf_up, wf_skip, wi, wg = pl.pallas_call(
        prepare_kernel,
        out_shape=(
            like((384, 1024)),
            like((256, 512)),
            like((192, 576)),
            like((192, 576)),
            like((384, 576)),
            like((128, 512)),
        ),
        in_specs=[VMEM] * 3,
        out_specs=(VMEM,) * 6,
        compiler_params=room(8),
        name="prepare",
    )(coarse, w_up, w_conv)
    held, wf_up, edge_before, edge_after = lax.optimization_barrier((held, wf_up, edge_before, edge_after))
    held_before = lax.ppermute(held, AXIS, up)
    held_after = lax.ppermute(held, AXIS, down)
    xb, xa, pre = pl.pallas_call(
        edge_kernel,
        out_shape=(like((384, 1024)), like((384, 1024)), like((256, 1024), F32)),
        in_specs=[VMEM] * 5,
        out_specs=(VMEM,) * 3,
        compiler_params=room(16),
        name="edges",
    )(edge_before, edge_after, w_up, xu, wf_up)

    scale = 1.0 / math.sqrt(n * planes * cells)
    rows = [v.reshape(8, 2, 64, 128) for v in (held, held_before, held_after)]
    act, gi, skip_part, keep, send = pl.pallas_call(
        functools.partial(main_kernel, scale),
        out_shape=(
            like((64, 2048)),
            like((128, 256)),
            like((16, 64, 128)),
            like((1152, 128), F32),
            like((1152, 128)),
        ),
        in_specs=[SMEM] + [VMEM] * 7 + [FAR] * 7,
        out_specs=(VMEM,) * 5,
        scratch_shapes=[
            pltpu.VMEM((1152, 1024), BF16),
            pltpu.VMEM((768, 1024), BF16),
            pltpu.VMEM((2304, 128), F32),
            pltpu.VMEM((1152, 1024), BF16),
            pltpu.VMEM((256, 1024), F32),
            pltpu.VMEM((256, 512), BF16),
            pltpu.VMEM((384, 576), BF16),
            pltpu.VMEM((128, 512), BF16),
            pltpu.SemaphoreType.DMA((7,)),
        ],
        compiler_params=room(24),
        name="section",
    )(index, *rows, flat, edge_before, edge_after, wf_skip, xb, xu, xa, pre, spread, wi, wg)
    if positions != 64:
        skip_part = skip_part.reshape(16, 64, 2, 64).transpose(1, 2, 0, 3)
        skip_part = skip_part.reshape(64, 2, n, positions).transpose(2, 0, 1, 3)
        skip_part = skip_part.reshape(n, 64, 2 * positions)
    back = lax.all_to_all(skip_part, AXIS, split_axis=0, concat_axis=0, tiled=True)

    def others(back):
        return (
            act.reshape(64, planes, cells),
            gi.reshape(128, 1, 256),
            back.transpose(1, 0, 2).reshape(64, 2 * n, positions),
        )

    grad_w_conv, grad_w_up, rest = reduce_weights(index, keep, send, back, others, n)
    return (*rest, grad_w_up, grad_w_conv)


def solution(mesh):
    spec = jax.sharding.PartitionSpec
    in_specs = (
        spec("groups", "space", None),
        spec("groups", None, "space"),
        spec("groups", "space", None),
        spec(),
        spec(),
    )
    out_specs = (
        spec("groups", "space", None),
        spec("groups", "space", None),
        spec("groups", None, "space"),
        spec("groups", None, None),
        spec("groups", None, None),
    )
    return jax.shard_map(local, mesh=mesh, in_specs=in_specs, out_specs=out_specs, check_vma=False)
```

```python
import functools
import math

import jax
import jax.numpy as jnp
from jax import lax
from jax.experimental import pallas as pl
from jax.experimental.pallas import tpu as pltpu

W = 128
AXIS = "space"
BF16 = jnp.bfloat16
F32 = jnp.float32
NT = (((1,), (1,)), ((), ()))


def mm(a, b):
    return jnp.dot(a, b, preferred_element_type=F32)


def one_hot(shape, cond):
    rows = lax.broadcasted_iota(jnp.int32, shape, 0)
    cols = lax.broadcasted_iota(jnp.int32, shape, 1)
    return jnp.where(cond(rows, cols), 1.0, 0.0).astype(BF16)


def row_taps(z, channels):
    zero = jnp.zeros((channels, W), F32)
    low = jnp.concatenate([zero, z[:channels, :-W]], axis=1)
    high = jnp.concatenate([z[2 * channels :, W:], zero], axis=1)
    return z[channels : 2 * channels] + low + high


def row_taps_back(z, channels):
    zero = jnp.zeros((channels, W), F32)
    low = jnp.concatenate([z[:channels, W:], zero], axis=1)
    high = jnp.concatenate([zero, z[2 * channels :, :-W]], axis=1)
    return z[channels : 2 * channels] + low + high


def spread_columns():
    def pick(lane_in, col):
        tap, k, parity, lane = (col >> 9, (col >> 8) & 1, (col >> 7) & 1, col & 127)
        return ((lane_in >> 6) == parity) & (2 * (lane_in & 63) + k == lane + tap - 1)

    return one_hot((128, 1536), pick)


def up_weights(wup_ref):
    return jnp.concatenate(
        [jnp.concatenate([wup_ref[2 * ij], wup_ref[2 * ij + 1]], axis=1) for ij in range(4)], axis=0
    )


def upsample(coarse_ref, weights, select, xu_ref, base, spread_ref=None):
    spread = [mm(coarse_ref[:, 128 * t : 128 * t + 128], select).astype(BF16) for t in range(2)]
    for tap in range(3):
        columns = []
        for h in range(4):
            at = 512 * tap + 128 * (h & 1)
            piece = spread[h >> 1]
            columns.append(jnp.concatenate([piece[:, at : at + 128], piece[:, at + 256 : at + 384]], axis=0))
        operand = jnp.concatenate(columns, axis=1)
        if spread_ref is not None and tap == 1:
            spread_ref[...] = operand
        up = mm(weights, operand).astype(BF16)
        for i in range(2):
            for j in range(2):
                at = base + i * 192 + tap * 64
                for h in range(4):
                    xu_ref[at : at + 64, (2 * h + j) * W : (2 * h + j + 1) * W] = up[
                        (2 * i + j) * 64 : (2 * i + j + 1) * 64, h * W : (h + 1) * W
                    ]


def prepare_kernel(own_ref, wup_ref, wc_ref, xu_ref, spread_ref, wfu_ref, wfs_ref, wi_ref, wg_ref):
    upsample(own_ref, up_weights(wup_ref), spread_columns(), xu_ref, 0, spread_ref)
    rows = []
    for b in range(3):
        taps = [wc_ref[9 * a + 3 * b + c] for a in range(3) for c in range(3)]
        rows.append(jnp.concatenate(taps + [jnp.zeros((64, 128), BF16)], axis=1))
    full = jnp.concatenate(rows, axis=0)
    for half, ref in enumerate((wfu_ref, wfs_ref)):
        select = one_hot((256, 128), lambda row, col: row == (col & 63) + 64 * half + 128 * (col >> 6))
        for m in range(5):
            part = mm(full[:, 256 * m : 256 * m + 256], select).astype(BF16)
            if m < 4:
                ref[:, 128 * m : 128 * m + 128] = part
            else:
                ref[:, 512:] = part[:, :64]
    for b in range(3):
        taps = [wc_ref[9 * (2 - jj) + 3 * b + c] for jj in range(3) for c in range(3)]
        wi_ref[b * 128 : (b + 1) * 128, :] = jnp.concatenate(taps, axis=0).T
    wg_ref[...] = jnp.concatenate([wup_ref[2 * ij + k] for k in range(2) for ij in range(4)], axis=0).T


def edge_kernel(
    before_ref,
    after_ref,
    wup_ref,
    own_ref,
    far_wfu_ref,
    far_wfs_ref,
    far_wg_ref,
    xu_ref,
    pre_ref,
    wfs_ref,
    wg_ref,
    wfu_ref,
    sems,
):
    pairs = (
        (own_ref, xu_ref.at[384:768]),
        (far_wfu_ref, wfu_ref),
        (far_wfs_ref, wfs_ref),
        (far_wg_ref, wg_ref),
    )
    copies = [pltpu.make_async_copy(src, dst, sems.at[i]) for i, (src, dst) in enumerate(pairs)]
    for copy in copies:
        copy.start()
    weights = up_weights(wup_ref)
    select = spread_columns()
    upsample(before_ref, weights, select, xu_ref, 0)
    upsample(after_ref, weights, select, xu_ref, 768)
    for copy in copies:
        copy.wait()
    for j in range(4):
        z = mm(wfu_ref[...], xu_ref[j * 192 : j * 192 + 576, :])
        pre_ref[j * 64 : (j + 1) * 64, :] = row_taps(z, 64)


def main_kernel(
    scale,
    index_ref,
    own_ref,
    before_ref,
    after_ref,
    cot_ref,
    edge_before_ref,
    edge_after_ref,
    xu_ref,
    pre_ref,
    spread_ref,
    wi_ref,
    wf_ref,
    wg_ref,
    act_ref,
    gi_ref,
    skip_ref,
    keep_ref,
    send_ref,
    xs_ref,
    gs_ref,
    gw_ref,
):
    def pick(row, col):
        out = jnp.where(col >= 384, 1, 0)
        rest = col - 384 * out
        tap, lane = (rest >> 7, rest & 127)
        return (((row >> 6) & 1) == out) & ((row >> 7) * 64 + (row & 63) == lane + tap - 1)

    select = one_hot((256, 768), pick)
    for part, ref in enumerate((before_ref, own_ref, after_ref)):
        left = ref[:, 0].reshape(512, 128)
        right = ref[:, 1].reshape(512, 128)
        placed = mm(jnp.concatenate([left, right], axis=1), select).astype(BF16)
        for parity in range(2):
            for tap in range(3):
                at = (2 * part + parity) * 192 + tap * 64
                for h in range(8):
                    xs_ref[at : at + 64, h * W : (h + 1) * W] = placed[
                        h * 64 : (h + 1) * 64, (3 * parity + tap) * W : (3 * parity + tap + 1) * W
                    ]

    shift = one_hot((128, 256), lambda row, col: row == (col & 127) + 1 - 2 * (col >> 7))
    for j in range(4):
        z = mm(wf_ref[...], xs_ref[j * 192 : j * 192 + 576, :])
        pre = pre_ref[j * 64 : (j + 1) * 64, :] + row_taps(z, 64)
        gate = 1.0 / (1.0 + jnp.exp(-pre))
        if j == 0:
            cot = jnp.concatenate([edge_before_ref[:64, 256:], edge_before_ref[64:, 256:]], axis=1)
        elif j == 3:
            cot = jnp.concatenate([edge_after_ref[:64, 256:], edge_after_ref[64:, 256:]], axis=1)
        else:
            cot = cot_ref[:, (j - 1) * 1024 : j * 1024]
            act_ref[:, (j - 1) * 1024 : j * 1024] = (pre * gate).astype(BF16)
        grad = (cot.astype(F32) * gate * (1.0 + pre * (1.0 - gate))).astype(BF16)
        gs_ref[j * 192 + 64 : j * 192 + 128, :] = grad
        tall = jnp.concatenate([grad[:, h * W : (h + 1) * W] for h in range(8)], axis=0)
        moved = mm(tall, shift).astype(BF16)
        for tap in (0, 2):
            at = j * 192 + tap * 64
            for h in range(8):
                gs_ref[at : at + 64, h * W : (h + 1) * W] = moved[
                    h * 64 : (h + 1) * 64, (tap >> 1) * W : (tap >> 1) * W + W
                ]

    zero = jnp.zeros((64, W), BF16)
    grads = []
    for j in (1, 2):
        grad = gs_ref[j * 192 + 64 : j * 192 + 128, :]
        low = jnp.concatenate([grad[:, W:], zero], axis=1)
        high = jnp.concatenate([zero, grad[:, :-W]], axis=1)
        grads.append(jnp.concatenate([low, grad, high], axis=0))
    for a in range(3):
        total = None
        for j in (1, 2):
            pieces = []
            for tap in range(3):
                at = (j + a) * 192 + tap * 64
                pieces += [xu_ref[at : at + 64, :], xs_ref[at : at + 64, :]]
            term = lax.dot_general(
                grads[j - 1], jnp.concatenate(pieces, axis=0), NT, preferred_element_type=F32
            )
            total = term if total is None else total + term
        total = total * scale
        for b in range(3):
            for tap in range(3):
                at = (9 * a + 3 * b + tap) * 64
                gw_ref[at : at + 64, :] = total[b * 64 : (b + 1) * 64, tap * W : (tap + 1) * W]

    lower = lax.broadcasted_iota(jnp.int32, (64, W), 1) < 64
    ups = []
    skips = []
    for j in range(2):
        z = mm(wi_ref[...], gs_ref[j * 192 : j * 192 + 576, :])
        grad = row_taps_back(z, 128)
        ups.append(grad[:64].astype(BF16))
        skips.append(grad[64:])
    for h in range(8):
        first = skips[0][:, h * W : (h + 1) * W]
        second = skips[1][:, h * W : (h + 1) * W]
        skip_ref[2 * h] = jnp.where(lower, first, pltpu.roll(second, 64, 1)).astype(BF16)
        skip_ref[2 * h + 1] = jnp.where(lower, pltpu.roll(first, 64, 1), second).astype(BF16)

    tiles = []
    for h in range(4):
        tiles.append(
            jnp.concatenate(
                [ups[i][:, (2 * h + j) * W : (2 * h + j + 1) * W] for i in range(2) for j in range(2)],
                axis=0,
            )
        )
    grad_up = lax.dot_general(
        jnp.concatenate(tiles, axis=1), spread_ref[...], NT, preferred_element_type=F32
    )
    grad_up = grad_up * scale
    for ij in range(4):
        for k in range(2):
            at = (27 + 2 * ij + k) * 64
            gw_ref[at : at + 64, :] = grad_up[ij * 64 : (ij + 1) * 64, k * W : (k + 1) * W]
    gw_ref[35 * 64 :, :] = jnp.zeros((64, W), F32)

    def part_lanes(row, col):
        return ((row >> 7) == ((col >> 6) & 1)) & ((row & 127) == 2 * (col & 63) + (col >> 7))

    apart = one_hot((256, 256), part_lanes)
    halves = [
        mm(jnp.concatenate([tiles[2 * t], tiles[2 * t + 1]], axis=1), apart).astype(BF16) for t in range(2)
    ]
    operand = jnp.concatenate(
        [jnp.concatenate([half[:, k * W : (k + 1) * W] for half in halves], axis=1) for k in range(2)],
        axis=0,
    )
    gi_ref[...] = mm(wg_ref[...], operand).astype(BF16)

    core = index_ref[0]
    quad = index_ref[1]
    for k in range(4):
        row = jnp.bitwise_xor(quad, k) * 288
        mine = pl.multiple_of(core * 1152 + row, 32)
        other = pl.multiple_of((1 - core) * 1152 + row, 32)
        keep_ref[k * 288 : (k + 1) * 288, :] = gw_ref[pl.ds(mine, 288), :]
        send_ref[k * 288 : (k + 1) * 288, :] = gw_ref[pl.ds(other, 288), :].astype(BF16)


def finish_kernel(index_ref, mine_ref, other_ref, conv_ref, up_ref):
    core = index_ref[0]
    quad = index_ref[1]
    for side, ref in ((core, mine_ref), (1 - core, other_ref)):
        for k in range(4):
            piece = 4 * side + jnp.bitwise_xor(quad, k)
            rows = slice(k * 288, (k + 1) * 288)

            @pl.when(piece < 6)
            def _():
                conv_ref[pl.ds(piece * 9, 9)] = ref[rows, :].astype(F32).reshape(9, 32, 128)

            @pl.when(piece == 6)
            def _():
                up_ref[0:9] = ref[rows, :].astype(F32).reshape(9, 32, 128)

            @pl.when(piece == 7)
            def _():
                up_ref[9:16] = ref[k * 288 : k * 288 + 224, :].astype(F32).reshape(7, 32, 128)


def room(mebibytes):
    return pltpu.CompilerParams(vmem_limit_bytes=mebibytes << 20)


VMEM = pl.BlockSpec(memory_space=pltpu.VMEM)
SMEM = pl.BlockSpec(memory_space=pltpu.SMEM)
FAR = pl.BlockSpec(memory_space=pl.ANY)


def far(value):
    return pltpu.with_memory_space_constraint(value, pltpu.HBM)


def near(value):
    return pltpu.with_memory_space_constraint(value, pltpu.VMEM)


def like(shape, dtype=BF16):
    return jax.ShapeDtypeStruct(shape, dtype)


def inside(shape, dtype=BF16):
    return pltpu.VMEM(shape, dtype)


def outside(shape, dtype=BF16):
    return pltpu.HBM(shape, dtype)


def reduce_weights(index, keep, send, back, finish_others, n):
    def swap(value, bit):
        return lax.ppermute(value, AXIS, [(i, i ^ bit) for i in range(n)])

    summed = keep + swap(send, 1).astype(F32)
    rounded = summed.astype(BF16)
    total = summed[:288]
    for k in (1, 2, 3):
        total = total + swap(rounded[k * 288 : (k + 1) * 288], 2 * k).astype(F32)
    total, back = lax.optimization_barrier((total, back))
    bit = 8
    while bit < n:
        own = total.astype(BF16)
        total = own.astype(F32) + swap(own, bit).astype(F32)
        bit *= 2
    own = total.astype(BF16)
    pieces = [own] + [swap(own, 2 * k) for k in (1, 2, 3)]
    pieces, others = lax.optimization_barrier((pieces, finish_others(back)))
    mine = jnp.concatenate(pieces, axis=0)
    other = swap(mine, 1)
    conv, up = pl.pallas_call(
        finish_kernel,
        out_shape=(like((54, 32, 128), F32), like((16, 32, 128), F32)),
        in_specs=[SMEM, VMEM, VMEM],
        out_specs=(VMEM, VMEM),
        compiler_params=room(6),
        cost_estimate=pl.CostEstimate(flops=1955000000, bytes_accessed=1000000, transcendentals=0),
        name="finish",
    )(index, mine, other)
    return conv.reshape(27, 64, 128), up.reshape(8, 64, 128), others


def local(coarse_input, skip, cotangent, w_up, w_conv):
    n = lax.axis_size(AXIS)
    cells = cotangent.shape[2]
    planes = cotangent.shape[1]
    positions = skip.shape[2]
    up = [(i, i + 1) for i in range(n - 1)]
    down = [(i + 1, i) for i in range(n - 1)]
    me = lax.axis_index(AXIS)
    index = jnp.stack([me & 1, (me >> 1) & 3]).astype(jnp.int32)

    sent = skip.reshape(64, n, 2 * positions).transpose(1, 0, 2)
    held = lax.all_to_all(sent, AXIS, split_axis=0, concat_axis=0, tiled=True)
    if positions != 64:
        held = held.reshape(n, 64, 2, positions).transpose(1, 2, 0, 3).reshape(64, 2, 16, 64)
        held = held.transpose(2, 0, 1, 3).reshape(16, 64, 128)

    coarse = coarse_input.reshape(128, 256)
    flat = lax.optimization_barrier(cotangent.reshape(64, 2048))

    def edge(plane):
        halves = [flat[:, 1024 * plane + 512 * i : 1024 * plane + 512 * (i + 1)] for i in range(2)]
        return jnp.concatenate([coarse, jnp.concatenate(halves, axis=0)], axis=1)

    edge_before = lax.ppermute(edge(1), AXIS, up)
    edge_after = lax.ppermute(edge(0), AXIS, down)
    xu, spread, wf_up, wf_skip, wi, wg = pl.pallas_call(
        prepare_kernel,
        out_shape=(
            inside((384, 1024)),
            inside((256, 512)),
            outside((192, 576)),
            outside((192, 576)),
            inside((384, 576)),
            outside((128, 512)),
        ),
        in_specs=[VMEM] * 3,
        out_specs=(VMEM,) * 6,
        compiler_params=room(8),
        cost_estimate=pl.CostEstimate(flops=1840000000, bytes_accessed=1000000, transcendentals=0),
        name="prepare",
    )(coarse, w_up, w_conv)
    held, wf_up = lax.optimization_barrier((held, wf_up))
    held_before = lax.ppermute(held, AXIS, up)
    held_after = lax.ppermute(held, AXIS, down)
    xu, pre, wf_skip, wg = pl.pallas_call(
        edge_kernel,
        out_shape=(
            inside((1152, 1024)),
            inside((256, 1024), F32),
            inside((192, 576)),
            inside((128, 512)),
        ),
        in_specs=[VMEM] * 4 + [FAR] * 3,
        out_specs=(VMEM,) * 4,
        scratch_shapes=[pltpu.VMEM((192, 576), BF16), pltpu.SemaphoreType.DMA((4,))],
        compiler_params=room(16),
        cost_estimate=pl.CostEstimate(flops=2990000000, bytes_accessed=1000000, transcendentals=0),
        name="edges",
    )(near(edge_before), near(edge_after), w_up, near(xu), far(wf_up), far(wf_skip), far(wg))

    scale = 1.0 / math.sqrt(n * planes * cells)
    rows = [v.reshape(8, 2, 64, 128) for v in (held, held_before, held_after)]
    act, gi, skip_part, keep, send = pl.pallas_call(
        functools.partial(main_kernel, scale),
        out_shape=(
            outside((64, 2048)),
            outside((128, 256)),
            outside((16, 64, 128)),
            inside((1152, 128), F32),
            inside((1152, 128)),
        ),
        in_specs=[SMEM] + [VMEM] * 12,
        out_specs=(VMEM,) * 5,
        scratch_shapes=[
            pltpu.VMEM((1152, 1024), BF16),
            pltpu.VMEM((768, 1024), BF16),
            pltpu.VMEM((2304, 128), F32),
        ],
        compiler_params=room(24),
        cost_estimate=pl.CostEstimate(flops=8280000000, bytes_accessed=1000000, transcendentals=0),
        name="section",
    )(index, *(near(v) for v in (*rows, flat, edge_before, edge_after, xu, pre, spread, wi, wf_skip, wg)))
    if positions != 64:
        skip_part = skip_part.reshape(16, 64, 2, 64).transpose(1, 2, 0, 3)
        skip_part = skip_part.reshape(64, 2, n, positions).transpose(2, 0, 1, 3)
        skip_part = skip_part.reshape(n, 64, 2 * positions)
    back = lax.all_to_all(skip_part, AXIS, split_axis=0, concat_axis=0, tiled=True)

    def others(back):
        return (
            act.reshape(64, planes, cells),
            gi.reshape(128, 1, 256),
            back.transpose(1, 0, 2).reshape(64, 2 * n, positions),
        )

    grad_w_conv, grad_w_up, rest = reduce_weights(index, keep, send, back, others, n)
    return (*rest, grad_w_up, grad_w_conv)


def solution(mesh):
    spec = jax.sharding.PartitionSpec
    in_specs = (
        spec("groups", "space", None),
        spec("groups", None, "space"),
        spec("groups", "space", None),
        spec(),
        spec(),
    )
    out_specs = (
        spec("groups", "space", None),
        spec("groups", "space", None),
        spec("groups", None, "space"),
        spec("groups", None, None),
        spec("groups", None, None),
    )
    return jax.shard_map(local, mesh=mesh, in_specs=in_specs, out_specs=out_specs, check_vma=False)
```

```python
import functools
import math

import jax
import jax.numpy as jnp
from jax import lax
from jax.experimental import pallas as pl
from jax.experimental.pallas import tpu as pltpu

W = 128
AXIS = "space"
BF16 = jnp.bfloat16
F32 = jnp.float32
NT = (((1,), (1,)), ((), ()))


def mm(a, b):
    return jnp.dot(a, b, preferred_element_type=F32)


def one_hot(shape, cond):
    rows = lax.broadcasted_iota(jnp.int32, shape, 0)
    cols = lax.broadcasted_iota(jnp.int32, shape, 1)
    return jnp.where(cond(rows, cols), 1.0, 0.0).astype(BF16)


def row_taps(z, channels):
    zero = jnp.zeros((channels, W), F32)
    low = jnp.concatenate([zero, z[:channels, :-W]], axis=1)
    high = jnp.concatenate([z[2 * channels :, W:], zero], axis=1)
    return z[channels : 2 * channels] + low + high


def row_taps_back(z, channels):
    zero = jnp.zeros((channels, W), F32)
    low = jnp.concatenate([z[:channels, W:], zero], axis=1)
    high = jnp.concatenate([zero, z[2 * channels :, :-W]], axis=1)
    return z[channels : 2 * channels] + low + high


def spread_columns():
    def pick(lane_in, col):
        tap, k, parity, lane = (col >> 9, (col >> 8) & 1, (col >> 7) & 1, col & 127)
        return ((lane_in >> 6) == parity) & (2 * (lane_in & 63) + k == lane + tap - 1)

    return one_hot((128, 1536), pick)


def skip_columns():
    def pick(row, col):
        out = jnp.where(col >= 384, 1, 0)
        rest = col - 384 * out
        tap, lane = (rest >> 7, rest & 127)
        return (((row >> 6) & 1) == out) & ((row >> 7) * 64 + (row & 63) == lane + tap - 1)

    return one_hot((256, 768), pick)


def place_skip(value, select, xs_ref, base):
    joined = jnp.concatenate([value[:, 0].reshape(512, 128), value[:, 1].reshape(512, 128)], axis=1)
    placed = mm(joined, select).astype(BF16)
    for parity in range(2):
        for tap in range(3):
            at = base + parity * 192 + tap * 64
            for h in range(8):
                xs_ref[at : at + 64, h * W : (h + 1) * W] = placed[
                    h * 64 : (h + 1) * 64, (3 * parity + tap) * W : (3 * parity + tap + 1) * W
                ]


def in_order(core, core_ref, cross_ref):
    near, far = (core_ref[...], cross_ref[...])
    even = core == 0
    return jnp.where(even, far, near), jnp.where(even, near, far)


def up_weights(wup_ref):
    return jnp.concatenate(
        [jnp.concatenate([wup_ref[2 * ij], wup_ref[2 * ij + 1]], axis=1) for ij in range(4)], axis=0
    )


def upsample(coarse, weights, select, xu_ref, base, spread_ref=None):
    spread = [mm(coarse[:, 128 * t : 128 * t + 128], select).astype(BF16) for t in range(2)]
    for tap in range(3):
        columns = []
        for h in range(4):
            at = 512 * tap + 128 * (h & 1)
            piece = spread[h >> 1]
            columns.append(jnp.concatenate([piece[:, at : at + 128], piece[:, at + 256 : at + 384]], axis=0))
        operand = jnp.concatenate(columns, axis=1)
        if spread_ref is not None and tap == 1:
            spread_ref[...] = operand
        up = mm(weights, operand).astype(BF16)
        for i in range(2):
            for j in range(2):
                at = base + i * 192 + tap * 64
                for h in range(4):
                    xu_ref[at : at + 64, (2 * h + j) * W : (2 * h + j + 1) * W] = up[
                        (2 * i + j) * 64 : (2 * i + j + 1) * 64, h * W : (h + 1) * W
                    ]


def prepare_kernel(
    own_ref, wup_ref, wc_ref, xu_ref, spread_ref, wfu_ref, wfs_ref, wi_ref, wg_ref, up_ref, skip_ref
):
    select = spread_columns()
    up_ref[...] = select
    skip_ref[...] = skip_columns()
    upsample(own_ref[...], up_weights(wup_ref), select, xu_ref, 0, spread_ref)
    rows = []
    for b in range(3):
        taps = [wc_ref[9 * a + 3 * b + c] for a in range(3) for c in range(3)]
        rows.append(jnp.concatenate(taps + [jnp.zeros((64, 128), BF16)], axis=1))
    full = jnp.concatenate(rows, axis=0)
    for half, ref in enumerate((wfu_ref, wfs_ref)):
        select = one_hot((256, 128), lambda row, col: row == (col & 63) + 64 * half + 128 * (col >> 6))
        for m in range(5):
            part = mm(full[:, 256 * m : 256 * m + 256], select).astype(BF16)
            if m < 4:
                ref[:, 128 * m : 128 * m + 128] = part
            else:
                ref[:, 512:] = part[:, :64]
    for b in range(3):
        taps = [wc_ref[9 * (2 - jj) + 3 * b + c] for jj in range(3) for c in range(3)]
        wi_ref[b * 128 : (b + 1) * 128, :] = jnp.concatenate(taps, axis=0).T
    wg_ref[...] = jnp.concatenate([wup_ref[2 * ij + k] for k in range(2) for ij in range(4)], axis=0).T


def edge_kernel(
    index_ref,
    core_ref,
    cross_ref,
    wup_ref,
    own_ref,
    held_ref,
    skip_ref,
    far_up_ref,
    far_wfu_ref,
    far_wfs_ref,
    far_spread_ref,
    far_wi_ref,
    far_wg_ref,
    xu_ref,
    xs_ref,
    pre_ref,
    wfs_ref,
    spread_ref,
    wi_ref,
    wg_ref,
    up_ref,
    wfu_ref,
    sems,
):
    pairs = (
        (far_up_ref, up_ref),
        (far_wfu_ref, wfu_ref),
        (far_wfs_ref, wfs_ref),
        (own_ref, xu_ref.at[384:768]),
        (far_spread_ref, spread_ref),
        (far_wi_ref, wi_ref),
        (far_wg_ref, wg_ref),
    )
    copies = [pltpu.make_async_copy(src, dst, sems.at[i]) for i, (src, dst) in enumerate(pairs)]
    for copy in copies:
        copy.start()
    place_skip(held_ref[...], skip_ref[...], xs_ref, 0)
    weights = up_weights(wup_ref)
    before, after = in_order(index_ref[0], core_ref, cross_ref)
    copies[0].wait()
    upsample(before[:, :256], weights, up_ref[...], xu_ref, 0)
    upsample(after[:, :256], weights, up_ref[...], xu_ref, 768)
    for copy in copies[1:]:
        copy.wait()
    for j in range(4):
        z = mm(wfu_ref[...], xu_ref[j * 192 : j * 192 + 576, :])
        low, high = (max(2 - j, 0), min(3 - j, 2))
        rows = slice((low + j - 2) * 192, (high + j - 1) * 192)
        z = z + mm(wfs_ref[:, low * 192 : (high + 1) * 192], xs_ref[rows, :])
        pre_ref[j * 64 : (j + 1) * 64, :] = row_taps(z, 64)


def main_kernel(
    scale,
    index_ref,
    near_ref,
    far_ref,
    cot_ref,
    edge_core_ref,
    edge_cross_ref,
    own_ref,
    select_ref,
    xu_ref,
    pre_ref,
    spread_ref,
    wi_ref,
    wf_ref,
    wg_ref,
    act_ref,
    gi_ref,
    skip_ref,
    keep_ref,
    send_ref,
    xs_ref,
    gs_ref,
    gw_ref,
    sem,
):
    copy = pltpu.make_async_copy(own_ref, xs_ref.at[384:768], sem)
    copy.start()
    core = index_ref[0]
    quad = index_ref[1]
    before, after = in_order(core, near_ref, far_ref)
    place_skip(before, select_ref[...], xs_ref, 0)
    place_skip(after, select_ref[...], xs_ref, 768)
    edges = [
        jnp.concatenate([edge[:64, 256:], edge[64:, 256:]], axis=1)
        for edge in in_order(core, edge_core_ref, edge_cross_ref)
    ]

    shift = one_hot((128, 256), lambda row, col: row == (col & 127) + 1 - 2 * (col >> 7))
    for j in range(4):
        taps = slice(0, 384 - 192 * j) if j < 2 else slice(192 * (4 - j), 576)
        planes = slice(192 * j, 384) if j < 2 else slice(768, 192 * (j + 3))
        z = mm(wf_ref[:, taps], xs_ref[planes, :])
        pre = pre_ref[j * 64 : (j + 1) * 64, :] + row_taps(z, 64)
        gate = 1.0 / (1.0 + jnp.exp(-pre))
        if j == 0:
            cot = edges[0]
        elif j == 3:
            cot = edges[1]
        else:
            cot = cot_ref[:, (j - 1) * 1024 : j * 1024]
            act_ref[:, (j - 1) * 1024 : j * 1024] = (pre * gate).astype(BF16)
        grad = (cot.astype(F32) * gate * (1.0 + pre * (1.0 - gate))).astype(BF16)
        gs_ref[j * 192 + 64 : j * 192 + 128, :] = grad
        tall = jnp.concatenate([grad[:, h * W : (h + 1) * W] for h in range(8)], axis=0)
        moved = mm(tall, shift).astype(BF16)
        for tap in (0, 2):
            at = j * 192 + tap * 64
            for h in range(8):
                gs_ref[at : at + 64, h * W : (h + 1) * W] = moved[
                    h * 64 : (h + 1) * 64, (tap >> 1) * W : (tap >> 1) * W + W
                ]

    copy.wait()
    zero = jnp.zeros((64, W), BF16)
    grads = []
    for j in (1, 2):
        grad = gs_ref[j * 192 + 64 : j * 192 + 128, :]
        low = jnp.concatenate([grad[:, W:], zero], axis=1)
        high = jnp.concatenate([zero, grad[:, :-W]], axis=1)
        grads.append(jnp.concatenate([low, grad, high], axis=0))
    for a in range(3):
        total = None
        for j in (1, 2):
            pieces = []
            for tap in range(3):
                at = (j + a) * 192 + tap * 64
                pieces += [xu_ref[at : at + 64, :], xs_ref[at : at + 64, :]]
            term = lax.dot_general(
                grads[j - 1], jnp.concatenate(pieces, axis=0), NT, preferred_element_type=F32
            )
            total = term if total is None else total + term
        total = total * scale
        for b in range(3):
            for tap in range(3):
                at = (9 * a + 3 * b + tap) * 64
                gw_ref[at : at + 64, :] = total[b * 64 : (b + 1) * 64, tap * W : (tap + 1) * W]

    lower = lax.broadcasted_iota(jnp.int32, (64, W), 1) < 64
    ups = []
    skips = []
    for j in range(2):
        z = mm(wi_ref[...], gs_ref[j * 192 : j * 192 + 576, :])
        grad = row_taps_back(z, 128)
        ups.append(grad[:64].astype(BF16))
        skips.append(grad[64:])
    for h in range(8):
        first = skips[0][:, h * W : (h + 1) * W]
        second = skips[1][:, h * W : (h + 1) * W]
        skip_ref[2 * h] = jnp.where(lower, first, pltpu.roll(second, 64, 1)).astype(BF16)
        skip_ref[2 * h + 1] = jnp.where(lower, pltpu.roll(first, 64, 1), second).astype(BF16)

    tiles = []
    for h in range(4):
        tiles.append(
            jnp.concatenate(
                [ups[i][:, (2 * h + j) * W : (2 * h + j + 1) * W] for i in range(2) for j in range(2)],
                axis=0,
            )
        )
    grad_up = lax.dot_general(
        jnp.concatenate(tiles, axis=1), spread_ref[...], NT, preferred_element_type=F32
    )
    grad_up = grad_up * scale
    for ij in range(4):
        for k in range(2):
            at = (27 + 2 * ij + k) * 64
            gw_ref[at : at + 64, :] = grad_up[ij * 64 : (ij + 1) * 64, k * W : (k + 1) * W]
    gw_ref[35 * 64 :, :] = jnp.zeros((64, W), F32)

    def part_lanes(row, col):
        return ((row >> 7) == ((col >> 6) & 1)) & ((row & 127) == 2 * (col & 63) + (col >> 7))

    apart = one_hot((256, 256), part_lanes)
    halves = [
        mm(jnp.concatenate([tiles[2 * t], tiles[2 * t + 1]], axis=1), apart).astype(BF16) for t in range(2)
    ]
    operand = jnp.concatenate(
        [jnp.concatenate([half[:, k * W : (k + 1) * W] for half in halves], axis=1) for k in range(2)],
        axis=0,
    )
    gi_ref[...] = mm(wg_ref[...], operand).astype(BF16)

    for k in range(4):
        row = jnp.bitwise_xor(quad, k) * 288
        mine = pl.multiple_of(core * 1152 + row, 32)
        other = pl.multiple_of((1 - core) * 1152 + row, 32)
        keep_ref[k * 288 : (k + 1) * 288, :] = gw_ref[pl.ds(mine, 288), :]
        send_ref[k * 288 : (k + 1) * 288, :] = gw_ref[pl.ds(other, 288), :].astype(BF16)


def finish_kernel(index_ref, mine_ref, other_ref, conv_ref, up_ref):
    core = index_ref[0]
    quad = index_ref[1]
    for side, ref in ((core, mine_ref), (1 - core, other_ref)):
        for k in range(4):
            piece = 4 * side + jnp.bitwise_xor(quad, k)
            rows = slice(k * 288, (k + 1) * 288)

            @pl.when(piece < 6)
            def _():
                conv_ref[pl.ds(piece * 9, 9)] = ref[rows, :].astype(F32).reshape(9, 32, 128)

            @pl.when(piece == 6)
            def _():
                up_ref[0:9] = ref[rows, :].astype(F32).reshape(9, 32, 128)

            @pl.when(piece == 7)
            def _():
                up_ref[9:16] = ref[k * 288 : k * 288 + 224, :].astype(F32).reshape(7, 32, 128)


def room(mebibytes):
    return pltpu.CompilerParams(vmem_limit_bytes=mebibytes << 20)


VMEM = pl.BlockSpec(memory_space=pltpu.VMEM)
SMEM = pl.BlockSpec(memory_space=pltpu.SMEM)
FAR = pl.BlockSpec(memory_space=pl.ANY)


def far(value):
    return pltpu.with_memory_space_constraint(value, pltpu.HBM)


def near(value):
    return pltpu.with_memory_space_constraint(value, pltpu.VMEM)


def like(shape, dtype=BF16):
    return jax.ShapeDtypeStruct(shape, dtype)


def inside(shape, dtype=BF16):
    return pltpu.VMEM(shape, dtype)


def outside(shape, dtype=BF16):
    return pltpu.HBM(shape, dtype)


def reduce_weights(index, keep, send, back, finish_others, n):
    def swap(value, bit):
        return lax.ppermute(value, AXIS, [(i, i ^ bit) for i in range(n)])

    summed = keep + swap(send, 1).astype(F32)
    rounded = summed.astype(BF16)
    total = summed[:288]
    for k in (1, 2, 3):
        total = total + swap(rounded[k * 288 : (k + 1) * 288], 2 * k).astype(F32)
    total, back = lax.optimization_barrier((total, back))
    bit = 8
    while bit < n:
        own = total.astype(BF16)
        total = own.astype(F32) + swap(own, bit).astype(F32)
        bit *= 2
    own = total.astype(BF16)
    pieces = [own] + [swap(own, 2 * k) for k in (1, 2, 3)]
    pieces, others = lax.optimization_barrier((pieces, finish_others(back)))
    mine = jnp.concatenate(pieces, axis=0)
    other = swap(mine, 1)
    conv, up = pl.pallas_call(
        finish_kernel,
        out_shape=(like((54, 32, 128), F32), like((16, 32, 128), F32)),
        in_specs=[SMEM, VMEM, VMEM],
        out_specs=(VMEM, VMEM),
        compiler_params=room(6),
        cost_estimate=pl.CostEstimate(flops=1955000000, bytes_accessed=1000000, transcendentals=0),
        name="finish",
    )(index, mine, other)
    return conv.reshape(27, 64, 128), up.reshape(8, 64, 128), others


def local(coarse_input, skip, cotangent, w_up, w_conv):
    n = lax.axis_size(AXIS)
    cells = cotangent.shape[2]
    planes = cotangent.shape[1]
    positions = skip.shape[2]
    core_pairs = [(i, i ^ 1) for i in range(n)]
    cross_pairs = [(i, i + 1 if i % 2 else i - 1) for i in range(1, n - 1)]
    me = lax.axis_index(AXIS)
    index = jnp.stack([me & 1, (me >> 1) & 3]).astype(jnp.int32)

    sent = skip.reshape(64, n, 2 * positions).transpose(1, 0, 2)
    held = lax.all_to_all(sent, AXIS, split_axis=0, concat_axis=0, tiled=True)
    if positions != 64:
        held = held.reshape(n, 64, 2, positions).transpose(1, 2, 0, 3).reshape(64, 2, 16, 64)
        held = held.transpose(2, 0, 1, 3).reshape(16, 64, 128)

    coarse = coarse_input.reshape(128, 256)
    flat = lax.optimization_barrier(cotangent.reshape(64, 2048))

    def edge(plane):
        halves = [lax.dynamic_slice_in_dim(flat, 1024 * plane + 512 * i, 512, 1) for i in range(2)]
        return jnp.concatenate([coarse, jnp.concatenate(halves, axis=0)], axis=1)

    edge_core = lax.ppermute(edge(1 - index[0]), AXIS, core_pairs)
    edge_cross = lax.ppermute(edge(index[0]), AXIS, cross_pairs)
    xu, spread, wf_up, wf_skip, wi, wg, pick_up, pick_skip = pl.pallas_call(
        prepare_kernel,
        out_shape=(
            inside((384, 1024)),
            outside((256, 512)),
            outside((192, 576)),
            outside((192, 576)),
            outside((384, 576)),
            outside((128, 512)),
            outside((128, 1536)),
            inside((256, 768)),
        ),
        in_specs=[VMEM] * 3,
        out_specs=(VMEM,) * 8,
        compiler_params=room(8),
        cost_estimate=pl.CostEstimate(flops=1840000000, bytes_accessed=1000000, transcendentals=0),
        name="prepare",
    )(coarse, w_up, w_conv)
    held, wf_up = lax.optimization_barrier((held, wf_up))
    held_core = lax.ppermute(held, AXIS, core_pairs)
    held_cross = lax.ppermute(held, AXIS, cross_pairs)
    held, held_core, held_cross = [v.reshape(8, 2, 64, 128) for v in (held, held_core, held_cross)]
    xu, xs, pre, wf_skip, spread, wi, wg = pl.pallas_call(
        edge_kernel,
        out_shape=(
            inside((1152, 1024)),
            inside((384, 1024)),
            inside((256, 1024), F32),
            inside((192, 576)),
            inside((256, 512)),
            inside((384, 576)),
            inside((128, 512)),
        ),
        in_specs=[SMEM] + [VMEM] * 6 + [FAR] * 6,
        out_specs=(VMEM,) * 7,
        scratch_shapes=[
            pltpu.VMEM((128, 1536), BF16),
            pltpu.VMEM((192, 576), BF16),
            pltpu.SemaphoreType.DMA((7,)),
        ],
        compiler_params=room(16),
        cost_estimate=pl.CostEstimate(flops=2990000000, bytes_accessed=1000000, transcendentals=0),
        name="edges",
    )(
        index,
        *(near(v) for v in (edge_core, edge_cross)),
        w_up,
        *(near(v) for v in (xu, held, pick_skip)),
        *(far(v) for v in (pick_up, wf_up, wf_skip, spread, wi, wg)),
    )

    scale = 1.0 / math.sqrt(n * planes * cells)
    act, gi, skip_part, keep, send = pl.pallas_call(
        functools.partial(main_kernel, scale),
        out_shape=(
            outside((64, 2048)),
            outside((128, 256)),
            outside((16, 64, 128)),
            inside((1152, 128), F32),
            inside((1152, 128)),
        ),
        in_specs=[SMEM] + [VMEM] * 13,
        out_specs=(VMEM,) * 5,
        scratch_shapes=[
            pltpu.VMEM((1152, 1024), BF16),
            pltpu.VMEM((768, 1024), BF16),
            pltpu.VMEM((2304, 128), F32),
            pltpu.SemaphoreType.DMA,
        ],
        compiler_params=room(24),
        cost_estimate=pl.CostEstimate(flops=8280000000, bytes_accessed=1000000, transcendentals=0),
        name="section",
    )(
        index,
        *(
            near(v)
            for v in (
                held_core,
                held_cross,
                flat,
                edge_core,
                edge_cross,
                xs,
                pick_skip,
                xu,
                pre,
                spread,
                wi,
                wf_skip,
                wg,
            )
        ),
    )
    if positions != 64:
        skip_part = skip_part.reshape(16, 64, 2, 64).transpose(1, 2, 0, 3)
        skip_part = skip_part.reshape(64, 2, n, positions).transpose(2, 0, 1, 3)
        skip_part = skip_part.reshape(n, 64, 2 * positions)
    back = lax.all_to_all(skip_part, AXIS, split_axis=0, concat_axis=0, tiled=True)

    def others(back):
        return (
            act.reshape(64, planes, cells),
            gi.reshape(128, 1, 256),
            back.transpose(1, 0, 2).reshape(64, 2 * n, positions),
        )

    grad_w_conv, grad_w_up, rest = reduce_weights(index, keep, send, back, others, n)
    return (*rest, grad_w_up, grad_w_conv)


def solution(mesh):
    spec = jax.sharding.PartitionSpec
    in_specs = (
        spec("groups", "space", None),
        spec("groups", None, "space"),
        spec("groups", "space", None),
        spec(),
        spec(),
    )
    out_specs = (
        spec("groups", "space", None),
        spec("groups", "space", None),
        spec("groups", None, "space"),
        spec("groups", None, None),
        spec("groups", None, None),
    )
    return jax.shard_map(local, mesh=mesh, in_specs=in_specs, out_specs=out_specs, check_vma=False)
```

```python
import functools
import math

import jax
import jax.numpy as jnp
from jax import lax
from jax.experimental import pallas as pl
from jax.experimental.pallas import tpu as pltpu

W = 128
AXIS = "space"
BF16 = jnp.bfloat16
F32 = jnp.float32
NT = (((1,), (1,)), ((), ()))


def mm(a, b):
    return jnp.dot(a, b, preferred_element_type=F32)


def one_hot(shape, cond):
    rows = lax.broadcasted_iota(jnp.int32, shape, 0)
    cols = lax.broadcasted_iota(jnp.int32, shape, 1)
    return jnp.where(cond(rows, cols), 1.0, 0.0).astype(BF16)


def row_taps(z, channels):
    zero = jnp.zeros((channels, W), F32)
    low = jnp.concatenate([zero, z[:channels, :-W]], axis=1)
    high = jnp.concatenate([z[2 * channels :, W:], zero], axis=1)
    return z[channels : 2 * channels] + low + high


def row_taps_back(z, channels):
    zero = jnp.zeros((channels, W), F32)
    low = jnp.concatenate([z[:channels, W:], zero], axis=1)
    high = jnp.concatenate([zero, z[2 * channels :, :-W]], axis=1)
    return z[channels : 2 * channels] + low + high


def spread_columns():
    def pick(lane_in, col):
        tap, k, parity, lane = (col >> 9, (col >> 8) & 1, (col >> 7) & 1, col & 127)
        return ((lane_in >> 6) == parity) & (2 * (lane_in & 63) + k == lane + tap - 1)

    return one_hot((128, 1536), pick)


def skip_columns():
    def pick(row, col):
        out = jnp.where(col >= 384, 1, 0)
        rest = col - 384 * out
        tap, lane = (rest >> 7, rest & 127)
        return (((row >> 6) & 1) == out) & ((row >> 7) * 64 + (row & 63) == lane + tap - 1)

    return one_hot((256, 768), pick)


def place_skip(value, select, xs_ref, base):
    joined = jnp.concatenate([value[:, 0].reshape(512, 128), value[:, 1].reshape(512, 128)], axis=1)
    placed = mm(joined, select).astype(BF16)
    for parity in range(2):
        for tap in range(3):
            at = base + parity * 192 + tap * 64
            for h in range(8):
                xs_ref[at : at + 64, h * W : (h + 1) * W] = placed[
                    h * 64 : (h + 1) * 64, (3 * parity + tap) * W : (3 * parity + tap + 1) * W
                ]


def in_order(core, core_ref, cross_ref):
    near, far = (core_ref[...], cross_ref[...])
    even = core == 0
    return jnp.where(even, far, near), jnp.where(even, near, far)


def up_weights(wup_ref):
    return jnp.concatenate(
        [jnp.concatenate([wup_ref[2 * ij], wup_ref[2 * ij + 1]], axis=1) for ij in range(4)], axis=0
    )


def upsample(coarse, weights, select, xu_ref, base, spread_ref=None):
    spread = [mm(coarse[:, 128 * t : 128 * t + 128], select).astype(BF16) for t in range(2)]
    for tap in range(3):
        columns = []
        for h in range(4):
            at = 512 * tap + 128 * (h & 1)
            piece = spread[h >> 1]
            columns.append(jnp.concatenate([piece[:, at : at + 128], piece[:, at + 256 : at + 384]], axis=0))
        operand = jnp.concatenate(columns, axis=1)
        if spread_ref is not None and tap == 1:
            spread_ref[...] = operand
        up = mm(weights, operand).astype(BF16)
        for i in range(2):
            for j in range(2):
                at = base + i * 192 + tap * 64
                for h in range(4):
                    xu_ref[at : at + 64, (2 * h + j) * W : (2 * h + j + 1) * W] = up[
                        (2 * i + j) * 64 : (2 * i + j + 1) * 64, h * W : (h + 1) * W
                    ]


def prepare_kernel(
    own_ref, wup_ref, wc_ref, xu_ref, spread_ref, wfu_ref, wfs_ref, wi_ref, wg_ref, up_ref, skip_ref
):
    select = spread_columns()
    up_ref[...] = select
    skip_ref[...] = skip_columns()
    upsample(own_ref[...], up_weights(wup_ref), select, xu_ref, 0, spread_ref)
    rows = []
    for b in range(3):
        taps = [wc_ref[9 * a + 3 * b + c] for a in range(3) for c in range(3)]
        rows.append(jnp.concatenate(taps + [jnp.zeros((64, 128), BF16)], axis=1))
    full = jnp.concatenate(rows, axis=0)
    for half, ref in enumerate((wfu_ref, wfs_ref)):
        select = one_hot((256, 128), lambda row, col: row == (col & 63) + 64 * half + 128 * (col >> 6))
        for m in range(5):
            part = mm(full[:, 256 * m : 256 * m + 256], select).astype(BF16)
            if m < 4:
                ref[:, 128 * m : 128 * m + 128] = part
            else:
                ref[:, 512:] = part[:, :64]
    for b in range(3):
        taps = [wc_ref[9 * (2 - jj) + 3 * b + c] for jj in range(3) for c in range(3)]
        wi_ref[b * 128 : (b + 1) * 128, :] = jnp.concatenate(taps, axis=0).T
    wg_ref[...] = jnp.concatenate([wup_ref[2 * ij + k] for k in range(2) for ij in range(4)], axis=0).T


def edge_kernel(
    index_ref,
    core_ref,
    cross_ref,
    wup_ref,
    own_ref,
    held_ref,
    skip_ref,
    far_up_ref,
    far_wfu_ref,
    far_wfs_ref,
    far_spread_ref,
    far_wi_ref,
    far_wg_ref,
    xu_ref,
    xs_ref,
    pre_ref,
    wfs_ref,
    spread_ref,
    wi_ref,
    wg_ref,
    up_ref,
    wfu_ref,
    sems,
):
    pairs = (
        (far_up_ref, up_ref),
        (far_wfu_ref, wfu_ref),
        (far_wfs_ref, wfs_ref),
        (own_ref, xu_ref.at[384:768]),
        (far_spread_ref, spread_ref),
        (far_wi_ref, wi_ref),
        (far_wg_ref, wg_ref),
    )
    copies = [pltpu.make_async_copy(src, dst, sems.at[i]) for i, (src, dst) in enumerate(pairs)]
    for copy in copies:
        copy.start()
    place_skip(held_ref[...], skip_ref[...], xs_ref, 0)
    weights = up_weights(wup_ref)
    before, after = in_order(index_ref[0], core_ref, cross_ref)
    copies[0].wait()
    upsample(before[:, :256], weights, up_ref[...], xu_ref, 0)
    upsample(after[:, :256], weights, up_ref[...], xu_ref, 768)
    for copy in copies[1:]:
        copy.wait()
    for j in range(4):
        z = mm(wfu_ref[...], xu_ref[j * 192 : j * 192 + 576, :])
        low, high = (max(2 - j, 0), min(3 - j, 2))
        rows = slice((low + j - 2) * 192, (high + j - 1) * 192)
        z = z + mm(wfs_ref[:, low * 192 : (high + 1) * 192], xs_ref[rows, :])
        pre_ref[j * 64 : (j + 1) * 64, :] = row_taps(z, 64)


def main_kernel(
    scale,
    index_ref,
    near_ref,
    far_ref,
    cot_ref,
    edge_core_ref,
    edge_cross_ref,
    own_ref,
    select_ref,
    xu_ref,
    pre_ref,
    spread_ref,
    wi_ref,
    wf_ref,
    wg_ref,
    far_act_ref,
    far_gi_ref,
    far_skip_ref,
    keep_ref,
    send_ref,
    xs_ref,
    gs_ref,
    gw_ref,
    act_ref,
    gi_ref,
    skip_ref,
    sems,
):
    copy = pltpu.make_async_copy(own_ref, xs_ref.at[384:768], sems.at[0])
    copy.start()
    act_copy = pltpu.make_async_copy(act_ref, far_act_ref, sems.at[1])
    skip_copy = pltpu.make_async_copy(skip_ref, far_skip_ref, sems.at[2])
    gi_copy = pltpu.make_async_copy(gi_ref, far_gi_ref, sems.at[3])
    core = index_ref[0]
    quad = index_ref[1]
    before, after = in_order(core, near_ref, far_ref)
    place_skip(before, select_ref[...], xs_ref, 0)
    place_skip(after, select_ref[...], xs_ref, 768)
    edges = [
        jnp.concatenate([edge[:64, 256:], edge[64:, 256:]], axis=1)
        for edge in in_order(core, edge_core_ref, edge_cross_ref)
    ]

    shift = one_hot((128, 256), lambda row, col: row == (col & 127) + 1 - 2 * (col >> 7))
    for j in range(4):
        taps = slice(0, 384 - 192 * j) if j < 2 else slice(192 * (4 - j), 576)
        planes = slice(192 * j, 384) if j < 2 else slice(768, 192 * (j + 3))
        z = mm(wf_ref[:, taps], xs_ref[planes, :])
        pre = pre_ref[j * 64 : (j + 1) * 64, :] + row_taps(z, 64)
        gate = 1.0 / (1.0 + jnp.exp(-pre))
        if j == 0:
            cot = edges[0]
        elif j == 3:
            cot = edges[1]
        else:
            cot = cot_ref[:, (j - 1) * 1024 : j * 1024]
            act_ref[:, (j - 1) * 1024 : j * 1024] = (pre * gate).astype(BF16)
        grad = (cot.astype(F32) * gate * (1.0 + pre * (1.0 - gate))).astype(BF16)
        gs_ref[j * 192 + 64 : j * 192 + 128, :] = grad
        tall = jnp.concatenate([grad[:, h * W : (h + 1) * W] for h in range(8)], axis=0)
        moved = mm(tall, shift).astype(BF16)
        for tap in (0, 2):
            at = j * 192 + tap * 64
            for h in range(8):
                gs_ref[at : at + 64, h * W : (h + 1) * W] = moved[
                    h * 64 : (h + 1) * 64, (tap >> 1) * W : (tap >> 1) * W + W
                ]

    act_copy.start()
    lower = lax.broadcasted_iota(jnp.int32, (64, W), 1) < 64
    ups = []
    skips = []
    for j in range(2):
        z = mm(wi_ref[...], gs_ref[j * 192 : j * 192 + 576, :])
        grad = row_taps_back(z, 128)
        ups.append(grad[:64].astype(BF16))
        skips.append(grad[64:])
    for h in range(8):
        first = skips[0][:, h * W : (h + 1) * W]
        second = skips[1][:, h * W : (h + 1) * W]
        skip_ref[2 * h] = jnp.where(lower, first, pltpu.roll(second, 64, 1)).astype(BF16)
        skip_ref[2 * h + 1] = jnp.where(lower, pltpu.roll(first, 64, 1), second).astype(BF16)

    skip_copy.start()
    tiles = []
    for h in range(4):
        tiles.append(
            jnp.concatenate(
                [ups[i][:, (2 * h + j) * W : (2 * h + j + 1) * W] for i in range(2) for j in range(2)],
                axis=0,
            )
        )
    grad_up = lax.dot_general(
        jnp.concatenate(tiles, axis=1), spread_ref[...], NT, preferred_element_type=F32
    )
    grad_up = grad_up * scale
    for ij in range(4):
        for k in range(2):
            at = (27 + 2 * ij + k) * 64
            gw_ref[at : at + 64, :] = grad_up[ij * 64 : (ij + 1) * 64, k * W : (k + 1) * W]
    gw_ref[35 * 64 :, :] = jnp.zeros((64, W), F32)

    def part_lanes(row, col):
        return ((row >> 7) == ((col >> 6) & 1)) & ((row & 127) == 2 * (col & 63) + (col >> 7))

    apart = one_hot((256, 256), part_lanes)
    halves = [
        mm(jnp.concatenate([tiles[2 * t], tiles[2 * t + 1]], axis=1), apart).astype(BF16) for t in range(2)
    ]
    operand = jnp.concatenate(
        [jnp.concatenate([half[:, k * W : (k + 1) * W] for half in halves], axis=1) for k in range(2)],
        axis=0,
    )
    gi_ref[...] = mm(wg_ref[...], operand).astype(BF16)
    gi_copy.start()

    copy.wait()
    zero = jnp.zeros((64, W), BF16)
    grads = []
    for j in (1, 2):
        grad = gs_ref[j * 192 + 64 : j * 192 + 128, :]
        low = jnp.concatenate([grad[:, W:], zero], axis=1)
        high = jnp.concatenate([zero, grad[:, :-W]], axis=1)
        grads.append(jnp.concatenate([low, grad, high], axis=0))
    total = None
    for j in (1, 2):
        pieces = []
        for e in range(j, j + 3):
            for tap in range(3):
                at = e * 192 + tap * 64
                pieces += [xu_ref[at : at + 64, :], xs_ref[at : at + 64, :]]
        term = lax.dot_general(
            jnp.concatenate(pieces, axis=0), grads[j - 1], NT, preferred_element_type=F32
        )
        total = term if total is None else total + term
    total = (total * scale).T
    for a in range(3):
        for b in range(3):
            for tap in range(3):
                at = (9 * a + 3 * b + tap) * 64
                column = (3 * a + tap) * W
                gw_ref[at : at + 64, :] = total[b * 64 : (b + 1) * 64, column : column + W]

    for k in range(4):
        row = jnp.bitwise_xor(quad, k) * 288
        mine = pl.multiple_of(core * 1152 + row, 32)
        other = pl.multiple_of((1 - core) * 1152 + row, 32)
        keep_ref[k * 288 : (k + 1) * 288, :] = gw_ref[pl.ds(mine, 288), :]
        send_ref[k * 288 : (k + 1) * 288, :] = gw_ref[pl.ds(other, 288), :].astype(BF16)
    for done in (act_copy, skip_copy, gi_copy):
        done.wait()


def finish_kernel(mine, index_ref, value_ref, *refs):
    conv_ref, up_ref, stage_ref, sems = refs[-4:]
    side = index_ref[0] if mine else 1 - index_ref[0]

    def each(act):
        for k in range(4):
            piece = 4 * side + jnp.bitwise_xor(index_ref[1], k)
            rows = slice(k * 9, k * 9 + 9)

            @pl.when(piece < 6)
            def _():
                dst = conv_ref.at[pl.ds(piece * 9, 9)]
                act(k, pltpu.make_async_copy(stage_ref.at[rows], dst, sems.at[k]))

            @pl.when(piece == 6)
            def _():
                act(k, pltpu.make_async_copy(stage_ref.at[rows], up_ref.at[0:9], sems.at[k]))

            @pl.when(piece == 7)
            def _():
                src = stage_ref.at[k * 9 : k * 9 + 7]
                act(k, pltpu.make_async_copy(src, up_ref.at[9:16], sems.at[k]))

    for k in range(4):
        rows = slice(k * 288, (k + 1) * 288)
        stage_ref[k * 9 : k * 9 + 9] = value_ref[rows, :].astype(F32).reshape(9, 32, 128)
    each(lambda k, copy: copy.start())
    each(lambda k, copy: copy.wait())


def room(mebibytes):
    return pltpu.CompilerParams(vmem_limit_bytes=mebibytes << 20)


VMEM = pl.BlockSpec(memory_space=pltpu.VMEM)
SMEM = pl.BlockSpec(memory_space=pltpu.SMEM)
FAR = pl.BlockSpec(memory_space=pl.ANY)


def far(value):
    return pltpu.with_memory_space_constraint(value, pltpu.HBM)


def near(value):
    return pltpu.with_memory_space_constraint(value, pltpu.VMEM)


def like(shape, dtype=BF16):
    return jax.ShapeDtypeStruct(shape, dtype)


def inside(shape, dtype=BF16):
    return pltpu.VMEM(shape, dtype)


def outside(shape, dtype=BF16):
    return pltpu.HBM(shape, dtype)


def reduce_weights(index, keep, send, back, finish_others, n):
    def swap(value, bit):
        return lax.ppermute(value, AXIS, [(i, i ^ bit) for i in range(n)])

    summed = keep + swap(send, 1).astype(F32)
    rounded = summed.astype(BF16)
    total = summed[:288]
    for k in (1, 2, 3):
        total = total + swap(rounded[k * 288 : (k + 1) * 288], 2 * k).astype(F32)
    total, back = lax.optimization_barrier((total, back))
    bit = 8
    while bit < n:
        own = total.astype(BF16)
        total = own.astype(F32) + swap(own, bit).astype(F32)
        bit *= 2
    own = total.astype(BF16)
    pieces = [own] + [swap(own, 2 * k) for k in (1, 2, 3)]
    pieces, others = lax.optimization_barrier((pieces, finish_others(back)))
    mine = jnp.concatenate(pieces, axis=0)
    other = swap(mine, 1)
    sums = ()
    for first, value in ((True, mine), (False, other)):
        sums = pl.pallas_call(
            functools.partial(finish_kernel, first),
            out_shape=(outside((54, 32, 128), F32), outside((16, 32, 128), F32)),
            in_specs=[SMEM, VMEM] + [FAR] * len(sums),
            out_specs=(FAR, FAR),
            scratch_shapes=[pltpu.VMEM((36, 32, 128), F32), pltpu.SemaphoreType.DMA((4,))],
            input_output_aliases={} if first else {2: 0, 3: 1},
            compiler_params=room(6),
            cost_estimate=pl.CostEstimate(flops=1200000000, bytes_accessed=1000000, transcendentals=0),
            name="finish",
        )(index, value, *sums)
    conv, up = sums
    return conv.reshape(27, 64, 128), up.reshape(8, 64, 128), others


def local(coarse_input, skip, cotangent, w_up, w_conv):
    n = lax.axis_size(AXIS)
    cells = cotangent.shape[2]
    planes = cotangent.shape[1]
    positions = skip.shape[2]
    core_pairs = [(i, i ^ 1) for i in range(n)]
    cross_pairs = [(i, i + 1 if i % 2 else i - 1) for i in range(1, n - 1)]
    me = lax.axis_index(AXIS)
    index = jnp.stack([me & 1, (me >> 1) & 3]).astype(jnp.int32)

    sent = skip.reshape(64, n, 2 * positions).transpose(1, 0, 2)
    held = lax.all_to_all(sent, AXIS, split_axis=0, concat_axis=0, tiled=True)
    if positions != 64:
        held = held.reshape(n, 64, 2, positions).transpose(1, 2, 0, 3).reshape(64, 2, 16, 64)
        held = held.transpose(2, 0, 1, 3).reshape(16, 64, 128)

    coarse = coarse_input.reshape(128, 256)
    flat = lax.optimization_barrier(cotangent.reshape(64, 2048))

    def edge(plane):
        halves = [lax.dynamic_slice_in_dim(flat, 1024 * plane + 512 * i, 512, 1) for i in range(2)]
        return jnp.concatenate([coarse, jnp.concatenate(halves, axis=0)], axis=1)

    edge_core = lax.ppermute(edge(1 - index[0]), AXIS, core_pairs)
    edge_cross = lax.ppermute(edge(index[0]), AXIS, cross_pairs)
    xu, spread, wf_up, wf_skip, wi, wg, pick_up, pick_skip = pl.pallas_call(
        prepare_kernel,
        out_shape=(
            inside((384, 1024)),
            outside((256, 512)),
            outside((192, 576)),
            outside((192, 576)),
            outside((384, 576)),
            outside((128, 512)),
            outside((128, 1536)),
            inside((256, 768)),
        ),
        in_specs=[VMEM] * 3,
        out_specs=(VMEM,) * 8,
        compiler_params=room(8),
        cost_estimate=pl.CostEstimate(flops=1840000000, bytes_accessed=1000000, transcendentals=0),
        name="prepare",
    )(coarse, w_up, w_conv)
    held, wf_up = lax.optimization_barrier((held, wf_up))
    held_core = lax.ppermute(held, AXIS, core_pairs)
    held_cross = lax.ppermute(held, AXIS, cross_pairs)
    held, held_core, held_cross = [v.reshape(8, 2, 64, 128) for v in (held, held_core, held_cross)]
    xu, xs, pre, wf_skip, spread, wi, wg = pl.pallas_call(
        edge_kernel,
        out_shape=(
            inside((1152, 1024)),
            inside((384, 1024)),
            inside((256, 1024), F32),
            inside((192, 576)),
            inside((256, 512)),
            inside((384, 576)),
            inside((128, 512)),
        ),
        in_specs=[SMEM] + [VMEM] * 6 + [FAR] * 6,
        out_specs=(VMEM,) * 7,
        scratch_shapes=[
            pltpu.VMEM((128, 1536), BF16),
            pltpu.VMEM((192, 576), BF16),
            pltpu.SemaphoreType.DMA((7,)),
        ],
        compiler_params=room(16),
        cost_estimate=pl.CostEstimate(flops=2990000000, bytes_accessed=1000000, transcendentals=0),
        name="edges",
    )(
        index,
        *(near(v) for v in (edge_core, edge_cross)),
        w_up,
        *(near(v) for v in (xu, held, pick_skip)),
        *(far(v) for v in (pick_up, wf_up, wf_skip, spread, wi, wg)),
    )

    scale = 1.0 / math.sqrt(n * planes * cells)
    act, gi, skip_part, keep, send = pl.pallas_call(
        functools.partial(main_kernel, scale),
        out_shape=(
            outside((64, 2048)),
            outside((128, 256)),
            outside((16, 64, 128)),
            inside((1152, 128), F32),
            inside((1152, 128)),
        ),
        in_specs=[SMEM] + [VMEM] * 13,
        out_specs=(FAR,) * 3 + (VMEM,) * 2,
        scratch_shapes=[
            pltpu.VMEM((1152, 1024), BF16),
            pltpu.VMEM((768, 1024), BF16),
            pltpu.VMEM((2304, 128), F32),
            pltpu.VMEM((64, 2048), BF16),
            pltpu.VMEM((128, 256), BF16),
            pltpu.VMEM((16, 64, 128), BF16),
            pltpu.SemaphoreType.DMA((4,)),
        ],
        compiler_params=room(24),
        cost_estimate=pl.CostEstimate(flops=8280000000, bytes_accessed=1000000, transcendentals=0),
        name="section",
    )(
        index,
        *(
            near(v)
            for v in (
                held_core,
                held_cross,
                flat,
                edge_core,
                edge_cross,
                xs,
                pick_skip,
                xu,
                pre,
                spread,
                wi,
                wf_skip,
                wg,
            )
        ),
    )
    if positions != 64:
        skip_part = skip_part.reshape(16, 64, 2, 64).transpose(1, 2, 0, 3)
        skip_part = skip_part.reshape(64, 2, n, positions).transpose(2, 0, 1, 3)
        skip_part = skip_part.reshape(n, 64, 2 * positions)
    back = lax.all_to_all(skip_part, AXIS, split_axis=0, concat_axis=0, tiled=True)

    def others(back):
        return (
            act.reshape(64, planes, cells),
            gi.reshape(128, 1, 256),
            back.transpose(1, 0, 2).reshape(64, 2 * n, positions),
        )

    grad_w_conv, grad_w_up, rest = reduce_weights(index, keep, send, back, others, n)
    return (*rest, grad_w_up, grad_w_conv)


def solution(mesh):
    spec = jax.sharding.PartitionSpec
    in_specs = (
        spec("groups", "space", None),
        spec("groups", None, "space"),
        spec("groups", "space", None),
        spec(),
        spec(),
    )
    out_specs = (
        spec("groups", "space", None),
        spec("groups", "space", None),
        spec("groups", None, "space"),
        spec("groups", None, None),
        spec("groups", None, None),
    )
    return jax.shard_map(local, mesh=mesh, in_specs=in_specs, out_specs=out_specs, check_vma=False)
```

```python
import functools
import math

import jax
import jax.numpy as jnp
from jax import lax
from jax.experimental import pallas as pl
from jax.experimental.pallas import tpu as pltpu

W = 128
AXIS = "space"
BF16 = jnp.bfloat16
F32 = jnp.float32
NT = (((1,), (1,)), ((), ()))


def mm(a, b):
    return jnp.dot(a, b, preferred_element_type=F32)


def one_hot(shape, cond):
    rows = lax.broadcasted_iota(jnp.int32, shape, 0)
    cols = lax.broadcasted_iota(jnp.int32, shape, 1)
    return jnp.where(cond(rows, cols), 1.0, 0.0).astype(BF16)


def row_taps(z, channels):
    zero = jnp.zeros((channels, W), F32)
    low = jnp.concatenate([zero, z[:channels, :-W]], axis=1)
    high = jnp.concatenate([z[2 * channels :, W:], zero], axis=1)
    return z[channels : 2 * channels] + low + high


def row_taps_back(z, channels):
    zero = jnp.zeros((channels, W), F32)
    low = jnp.concatenate([z[:channels, W:], zero], axis=1)
    high = jnp.concatenate([zero, z[2 * channels :, :-W]], axis=1)
    return z[channels : 2 * channels] + low + high


def spread_columns():
    def pick(lane_in, col):
        tap, k, parity, lane = (col >> 9, (col >> 8) & 1, (col >> 7) & 1, col & 127)
        return ((lane_in >> 6) == parity) & (2 * (lane_in & 63) + k == lane + tap - 1)

    return one_hot((128, 1536), pick)


def skip_columns():
    def pick(row, col):
        out = jnp.where(col >= 384, 1, 0)
        rest = col - 384 * out
        tap, lane = (rest >> 7, rest & 127)
        return (((row >> 6) & 1) == out) & ((row >> 7) * 64 + (row & 63) == lane + tap - 1)

    return one_hot((256, 768), pick)


def place_skip(value, select, xs_ref, base):
    joined = jnp.concatenate([value[:, 0].reshape(512, 128), value[:, 1].reshape(512, 128)], axis=1)
    placed = mm(joined, select).astype(BF16)
    for parity in range(2):
        for tap in range(3):
            at = base + parity * 192 + tap * 64
            for h in range(8):
                xs_ref[at : at + 64, h * W : (h + 1) * W] = placed[
                    h * 64 : (h + 1) * 64, (3 * parity + tap) * W : (3 * parity + tap + 1) * W
                ]


def shift_columns():
    return one_hot((128, 256), lambda row, col: row == (col & 127) + 1 - 2 * (col >> 7))


def gated(pre, cot):
    gate = 1.0 / (1.0 + jnp.exp(-pre))
    grad = (cot.astype(F32) * gate * (1.0 + pre * (1.0 - gate))).astype(BF16)
    return (pre * gate).astype(BF16), grad


def place_grad(grad, shift, gs_ref, base):
    gs_ref[base + 64 : base + 128, :] = grad
    tall = jnp.concatenate([grad[:, h * W : (h + 1) * W] for h in range(8)], axis=0)
    moved = mm(tall, shift).astype(BF16)
    for side in range(2):
        at = base + side * 128
        for h in range(8):
            gs_ref[at : at + 64, h * W : (h + 1) * W] = moved[
                h * 64 : (h + 1) * 64, side * W : side * W + W
            ]


def weight_term(grad, xu_ref, skip_rows, first):
    zero = jnp.zeros((64, W), BF16)
    low = jnp.concatenate([grad[:, W:], zero], axis=1)
    high = jnp.concatenate([zero, grad[:, :-W]], axis=1)
    pieces = []
    for e in range(first, first + 3):
        for tap in range(3):
            at = e * 192 + tap * 64
            pieces += [xu_ref[at : at + 64, :], skip_rows(e, tap)]
    rows = jnp.concatenate([low, grad, high], axis=0)
    return lax.dot_general(jnp.concatenate(pieces, axis=0), rows, NT, preferred_element_type=F32)


def edge_cot(edge_ref):
    return jnp.concatenate([edge_ref[:64, 256:], edge_ref[64:, 256:]], axis=1)


def for_parity(core, body):
    @pl.when(core == 0)
    def _():
        body(0)

    @pl.when(core == 1)
    def _():
        body(1)


def up_weights(wup_ref):
    return jnp.concatenate(
        [jnp.concatenate([wup_ref[2 * ij], wup_ref[2 * ij + 1]], axis=1) for ij in range(4)], axis=0
    )


def upsample(coarse, weights, select, xu_ref, base, spread_ref=None):
    spread = [mm(coarse[:, 128 * t : 128 * t + 128], select).astype(BF16) for t in range(2)]
    for tap in range(3):
        columns = []
        for h in range(4):
            at = 512 * tap + 128 * (h & 1)
            piece = spread[h >> 1]
            columns.append(jnp.concatenate([piece[:, at : at + 128], piece[:, at + 256 : at + 384]], axis=0))
        operand = jnp.concatenate(columns, axis=1)
        if spread_ref is not None and tap == 1:
            spread_ref[...] = operand
        up = mm(weights, operand).astype(BF16)
        for i in range(2):
            for j in range(2):
                at = base + i * 192 + tap * 64
                for h in range(4):
                    xu_ref[at : at + 64, (2 * h + j) * W : (2 * h + j + 1) * W] = up[
                        (2 * i + j) * 64 : (2 * i + j + 1) * 64, h * W : (h + 1) * W
                    ]


def prepare_kernel(
    own_ref, wup_ref, wc_ref, xu_ref, spread_ref, wfu_ref, wfs_ref, wi_ref, wg_ref, skip_ref
):
    select = spread_columns()
    skip_ref[...] = skip_columns()
    upsample(own_ref[...], up_weights(wup_ref), select, xu_ref, 0, spread_ref)
    rows = []
    for b in range(3):
        taps = [wc_ref[9 * a + 3 * b + c] for a in range(3) for c in range(3)]
        rows.append(jnp.concatenate(taps + [jnp.zeros((64, 128), BF16)], axis=1))
    full = jnp.concatenate(rows, axis=0)
    for half, ref in enumerate((wfu_ref, wfs_ref)):
        select = one_hot((256, 128), lambda row, col: row == (col & 63) + 64 * half + 128 * (col >> 6))
        for m in range(5):
            part = mm(full[:, 256 * m : 256 * m + 256], select).astype(BF16)
            if m < 4:
                ref[:, 128 * m : 128 * m + 128] = part
            else:
                ref[:, 512:] = part[:, :64]
    for b in range(3):
        taps = [wc_ref[9 * (2 - jj) + 3 * b + c] for jj in range(3) for c in range(3)]
        wi_ref[b * 128 : (b + 1) * 128, :] = jnp.concatenate(taps, axis=0).T
    wg_ref[...] = jnp.concatenate([wup_ref[2 * ij + k] for k in range(2) for ij in range(4)], axis=0).T


def edge_kernel(
    index_ref, core_ref, cross_ref, wup_ref, own_ref, far_wfu_ref, xu_ref, pre_ref, wfu_ref, sems
):
    pairs = ((far_wfu_ref, wfu_ref), (own_ref, xu_ref.at[384:768]))
    copies = [pltpu.make_async_copy(src, dst, sems.at[i]) for i, (src, dst) in enumerate(pairs)]
    for copy in copies:
        copy.start()
    weights = up_weights(wup_ref)
    select = spread_columns()
    even = index_ref[0] == 0
    near, other = (core_ref[:, :256], cross_ref[:, :256])
    upsample(jnp.where(even, other, near), weights, select, xu_ref, 0)
    upsample(jnp.where(even, near, other), weights, select, xu_ref, 768)
    for copy in copies:
        copy.wait()
    for j in range(4):
        z = mm(wfu_ref[...], xu_ref[j * 192 : j * 192 + 576, :])
        pre_ref[j * 64 : (j + 1) * 64, :] = row_taps(z, 64)


def inner_kernel(
    index_ref,
    edge_ref,
    held_ref,
    held_core_ref,
    cot_ref,
    skip_ref,
    xu_ref,
    pre_up_ref,
    far_wfs_ref,
    far_spread_ref,
    far_wi_ref,
    far_wg_ref,
    xs_ref,
    pre_ref,
    gs_ref,
    act_ref,
    term_ref,
    wfs_ref,
    spread_ref,
    wi_ref,
    wg_ref,
    sems,
):
    pairs = (
        (far_wfs_ref, wfs_ref),
        (far_spread_ref, spread_ref),
        (far_wi_ref, wi_ref),
        (far_wg_ref, wg_ref),
    )
    copies = [pltpu.make_async_copy(src, dst, sems.at[i]) for i, (src, dst) in enumerate(pairs)]
    for copy in copies:
        copy.start()

    def body(odd):
        base = 0 if odd else 2
        place_skip(held_ref[...], skip_ref[...], xs_ref, 384 * odd)
        place_skip(held_core_ref[...], skip_ref[...], xs_ref, 384 * (1 - odd))
        for copy in copies:
            copy.wait()
        shift = shift_columns()
        for j in range(4):
            planes = [e for e in range(j, j + 3) if base <= e < base + 4]
            taps = slice((planes[0] - j) * 192, (planes[-1] - j + 1) * 192)
            rows = slice((planes[0] - base) * 192, (planes[-1] - base + 1) * 192)
            pre = pre_up_ref[j * 64 : (j + 1) * 64, :] + row_taps(mm(wfs_ref[:, taps], xs_ref[rows, :]), 64)
            if (j >= 2) == bool(odd):
                at = (j % 2) * 64
                pre_ref[at : at + 64, :] = pre
                continue
            inner = j in (1, 2)
            cot = cot_ref[:, (j - 1) * 1024 : j * 1024] if inner else edge_cot(edge_ref)
            act, grad = gated(pre, cot)
            place_grad(grad, shift, gs_ref, (j % 2) * 192)
            if inner:
                act_ref[...] = act

                def skip_rows(e, tap):
                    at = (e - base) * 192 + tap * 64
                    return xs_ref[at : at + 64, :]

                term_ref[...] = weight_term(grad, xu_ref, skip_rows, j)

    for_parity(index_ref[0], body)


def main_kernel(
    scale,
    index_ref,
    cross_ref,
    cot_ref,
    edge_ref,
    select_ref,
    xs_ref,
    half_gs_ref,
    half_act_ref,
    xu_ref,
    pre_ref,
    term_ref,
    spread_ref,
    wi_ref,
    wf_ref,
    wg_ref,
    far_act_ref,
    far_gi_ref,
    far_skip_ref,
    keep_ref,
    send_ref,
    xc_ref,
    gs_ref,
    gw_ref,
    act_ref,
    gi_ref,
    skip_ref,
    sems,
):
    core = index_ref[0]
    quad = index_ref[1]
    skip_copy = pltpu.make_async_copy(skip_ref, far_skip_ref, sems.at[3])
    gi_copy = pltpu.make_async_copy(gi_ref, far_gi_ref, sems.at[4])

    def copies_of(odd):
        ready, late = (slice(0, 1024), slice(1024, 2048)) if odd else (slice(1024, 2048), slice(0, 1024))
        return (
            pltpu.make_async_copy(half_gs_ref, gs_ref.at[384 * (1 - odd) : 384 * (2 - odd)], sems.at[0]),
            pltpu.make_async_copy(half_act_ref, far_act_ref.at[:, ready], sems.at[1]),
            pltpu.make_async_copy(act_ref, far_act_ref.at[:, late], sems.at[2]),
        )

    def first(odd):
        gs_copy, ready_copy, late_copy = copies_of(odd)
        gs_copy.start()
        ready_copy.start()
        place_skip(cross_ref[...], select_ref[...], xc_ref, 0)
        shift = shift_columns()
        for j in (2, 3) if odd else (0, 1):
            start = 4 * odd
            planes = [e for e in range(j, j + 3) if start <= e < start + 2]
            taps = slice((planes[0] - j) * 192, (planes[-1] - j + 1) * 192)
            rows = slice((planes[0] - start) * 192, (planes[-1] - start + 1) * 192)
            z = mm(wf_ref[:, taps], xc_ref[rows, :])
            at = (j % 2) * 64
            pre = pre_ref[at : at + 64, :] + row_taps(z, 64)
            inner = j in (1, 2)
            cot = cot_ref[:, (j - 1) * 1024 : j * 1024] if inner else edge_cot(edge_ref)
            act, grad = gated(pre, cot)
            place_grad(grad, shift, gs_ref, j * 192)
            if inner:
                act_ref[...] = act
                late_copy.start()
        gs_copy.wait()

    for_parity(core, first)

    lower = lax.broadcasted_iota(jnp.int32, (64, W), 1) < 64
    ups = []
    skips = []
    for j in range(2):
        z = mm(wi_ref[...], gs_ref[j * 192 : j * 192 + 576, :])
        grad = row_taps_back(z, 128)
        ups.append(grad[:64].astype(BF16))
        skips.append(grad[64:])
    for h in range(8):
        first = skips[0][:, h * W : (h + 1) * W]
        second = skips[1][:, h * W : (h + 1) * W]
        skip_ref[2 * h] = jnp.where(lower, first, pltpu.roll(second, 64, 1)).astype(BF16)
        skip_ref[2 * h + 1] = jnp.where(lower, pltpu.roll(first, 64, 1), second).astype(BF16)

    skip_copy.start()
    tiles = []
    for h in range(4):
        tiles.append(
            jnp.concatenate(
                [ups[i][:, (2 * h + j) * W : (2 * h + j + 1) * W] for i in range(2) for j in range(2)],
                axis=0,
            )
        )
    grad_up = lax.dot_general(
        jnp.concatenate(tiles, axis=1), spread_ref[...], NT, preferred_element_type=F32
    )
    grad_up = grad_up * scale
    for ij in range(4):
        for k in range(2):
            at = (27 + 2 * ij + k) * 64
            gw_ref[at : at + 64, :] = grad_up[ij * 64 : (ij + 1) * 64, k * W : (k + 1) * W]
    gw_ref[35 * 64 :, :] = jnp.zeros((64, W), F32)

    def part_lanes(row, col):
        return ((row >> 7) == ((col >> 6) & 1)) & ((row & 127) == 2 * (col & 63) + (col >> 7))

    apart = one_hot((256, 256), part_lanes)
    halves = [
        mm(jnp.concatenate([tiles[2 * t], tiles[2 * t + 1]], axis=1), apart).astype(BF16) for t in range(2)
    ]
    operand = jnp.concatenate(
        [jnp.concatenate([half[:, k * W : (k + 1) * W] for half in halves], axis=1) for k in range(2)],
        axis=0,
    )
    gi_ref[...] = mm(wg_ref[...], operand).astype(BF16)
    gi_copy.start()

    def second(odd):
        j = 2 if odd else 1

        def skip_rows(e, tap):
            start = 4 * odd
            if start <= e < start + 2:
                ref, at = (xc_ref, (e - start) * 192 + tap * 64)
            else:
                ref, at = (xs_ref, (e - (0 if odd else 2)) * 192 + tap * 64)
            return ref[at : at + 64, :]

        grad = gs_ref[j * 192 + 64 : j * 192 + 128, :]
        total = weight_term(grad, xu_ref, skip_rows, j) + term_ref[...]
        total = (total * scale).T
        for a in range(3):
            for b in range(3):
                for tap in range(3):
                    at = (9 * a + 3 * b + tap) * 64
                    column = (3 * a + tap) * W
                    gw_ref[at : at + 64, :] = total[b * 64 : (b + 1) * 64, column : column + W]
        for done in copies_of(odd)[1:]:
            done.wait()

    for_parity(core, second)

    for k in range(4):
        row = jnp.bitwise_xor(quad, k) * 288
        mine = pl.multiple_of(core * 1152 + row, 32)
        other = pl.multiple_of((1 - core) * 1152 + row, 32)
        keep_ref[k * 288 : (k + 1) * 288, :] = gw_ref[pl.ds(mine, 288), :]
        send_ref[k * 288 : (k + 1) * 288, :] = gw_ref[pl.ds(other, 288), :].astype(BF16)
    for done in (skip_copy, gi_copy):
        done.wait()


def finish_kernel(mine, index_ref, value_ref, *refs):
    conv_ref, up_ref, stage_ref, sems = refs[-4:]
    side = index_ref[0] if mine else 1 - index_ref[0]

    def each(act):
        for k in range(4):
            piece = 4 * side + jnp.bitwise_xor(index_ref[1], k)
            rows = slice(k * 9, k * 9 + 9)

            @pl.when(piece < 6)
            def _():
                dst = conv_ref.at[pl.ds(piece * 9, 9)]
                act(k, pltpu.make_async_copy(stage_ref.at[rows], dst, sems.at[k]))

            @pl.when(piece == 6)
            def _():
                act(k, pltpu.make_async_copy(stage_ref.at[rows], up_ref.at[0:9], sems.at[k]))

            @pl.when(piece == 7)
            def _():
                src = stage_ref.at[k * 9 : k * 9 + 7]
                act(k, pltpu.make_async_copy(src, up_ref.at[9:16], sems.at[k]))

    for k in range(4):
        rows = slice(k * 288, (k + 1) * 288)
        stage_ref[k * 9 : k * 9 + 9] = value_ref[rows, :].astype(F32).reshape(9, 32, 128)
    each(lambda k, copy: copy.start())
    each(lambda k, copy: copy.wait())


def room(mebibytes):
    return pltpu.CompilerParams(vmem_limit_bytes=mebibytes << 20)


VMEM = pl.BlockSpec(memory_space=pltpu.VMEM)
SMEM = pl.BlockSpec(memory_space=pltpu.SMEM)
FAR = pl.BlockSpec(memory_space=pl.ANY)


def far(value):
    return pltpu.with_memory_space_constraint(value, pltpu.HBM)


def near(value):
    return pltpu.with_memory_space_constraint(value, pltpu.VMEM)


def like(shape, dtype=BF16):
    return jax.ShapeDtypeStruct(shape, dtype)


def inside(shape, dtype=BF16):
    return pltpu.VMEM(shape, dtype)


def outside(shape, dtype=BF16):
    return pltpu.HBM(shape, dtype)


def reduce_weights(index, keep, send, back, finish_others, n):
    def swap(value, bit):
        return lax.ppermute(value, AXIS, [(i, i ^ bit) for i in range(n)])

    summed = keep + swap(send, 1).astype(F32)
    rounded = summed.astype(BF16)
    total = summed[:288]
    for k in (1, 2, 3):
        total = total + swap(rounded[k * 288 : (k + 1) * 288], 2 * k).astype(F32)
    total, back = lax.optimization_barrier((total, back))
    bit = 8
    while bit < n:
        own = total.astype(BF16)
        total = own.astype(F32) + swap(own, bit).astype(F32)
        bit *= 2
    own = total.astype(BF16)
    pieces = [own] + [swap(own, 2 * k) for k in (1, 2, 3)]
    pieces, others = lax.optimization_barrier((pieces, finish_others(back)))
    mine = jnp.concatenate(pieces, axis=0)
    other = swap(mine, 1)
    sums = ()
    for first, value in ((True, mine), (False, other)):
        sums = pl.pallas_call(
            functools.partial(finish_kernel, first),
            out_shape=(outside((54, 32, 128), F32), outside((16, 32, 128), F32)),
            in_specs=[SMEM, VMEM] + [FAR] * len(sums),
            out_specs=(FAR, FAR),
            scratch_shapes=[pltpu.VMEM((36, 32, 128), F32), pltpu.SemaphoreType.DMA((4,))],
            input_output_aliases={} if first else {2: 0, 3: 1},
            compiler_params=room(6),
            cost_estimate=pl.CostEstimate(flops=1200000000, bytes_accessed=1000000, transcendentals=0),
            name="finish",
        )(index, value, *sums)
    conv, up = sums
    return conv.reshape(27, 64, 128), up.reshape(8, 64, 128), others


def local(coarse_input, skip, cotangent, w_up, w_conv):
    n = lax.axis_size(AXIS)
    cells = cotangent.shape[2]
    planes = cotangent.shape[1]
    positions = skip.shape[2]
    core_pairs = [(i, i ^ 1) for i in range(n)]
    cross_pairs = [(i, i + 1 if i % 2 else i - 1) for i in range(1, n - 1)]
    me = lax.axis_index(AXIS)
    index = jnp.stack([me & 1, (me >> 1) & 3]).astype(jnp.int32)

    sent = skip.reshape(64, n, 2 * positions).transpose(1, 0, 2)
    held = lax.all_to_all(sent, AXIS, split_axis=0, concat_axis=0, tiled=True)
    if positions != 64:
        held = held.reshape(n, 64, 2, positions).transpose(1, 2, 0, 3).reshape(64, 2, 16, 64)
        held = held.transpose(2, 0, 1, 3).reshape(16, 64, 128)

    coarse = coarse_input.reshape(128, 256)
    flat = lax.optimization_barrier(cotangent.reshape(64, 2048))

    def edge(plane):
        halves = [lax.dynamic_slice_in_dim(flat, 1024 * plane + 512 * i, 512, 1) for i in range(2)]
        return jnp.concatenate([coarse, jnp.concatenate(halves, axis=0)], axis=1)

    edge_core = lax.ppermute(edge(1 - index[0]), AXIS, core_pairs)
    edge_cross = lax.ppermute(edge(index[0]), AXIS, cross_pairs)
    xu, spread, wf_up, wf_skip, wi, wg, pick_skip = pl.pallas_call(
        prepare_kernel,
        out_shape=(
            inside((384, 1024)),
            outside((256, 512)),
            outside((192, 576)),
            outside((192, 576)),
            outside((384, 576)),
            outside((128, 512)),
            inside((256, 768)),
        ),
        in_specs=[VMEM] * 3,
        out_specs=(VMEM,) * 7,
        compiler_params=room(8),
        cost_estimate=pl.CostEstimate(flops=1840000000, bytes_accessed=1000000, transcendentals=0),
        name="prepare",
    )(coarse, w_up, w_conv)
    held, wf_up = lax.optimization_barrier((held, wf_up))
    held_core = lax.ppermute(held, AXIS, core_pairs)
    held_cross = lax.ppermute(held, AXIS, cross_pairs)
    held, held_core, held_cross = [v.reshape(8, 2, 64, 128) for v in (held, held_core, held_cross)]
    xu, pre_up = pl.pallas_call(
        edge_kernel,
        out_shape=(inside((1152, 1024)), inside((256, 1024), F32)),
        in_specs=[SMEM] + [VMEM] * 4 + [FAR],
        out_specs=(VMEM,) * 2,
        scratch_shapes=[pltpu.VMEM((192, 576), BF16), pltpu.SemaphoreType.DMA((2,))],
        compiler_params=room(16),
        cost_estimate=pl.CostEstimate(flops=3000000000, bytes_accessed=1000000, transcendentals=0),
        name="edges",
    )(index, near(edge_core), near(edge_cross), w_up, near(xu), far(wf_up))
    xs, pre, half_gs, half_act, term, wf_skip, spread, wi, wg = pl.pallas_call(
        inner_kernel,
        out_shape=(
            inside((768, 1024)),
            inside((128, 1024), F32),
            inside((384, 1024)),
            inside((64, 1024)),
            inside((1152, 192), F32),
            inside((192, 576)),
            inside((256, 512)),
            inside((384, 576)),
            inside((128, 512)),
        ),
        in_specs=[SMEM] + [VMEM] * 7 + [FAR] * 4,
        out_specs=(VMEM,) * 9,
        scratch_shapes=[pltpu.SemaphoreType.DMA((4,))],
        compiler_params=room(20),
        cost_estimate=pl.CostEstimate(flops=4000000000, bytes_accessed=1000000, transcendentals=0),
        name="inner",
    )(
        index,
        *(near(v) for v in (edge_core, held, held_core, flat, pick_skip, xu, pre_up)),
        *(far(v) for v in (wf_skip, spread, wi, wg)),
    )

    scale = 1.0 / math.sqrt(n * planes * cells)
    act, gi, skip_part, keep, send = pl.pallas_call(
        functools.partial(main_kernel, scale),
        out_shape=(
            outside((64, 2048)),
            outside((128, 256)),
            outside((16, 64, 128)),
            inside((1152, 128), F32),
            inside((1152, 128)),
        ),
        in_specs=[SMEM] + [VMEM] * 14,
        out_specs=(FAR,) * 3 + (VMEM,) * 2,
        scratch_shapes=[
            pltpu.VMEM((384, 1024), BF16),
            pltpu.VMEM((768, 1024), BF16),
            pltpu.VMEM((2304, 128), F32),
            pltpu.VMEM((64, 1024), BF16),
            pltpu.VMEM((128, 256), BF16),
            pltpu.VMEM((16, 64, 128), BF16),
            pltpu.SemaphoreType.DMA((5,)),
        ],
        compiler_params=room(24),
        cost_estimate=pl.CostEstimate(flops=8280000000, bytes_accessed=1000000, transcendentals=0),
        name="section",
    )(
        index,
        *(
            near(v)
            for v in (
                held_cross,
                flat,
                edge_cross,
                pick_skip,
                xs,
                half_gs,
                half_act,
                xu,
                pre,
                term,
                spread,
                wi,
                wf_skip,
                wg,
            )
        ),
    )
    if positions != 64:
        skip_part = skip_part.reshape(16, 64, 2, 64).transpose(1, 2, 0, 3)
        skip_part = skip_part.reshape(64, 2, n, positions).transpose(2, 0, 1, 3)
        skip_part = skip_part.reshape(n, 64, 2 * positions)
    back = lax.all_to_all(skip_part, AXIS, split_axis=0, concat_axis=0, tiled=True)

    def others(back):
        return (
            act.reshape(64, planes, cells),
            gi.reshape(128, 1, 256),
            back.transpose(1, 0, 2).reshape(64, 2 * n, positions),
        )

    grad_w_conv, grad_w_up, rest = reduce_weights(index, keep, send, back, others, n)
    return (*rest, grad_w_up, grad_w_conv)


def solution(mesh):
    spec = jax.sharding.PartitionSpec
    in_specs = (
        spec("groups", "space", None),
        spec("groups", None, "space"),
        spec("groups", "space", None),
        spec(),
        spec(),
    )
    out_specs = (
        spec("groups", "space", None),
        spec("groups", "space", None),
        spec("groups", None, "space"),
        spec("groups", None, None),
        spec("groups", None, None),
    )
    return jax.shard_map(local, mesh=mesh, in_specs=in_specs, out_specs=out_specs, check_vma=False)
```

```python
import functools
import math

import jax
import jax.numpy as jnp
from jax import lax
from jax.experimental import pallas as pl
from jax.experimental.pallas import tpu as pltpu

W = 128
AXIS = "space"
BF16 = jnp.bfloat16
F32 = jnp.float32
NT = (((1,), (1,)), ((), ()))


def mm(a, b):
    return jnp.dot(a, b, preferred_element_type=F32)


def one_hot(shape, cond):
    rows = lax.broadcasted_iota(jnp.int32, shape, 0)
    cols = lax.broadcasted_iota(jnp.int32, shape, 1)
    return jnp.where(cond(rows, cols), 1.0, 0.0).astype(BF16)


def row_taps(z, channels):
    zero = jnp.zeros((channels, W), F32)
    low = jnp.concatenate([zero, z[:channels, :-W]], axis=1)
    high = jnp.concatenate([z[2 * channels :, W:], zero], axis=1)
    return z[channels : 2 * channels] + low + high


def row_taps_back(z, channels):
    zero = jnp.zeros((channels, W), F32)
    low = jnp.concatenate([z[:channels, W:], zero], axis=1)
    high = jnp.concatenate([zero, z[2 * channels :, :-W]], axis=1)
    return z[channels : 2 * channels] + low + high


def spread_columns():
    def pick(lane_in, col):
        tap, k, parity, lane = (col >> 9, (col >> 8) & 1, (col >> 7) & 1, col & 127)
        return ((lane_in >> 6) == parity) & (2 * (lane_in & 63) + k == lane + tap - 1)

    return one_hot((128, 1536), pick)


def skip_columns():
    def pick(row, col):
        out = jnp.where(col >= 384, 1, 0)
        rest = col - 384 * out
        tap, lane = (rest >> 7, rest & 127)
        return (((row >> 6) & 1) == out) & ((row >> 7) * 64 + (row & 63) == lane + tap - 1)

    return one_hot((256, 768), pick)


def place_skip(value, select, xs_ref, base):
    joined = jnp.concatenate([value[:, 0].reshape(512, 128), value[:, 1].reshape(512, 128)], axis=1)
    placed = mm(joined, select).astype(BF16)
    for parity in range(2):
        for tap in range(3):
            at = base + parity * 192 + tap * 64
            for h in range(8):
                xs_ref[at : at + 64, h * W : (h + 1) * W] = placed[
                    h * 64 : (h + 1) * 64, (3 * parity + tap) * W : (3 * parity + tap + 1) * W
                ]


def shift_columns():
    return one_hot((128, 256), lambda row, col: row == (col & 127) + 1 - 2 * (col >> 7))


def gated(pre, cot):
    gate = 1.0 / (1.0 + jnp.exp(-pre))
    grad = (cot.astype(F32) * gate * (1.0 + pre * (1.0 - gate))).astype(BF16)
    return (pre * gate).astype(BF16), grad


def place_grad(grad, shift, gs_ref, base):
    gs_ref[base + 64 : base + 128, :] = grad
    tall = jnp.concatenate([grad[:, h * W : (h + 1) * W] for h in range(8)], axis=0)
    moved = mm(tall, shift).astype(BF16)
    for side in range(2):
        at = base + side * 128
        for h in range(8):
            gs_ref[at : at + 64, h * W : (h + 1) * W] = moved[
                h * 64 : (h + 1) * 64, side * W : side * W + W
            ]


def weight_term(grad, xu_ref, skip_rows, first):
    zero = jnp.zeros((64, W), BF16)
    low = jnp.concatenate([grad[:, W:], zero], axis=1)
    high = jnp.concatenate([zero, grad[:, :-W]], axis=1)
    pieces = []
    for e in range(first, first + 3):
        for tap in range(3):
            at = e * 192 + tap * 64
            pieces += [xu_ref[at : at + 64, :], skip_rows(e, tap)]
    rows = jnp.concatenate([low, grad, high], axis=0)
    return lax.dot_general(jnp.concatenate(pieces, axis=0), rows, NT, preferred_element_type=F32)


def edge_cot(edge_ref):
    return jnp.concatenate([edge_ref[:64, 256:], edge_ref[64:, 256:]], axis=1)


def position():
    me = lax.axis_index(AXIS)
    return me & 1, (me >> 1) & 3


def for_parity(core, body):
    @pl.when(core == 0)
    def _():
        body(0)

    @pl.when(core == 1)
    def _():
        body(1)


def up_weights(wup_ref):
    return jnp.concatenate(
        [jnp.concatenate([wup_ref[2 * ij], wup_ref[2 * ij + 1]], axis=1) for ij in range(4)], axis=0
    )


def upsample(coarse, weights, select, xu_ref, base, spread_ref=None):
    spread = [mm(coarse[:, 128 * t : 128 * t + 128], select).astype(BF16) for t in range(2)]
    for tap in range(3):
        columns = []
        for h in range(4):
            at = 512 * tap + 128 * (h & 1)
            piece = spread[h >> 1]
            columns.append(jnp.concatenate([piece[:, at : at + 128], piece[:, at + 256 : at + 384]], axis=0))
        operand = jnp.concatenate(columns, axis=1)
        if spread_ref is not None and tap == 1:
            spread_ref[...] = operand
        up = mm(weights, operand).astype(BF16)
        for i in range(2):
            for j in range(2):
                at = base + i * 192 + tap * 64
                for h in range(4):
                    xu_ref[at : at + 64, (2 * h + j) * W : (2 * h + j + 1) * W] = up[
                        (2 * i + j) * 64 : (2 * i + j + 1) * 64, h * W : (h + 1) * W
                    ]


def prepare_kernel(
    own_ref, wup_ref, wc_ref, xu_ref, spread_ref, wfu_ref, wfs_ref, wi_ref, wg_ref, skip_ref
):
    select = spread_columns()
    skip_ref[...] = skip_columns()
    upsample(own_ref[...], up_weights(wup_ref), select, xu_ref, 0, spread_ref)
    rows = []
    for b in range(3):
        taps = [wc_ref[9 * a + 3 * b + c] for a in range(3) for c in range(3)]
        rows.append(jnp.concatenate(taps + [jnp.zeros((64, 128), BF16)], axis=1))
    full = jnp.concatenate(rows, axis=0)
    for half, ref in enumerate((wfu_ref, wfs_ref)):
        select = one_hot((256, 128), lambda row, col: row == (col & 63) + 64 * half + 128 * (col >> 6))
        for m in range(5):
            part = mm(full[:, 256 * m : 256 * m + 256], select).astype(BF16)
            if m < 4:
                ref[:, 128 * m : 128 * m + 128] = part
            else:
                ref[:, 512:] = part[:, :64]
    for b in range(3):
        taps = [wc_ref[9 * (2 - jj) + 3 * b + c] for jj in range(3) for c in range(3)]
        wi_ref[b * 128 : (b + 1) * 128, :] = jnp.concatenate(taps, axis=0).T
    wg_ref[...] = jnp.concatenate([wup_ref[2 * ij + k] for k in range(2) for ij in range(4)], axis=0).T


def edge_kernel(
    core_ref, cross_ref, wup_ref, own_ref, far_wfu_ref, xu_ref, pre_ref, wfu_ref, sems
):
    pairs = ((far_wfu_ref, wfu_ref), (own_ref, xu_ref.at[384:768]))
    copies = [pltpu.make_async_copy(src, dst, sems.at[i]) for i, (src, dst) in enumerate(pairs)]
    for copy in copies:
        copy.start()
    weights = up_weights(wup_ref)
    select = spread_columns()
    even = position()[0] == 0
    near, other = (core_ref[:, :256], cross_ref[:, :256])
    upsample(jnp.where(even, other, near), weights, select, xu_ref, 0)
    upsample(jnp.where(even, near, other), weights, select, xu_ref, 768)
    for copy in copies:
        copy.wait()
    for j in range(4):
        z = mm(wfu_ref[...], xu_ref[j * 192 : j * 192 + 576, :])
        pre_ref[j * 64 : (j + 1) * 64, :] = row_taps(z, 64)


def inner_kernel(
    edge_ref,
    held_ref,
    held_core_ref,
    cot_ref,
    skip_ref,
    xu_ref,
    pre_up_ref,
    far_wfs_ref,
    far_spread_ref,
    far_wi_ref,
    far_wg_ref,
    xs_ref,
    pre_ref,
    gs_ref,
    act_ref,
    term_ref,
    wfs_ref,
    spread_ref,
    wi_ref,
    wg_ref,
    sems,
):
    pairs = (
        (far_wfs_ref, wfs_ref),
        (far_spread_ref, spread_ref),
        (far_wi_ref, wi_ref),
        (far_wg_ref, wg_ref),
    )
    copies = [pltpu.make_async_copy(src, dst, sems.at[i]) for i, (src, dst) in enumerate(pairs)]
    for copy in copies:
        copy.start()

    def body(odd):
        base = 0 if odd else 2
        place_skip(held_ref[...], skip_ref[...], xs_ref, 384 * odd)
        place_skip(held_core_ref[...], skip_ref[...], xs_ref, 384 * (1 - odd))
        for copy in copies:
            copy.wait()
        shift = shift_columns()
        for j in range(4):
            planes = [e for e in range(j, j + 3) if base <= e < base + 4]
            taps = slice((planes[0] - j) * 192, (planes[-1] - j + 1) * 192)
            rows = slice((planes[0] - base) * 192, (planes[-1] - base + 1) * 192)
            pre = pre_up_ref[j * 64 : (j + 1) * 64, :] + row_taps(mm(wfs_ref[:, taps], xs_ref[rows, :]), 64)
            if (j >= 2) == bool(odd):
                at = (j % 2) * 64
                pre_ref[at : at + 64, :] = pre
                continue
            inner = j in (1, 2)
            cot = cot_ref[:, (j - 1) * 1024 : j * 1024] if inner else edge_cot(edge_ref)
            act, grad = gated(pre, cot)
            place_grad(grad, shift, gs_ref, (j % 2) * 192)
            if inner:
                act_ref[...] = act

                def skip_rows(e, tap):
                    at = (e - base) * 192 + tap * 64
                    return xs_ref[at : at + 64, :]

                term_ref[...] = weight_term(grad, xu_ref, skip_rows, j)

    for_parity(position()[0], body)


def main_kernel(
    scale,
    cross_ref,
    cot_ref,
    edge_ref,
    select_ref,
    xs_ref,
    half_gs_ref,
    half_act_ref,
    xu_ref,
    pre_ref,
    term_ref,
    spread_ref,
    wi_ref,
    wf_ref,
    wg_ref,
    far_act_ref,
    far_gi_ref,
    far_skip_ref,
    keep_ref,
    send_ref,
    xc_ref,
    gs_ref,
    gw_ref,
    act_ref,
    gi_ref,
    skip_ref,
    sems,
):
    core, quad = position()
    skip_copy = pltpu.make_async_copy(skip_ref, far_skip_ref, sems.at[3])
    gi_copy = pltpu.make_async_copy(gi_ref, far_gi_ref, sems.at[4])

    def copies_of(odd):
        ready, late = (slice(0, 1024), slice(1024, 2048)) if odd else (slice(1024, 2048), slice(0, 1024))
        return (
            pltpu.make_async_copy(half_gs_ref, gs_ref.at[384 * (1 - odd) : 384 * (2 - odd)], sems.at[0]),
            pltpu.make_async_copy(half_act_ref, far_act_ref.at[:, ready], sems.at[1]),
            pltpu.make_async_copy(act_ref, far_act_ref.at[:, late], sems.at[2]),
        )

    def first(odd):
        gs_copy, ready_copy, late_copy = copies_of(odd)
        gs_copy.start()
        ready_copy.start()
        place_skip(cross_ref[...], select_ref[...], xc_ref, 0)
        shift = shift_columns()
        for j in (2, 3) if odd else (0, 1):
            start = 4 * odd
            planes = [e for e in range(j, j + 3) if start <= e < start + 2]
            taps = slice((planes[0] - j) * 192, (planes[-1] - j + 1) * 192)
            rows = slice((planes[0] - start) * 192, (planes[-1] - start + 1) * 192)
            z = mm(wf_ref[:, taps], xc_ref[rows, :])
            at = (j % 2) * 64
            pre = pre_ref[at : at + 64, :] + row_taps(z, 64)
            inner = j in (1, 2)
            cot = cot_ref[:, (j - 1) * 1024 : j * 1024] if inner else edge_cot(edge_ref)
            act, grad = gated(pre, cot)
            place_grad(grad, shift, gs_ref, j * 192)
            if inner:
                act_ref[...] = act
                late_copy.start()
        gs_copy.wait()

    for_parity(core, first)

    lower = lax.broadcasted_iota(jnp.int32, (64, W), 1) < 64
    ups = []
    skips = []
    for j in range(2):
        z = mm(wi_ref[...], gs_ref[j * 192 : j * 192 + 576, :])
        grad = row_taps_back(z, 128)
        ups.append(grad[:64].astype(BF16))
        skips.append(grad[64:])
    for h in range(8):
        first = skips[0][:, h * W : (h + 1) * W]
        second = skips[1][:, h * W : (h + 1) * W]
        skip_ref[2 * h] = jnp.where(lower, first, pltpu.roll(second, 64, 1)).astype(BF16)
        skip_ref[2 * h + 1] = jnp.where(lower, pltpu.roll(first, 64, 1), second).astype(BF16)

    skip_copy.start()
    tiles = []
    for h in range(4):
        tiles.append(
            jnp.concatenate(
                [ups[i][:, (2 * h + j) * W : (2 * h + j + 1) * W] for i in range(2) for j in range(2)],
                axis=0,
            )
        )
    grad_up = lax.dot_general(
        jnp.concatenate(tiles, axis=1), spread_ref[...], NT, preferred_element_type=F32
    )
    grad_up = grad_up * scale
    for ij in range(4):
        for k in range(2):
            at = (27 + 2 * ij + k) * 64
            gw_ref[at : at + 64, :] = grad_up[ij * 64 : (ij + 1) * 64, k * W : (k + 1) * W]
    gw_ref[35 * 64 :, :] = jnp.zeros((64, W), F32)

    def part_lanes(row, col):
        return ((row >> 7) == ((col >> 6) & 1)) & ((row & 127) == 2 * (col & 63) + (col >> 7))

    apart = one_hot((256, 256), part_lanes)
    halves = [
        mm(jnp.concatenate([tiles[2 * t], tiles[2 * t + 1]], axis=1), apart).astype(BF16) for t in range(2)
    ]
    operand = jnp.concatenate(
        [jnp.concatenate([half[:, k * W : (k + 1) * W] for half in halves], axis=1) for k in range(2)],
        axis=0,
    )
    gi_ref[...] = mm(wg_ref[...], operand).astype(BF16)
    gi_copy.start()

    def second(odd):
        j = 2 if odd else 1

        def skip_rows(e, tap):
            start = 4 * odd
            if start <= e < start + 2:
                ref, at = (xc_ref, (e - start) * 192 + tap * 64)
            else:
                ref, at = (xs_ref, (e - (0 if odd else 2)) * 192 + tap * 64)
            return ref[at : at + 64, :]

        grad = gs_ref[j * 192 + 64 : j * 192 + 128, :]
        total = weight_term(grad, xu_ref, skip_rows, j) + term_ref[...]
        total = (total * scale).T
        for a in range(3):
            for b in range(3):
                for tap in range(3):
                    at = (9 * a + 3 * b + tap) * 64
                    column = (3 * a + tap) * W
                    gw_ref[at : at + 64, :] = total[b * 64 : (b + 1) * 64, column : column + W]
        for done in copies_of(odd)[1:]:
            done.wait()

    for_parity(core, second)

    for k in range(4):
        row = jnp.bitwise_xor(quad, k) * 288
        mine = pl.multiple_of(core * 1152 + row, 32)
        other = pl.multiple_of((1 - core) * 1152 + row, 32)
        keep_ref[k * 288 : (k + 1) * 288, :] = gw_ref[pl.ds(mine, 288), :]
        send_ref[k * 288 : (k + 1) * 288, :] = gw_ref[pl.ds(other, 288), :].astype(BF16)
    for done in (skip_copy, gi_copy):
        done.wait()


def finish_kernel(mine, value_ref, *refs):
    conv_ref, up_ref, stage_ref, sems = refs[-4:]
    core, quad = position()
    side = core if mine else 1 - core

    def each(act):
        for k in range(4):
            piece = 4 * side + jnp.bitwise_xor(quad, k)
            rows = slice(k * 9, k * 9 + 9)

            @pl.when(piece < 6)
            def _():
                dst = conv_ref.at[pl.ds(piece * 9, 9)]
                act(k, pltpu.make_async_copy(stage_ref.at[rows], dst, sems.at[k]))

            @pl.when(piece == 6)
            def _():
                act(k, pltpu.make_async_copy(stage_ref.at[rows], up_ref.at[0:9], sems.at[k]))

            @pl.when(piece == 7)
            def _():
                src = stage_ref.at[k * 9 : k * 9 + 7]
                act(k, pltpu.make_async_copy(src, up_ref.at[9:16], sems.at[k]))

    for k in range(4):
        rows = slice(k * 288, (k + 1) * 288)
        stage_ref[k * 9 : k * 9 + 9] = value_ref[rows, :].astype(F32).reshape(9, 32, 128)
    each(lambda k, copy: copy.start())
    each(lambda k, copy: copy.wait())


def room(mebibytes):
    return pltpu.CompilerParams(vmem_limit_bytes=mebibytes << 20)


VMEM = pl.BlockSpec(memory_space=pltpu.VMEM)
FAR = pl.BlockSpec(memory_space=pl.ANY)


def far(value):
    return pltpu.with_memory_space_constraint(value, pltpu.HBM)


def near(value):
    return pltpu.with_memory_space_constraint(value, pltpu.VMEM)


def like(shape, dtype=BF16):
    return jax.ShapeDtypeStruct(shape, dtype)


def inside(shape, dtype=BF16):
    return pltpu.VMEM(shape, dtype)


def outside(shape, dtype=BF16):
    return pltpu.HBM(shape, dtype)


def reduce_weights(keep, send, back, finish_others, n):
    def swap(value, bit):
        return lax.ppermute(value, AXIS, [(i, i ^ bit) for i in range(n)])

    summed = keep + swap(send, 1).astype(F32)
    rounded = summed.astype(BF16)
    total = summed[:288]
    for k in (1, 2, 3):
        total = total + swap(rounded[k * 288 : (k + 1) * 288], 2 * k).astype(F32)
    total, back = lax.optimization_barrier((total, back))
    bit = 8
    while bit < n:
        own = total.astype(BF16)
        total = own.astype(F32) + swap(own, bit).astype(F32)
        bit *= 2
    own = total.astype(BF16)
    pieces = [own] + [swap(own, 2 * k) for k in (1, 2, 3)]
    pieces, others = lax.optimization_barrier((pieces, finish_others(back)))
    mine = jnp.concatenate(pieces, axis=0)
    other = swap(mine, 1)
    sums = ()
    for first, value in ((True, mine), (False, other)):
        sums = pl.pallas_call(
            functools.partial(finish_kernel, first),
            out_shape=(outside((54, 32, 128), F32), outside((16, 32, 128), F32)),
            in_specs=[VMEM] + [FAR] * len(sums),
            out_specs=(FAR, FAR),
            scratch_shapes=[pltpu.VMEM((36, 32, 128), F32), pltpu.SemaphoreType.DMA((4,))],
            input_output_aliases={} if first else {1: 0, 2: 1},
            compiler_params=room(6),
            cost_estimate=pl.CostEstimate(flops=1200000000, bytes_accessed=1000000, transcendentals=0),
            name="finish",
        )(near(value), *sums)
    conv, up = sums
    return conv.reshape(27, 64, 128), up.reshape(8, 64, 128), others


def local(coarse_input, skip, cotangent, w_up, w_conv):
    n = lax.axis_size(AXIS)
    cells = cotangent.shape[2]
    planes = cotangent.shape[1]
    positions = skip.shape[2]
    core_pairs = [(i, i ^ 1) for i in range(n)]
    cross_pairs = [(i, i + 1 if i % 2 else i - 1) for i in range(1, n - 1)]
    me = lax.axis_index(AXIS)
    core = me & 1

    sent = skip.reshape(64, n, 2 * positions).transpose(1, 0, 2)
    held = lax.all_to_all(sent, AXIS, split_axis=0, concat_axis=0, tiled=True)
    if positions != 64:
        held = held.reshape(n, 64, 2, positions).transpose(1, 2, 0, 3).reshape(64, 2, 16, 64)
        held = held.transpose(2, 0, 1, 3).reshape(16, 64, 128)

    coarse = coarse_input.reshape(128, 256)
    flat = lax.optimization_barrier(cotangent.reshape(64, 2048))

    def edge(plane):
        halves = [lax.dynamic_slice_in_dim(flat, 1024 * plane + 512 * i, 512, 1) for i in range(2)]
        return jnp.concatenate([coarse, jnp.concatenate(halves, axis=0)], axis=1)

    edge_core = lax.ppermute(edge(1 - core), AXIS, core_pairs)
    edge_cross = lax.ppermute(edge(core), AXIS, cross_pairs)
    xu, spread, wf_up, wf_skip, wi, wg, pick_skip = pl.pallas_call(
        prepare_kernel,
        out_shape=(
            inside((384, 1024)),
            outside((256, 512)),
            outside((192, 576)),
            outside((192, 576)),
            outside((384, 576)),
            outside((128, 512)),
            inside((256, 768)),
        ),
        in_specs=[VMEM] * 3,
        out_specs=(VMEM,) * 7,
        compiler_params=room(8),
        cost_estimate=pl.CostEstimate(flops=1840000000, bytes_accessed=1000000, transcendentals=0),
        name="prepare",
    )(coarse, w_up, w_conv)
    held, wf_up = lax.optimization_barrier((held, wf_up))
    held_core = lax.ppermute(held, AXIS, core_pairs)
    held_cross = lax.ppermute(held, AXIS, cross_pairs)
    held, held_core, held_cross = [v.reshape(8, 2, 64, 128) for v in (held, held_core, held_cross)]
    xu, pre_up = pl.pallas_call(
        edge_kernel,
        out_shape=(inside((1152, 1024)), inside((256, 1024), F32)),
        in_specs=[VMEM] * 4 + [FAR],
        out_specs=(VMEM,) * 2,
        scratch_shapes=[pltpu.VMEM((192, 576), BF16), pltpu.SemaphoreType.DMA((2,))],
        compiler_params=room(16),
        cost_estimate=pl.CostEstimate(flops=3000000000, bytes_accessed=1000000, transcendentals=0),
        name="edges",
    )(near(edge_core), near(edge_cross), w_up, near(xu), far(wf_up))
    xs, pre, half_gs, half_act, term, wf_skip, spread, wi, wg = pl.pallas_call(
        inner_kernel,
        out_shape=(
            inside((768, 1024)),
            inside((128, 1024), F32),
            inside((384, 1024)),
            inside((64, 1024)),
            inside((1152, 192), F32),
            inside((192, 576)),
            inside((256, 512)),
            inside((384, 576)),
            inside((128, 512)),
        ),
        in_specs=[VMEM] * 7 + [FAR] * 4,
        out_specs=(VMEM,) * 9,
        scratch_shapes=[pltpu.SemaphoreType.DMA((4,))],
        compiler_params=room(20),
        cost_estimate=pl.CostEstimate(flops=4000000000, bytes_accessed=1000000, transcendentals=0),
        name="inner",
    )(
        *(near(v) for v in (edge_core, held, held_core, flat, pick_skip, xu, pre_up)),
        *(far(v) for v in (wf_skip, spread, wi, wg)),
    )

    scale = 1.0 / math.sqrt(n * planes * cells)
    act, gi, skip_part, keep, send = pl.pallas_call(
        functools.partial(main_kernel, scale),
        out_shape=(
            outside((64, 2048)),
            outside((128, 256)),
            outside((16, 64, 128)),
            inside((1152, 128), F32),
            inside((1152, 128)),
        ),
        in_specs=[VMEM] * 14,
        out_specs=(FAR,) * 3 + (VMEM,) * 2,
        scratch_shapes=[
            pltpu.VMEM((384, 1024), BF16),
            pltpu.VMEM((768, 1024), BF16),
            pltpu.VMEM((2304, 128), F32),
            pltpu.VMEM((64, 1024), BF16),
            pltpu.VMEM((128, 256), BF16),
            pltpu.VMEM((16, 64, 128), BF16),
            pltpu.SemaphoreType.DMA((5,)),
        ],
        compiler_params=room(24),
        cost_estimate=pl.CostEstimate(flops=8280000000, bytes_accessed=1000000, transcendentals=0),
        name="section",
    )(
        *(
            near(v)
            for v in (
                held_cross,
                flat,
                edge_cross,
                pick_skip,
                xs,
                half_gs,
                half_act,
                xu,
                pre,
                term,
                spread,
                wi,
                wf_skip,
                wg,
            )
        ),
    )
    if positions != 64:
        skip_part = skip_part.reshape(16, 64, 2, 64).transpose(1, 2, 0, 3)
        skip_part = skip_part.reshape(64, 2, n, positions).transpose(2, 0, 1, 3)
        skip_part = skip_part.reshape(n, 64, 2 * positions)
    back = lax.all_to_all(skip_part, AXIS, split_axis=0, concat_axis=0, tiled=True)

    def others(back):
        return (
            act.reshape(64, planes, cells),
            gi.reshape(128, 1, 256),
            back.transpose(1, 0, 2).reshape(64, 2 * n, positions),
        )

    grad_w_conv, grad_w_up, rest = reduce_weights(keep, send, back, others, n)
    return (*rest, grad_w_up, grad_w_conv)


def solution(mesh):
    spec = jax.sharding.PartitionSpec
    in_specs = (
        spec("groups", "space", None),
        spec("groups", None, "space"),
        spec("groups", "space", None),
        spec(),
        spec(),
    )
    out_specs = (
        spec("groups", "space", None),
        spec("groups", "space", None),
        spec("groups", None, "space"),
        spec("groups", None, None),
        spec("groups", None, None),
    )
    return jax.shard_map(local, mesh=mesh, in_specs=in_specs, out_specs=out_specs, check_vma=False)
```

```python
import functools
import math

import jax
import jax.numpy as jnp
from jax import lax
from jax.experimental import pallas as pl
from jax.experimental.pallas import tpu as pltpu

W = 128
AXIS = "space"
BF16 = jnp.bfloat16
F32 = jnp.float32
NT = (((1,), (1,)), ((), ()))


def mm(a, b):
    return jnp.dot(a, b, preferred_element_type=F32)


def one_hot(shape, cond):
    rows = lax.broadcasted_iota(jnp.int32, shape, 0)
    cols = lax.broadcasted_iota(jnp.int32, shape, 1)
    return jnp.where(cond(rows, cols), 1.0, 0.0).astype(BF16)


def row_taps(z, channels):
    zero = jnp.zeros((channels, W), F32)
    low = jnp.concatenate([zero, z[:channels, :-W]], axis=1)
    high = jnp.concatenate([z[2 * channels :, W:], zero], axis=1)
    return z[channels : 2 * channels] + low + high


def row_taps_back(z, channels):
    zero = jnp.zeros((channels, W), F32)
    low = jnp.concatenate([z[:channels, W:], zero], axis=1)
    high = jnp.concatenate([zero, z[2 * channels :, :-W]], axis=1)
    return z[channels : 2 * channels] + low + high


def spread_columns():
    def pick(lane_in, col):
        tap, k, parity, lane = (col >> 9, (col >> 8) & 1, (col >> 7) & 1, col & 127)
        return ((lane_in >> 6) == parity) & (2 * (lane_in & 63) + k == lane + tap - 1)

    return one_hot((128, 1536), pick)


def skip_columns():
    def pick(row, col):
        out = jnp.where(col >= 384, 1, 0)
        rest = col - 384 * out
        tap, lane = (rest >> 7, rest & 127)
        return (((row >> 6) & 1) == out) & ((row >> 7) * 64 + (row & 63) == lane + tap - 1)

    return one_hot((256, 768), pick)


def place_skip(value, select, xs_ref, base):
    joined = jnp.concatenate([value[:, 0].reshape(512, 128), value[:, 1].reshape(512, 128)], axis=1)
    placed = mm(joined, select).astype(BF16)
    for parity in range(2):
        for tap in range(3):
            at = base + parity * 192 + tap * 64
            for h in range(8):
                xs_ref[at : at + 64, h * W : (h + 1) * W] = placed[
                    h * 64 : (h + 1) * 64, (3 * parity + tap) * W : (3 * parity + tap + 1) * W
                ]


def shift_columns():
    return one_hot((128, 256), lambda row, col: row == (col & 127) + 1 - 2 * (col >> 7))


def gated(pre, cot):
    gate = 1.0 / (1.0 + jnp.exp(-pre))
    grad = (cot.astype(F32) * gate * (1.0 + pre * (1.0 - gate))).astype(BF16)
    return (pre * gate).astype(BF16), grad


def place_grad(grad, shift, gs_ref, base):
    gs_ref[base + 64 : base + 128, :] = grad
    tall = jnp.concatenate([grad[:, h * W : (h + 1) * W] for h in range(8)], axis=0)
    moved = mm(tall, shift).astype(BF16)
    for side in range(2):
        at = base + side * 128
        for h in range(8):
            gs_ref[at : at + 64, h * W : (h + 1) * W] = moved[
                h * 64 : (h + 1) * 64, side * W : side * W + W
            ]


def weight_term(grad, xu_ref, skip_rows, first):
    zero = jnp.zeros((64, W), BF16)
    low = jnp.concatenate([grad[:, W:], zero], axis=1)
    high = jnp.concatenate([zero, grad[:, :-W]], axis=1)
    pieces = []
    for e in range(first, first + 3):
        for tap in range(3):
            at = e * 192 + tap * 64
            pieces += [xu_ref[at : at + 64, :], skip_rows(e, tap)]
    rows = jnp.concatenate([low, grad, high], axis=0)
    return lax.dot_general(jnp.concatenate(pieces, axis=0), rows, NT, preferred_element_type=F32)


def input_grad(held, gs_ref, wi_ref, plane):
    ours = [j for j in range(plane, plane + 3) if j in held]
    taps = slice((ours[0] - plane) * 192, (ours[-1] - plane + 1) * 192)
    rows = slice((ours[0] - held[0]) * 192, (ours[-1] - held[0] + 1) * 192)
    return row_taps_back(mm(wi_ref[:, taps], gs_ref[rows, :]), 128)


def edge_cot(edge_ref):
    return jnp.concatenate([edge_ref[:64, 256:], edge_ref[64:, 256:]], axis=1)


def position():
    me = lax.axis_index(AXIS)
    return me & 1, (me >> 1) & 3


def for_parity(core, body):
    @pl.when(core == 0)
    def _():
        body(0)

    @pl.when(core == 1)
    def _():
        body(1)


def up_weights(wup_ref):
    return jnp.concatenate(
        [jnp.concatenate([wup_ref[2 * ij], wup_ref[2 * ij + 1]], axis=1) for ij in range(4)], axis=0
    )


def upsample(coarse, weights, select, xu_ref, base, spread_ref=None):
    spread = [mm(coarse[:, 128 * t : 128 * t + 128], select).astype(BF16) for t in range(2)]
    for tap in range(3):
        columns = []
        for h in range(4):
            at = 512 * tap + 128 * (h & 1)
            piece = spread[h >> 1]
            columns.append(jnp.concatenate([piece[:, at : at + 128], piece[:, at + 256 : at + 384]], axis=0))
        operand = jnp.concatenate(columns, axis=1)
        if spread_ref is not None and tap == 1:
            spread_ref[...] = operand
        up = mm(weights, operand).astype(BF16)
        for i in range(2):
            for j in range(2):
                at = base + i * 192 + tap * 64
                for h in range(4):
                    xu_ref[at : at + 64, (2 * h + j) * W : (2 * h + j + 1) * W] = up[
                        (2 * i + j) * 64 : (2 * i + j + 1) * 64, h * W : (h + 1) * W
                    ]


def prepare_kernel(
    own_ref, wup_ref, wc_ref, xu_ref, spread_ref, wfu_ref, wfs_ref, wi_ref, wg_ref, skip_ref
):
    select = spread_columns()
    skip_ref[...] = skip_columns()
    upsample(own_ref[...], up_weights(wup_ref), select, xu_ref, 0, spread_ref)
    rows = []
    for b in range(3):
        taps = [wc_ref[9 * a + 3 * b + c] for a in range(3) for c in range(3)]
        rows.append(jnp.concatenate(taps + [jnp.zeros((64, 128), BF16)], axis=1))
    full = jnp.concatenate(rows, axis=0)
    for half, ref in enumerate((wfu_ref, wfs_ref)):
        select = one_hot((256, 128), lambda row, col: row == (col & 63) + 64 * half + 128 * (col >> 6))
        for m in range(5):
            part = mm(full[:, 256 * m : 256 * m + 256], select).astype(BF16)
            if m < 4:
                ref[:, 128 * m : 128 * m + 128] = part
            else:
                ref[:, 512:] = part[:, :64]
    for b in range(3):
        taps = [wc_ref[9 * (2 - jj) + 3 * b + c] for jj in range(3) for c in range(3)]
        wi_ref[b * 128 : (b + 1) * 128, :] = jnp.concatenate(taps, axis=0).T
    wg_ref[...] = jnp.concatenate([wup_ref[2 * ij + k] for k in range(2) for ij in range(4)], axis=0).T


def edge_kernel(
    core_ref, cross_ref, wup_ref, own_ref, far_wfu_ref, xu_ref, pre_ref, wfu_ref, sems
):
    pairs = ((far_wfu_ref, wfu_ref), (own_ref, xu_ref.at[384:768]))
    copies = [pltpu.make_async_copy(src, dst, sems.at[i]) for i, (src, dst) in enumerate(pairs)]
    for copy in copies:
        copy.start()
    weights = up_weights(wup_ref)
    select = spread_columns()
    even = position()[0] == 0
    near, other = (core_ref[:, :256], cross_ref[:, :256])
    upsample(jnp.where(even, other, near), weights, select, xu_ref, 0)
    upsample(jnp.where(even, near, other), weights, select, xu_ref, 768)
    for copy in copies:
        copy.wait()
    for j in range(4):
        z = mm(wfu_ref[...], xu_ref[j * 192 : j * 192 + 576, :])
        pre_ref[j * 64 : (j + 1) * 64, :] = row_taps(z, 64)


def inner_kernel(
    edge_ref,
    held_ref,
    held_core_ref,
    cot_ref,
    skip_ref,
    xu_ref,
    pre_up_ref,
    far_wfs_ref,
    far_spread_ref,
    far_wi_ref,
    far_wg_ref,
    xs_ref,
    pre_ref,
    part_ref,
    act_ref,
    term_ref,
    wfs_ref,
    spread_ref,
    wi_ref,
    wg_ref,
    gs_ref,
    sems,
):
    pairs = (
        (far_wfs_ref, wfs_ref),
        (far_spread_ref, spread_ref),
        (far_wi_ref, wi_ref),
        (far_wg_ref, wg_ref),
    )
    copies = [pltpu.make_async_copy(src, dst, sems.at[i]) for i, (src, dst) in enumerate(pairs)]
    for copy in copies:
        copy.start()

    def body(odd):
        base = 0 if odd else 2
        place_skip(held_ref[...], skip_ref[...], xs_ref, 384 * odd)
        place_skip(held_core_ref[...], skip_ref[...], xs_ref, 384 * (1 - odd))
        for copy in copies:
            copy.wait()
        shift = shift_columns()
        for j in range(4):
            planes = [e for e in range(j, j + 3) if base <= e < base + 4]
            taps = slice((planes[0] - j) * 192, (planes[-1] - j + 1) * 192)
            rows = slice((planes[0] - base) * 192, (planes[-1] - base + 1) * 192)
            pre = pre_up_ref[j * 64 : (j + 1) * 64, :] + row_taps(mm(wfs_ref[:, taps], xs_ref[rows, :]), 64)
            if (j >= 2) == bool(odd):
                at = (j % 2) * 64
                pre_ref[at : at + 64, :] = pre
                continue
            inner = j in (1, 2)
            cot = cot_ref[:, (j - 1) * 1024 : j * 1024] if inner else edge_cot(edge_ref)
            act, grad = gated(pre, cot)
            place_grad(grad, shift, gs_ref, (j % 2) * 192)
            if inner:
                act_ref[...] = act

                def skip_rows(e, tap):
                    at = (e - base) * 192 + tap * 64
                    return xs_ref[at : at + 64, :]

                term_ref[...] = weight_term(grad, xu_ref, skip_rows, j)

        for plane in range(2):
            part = input_grad((0, 1) if odd else (2, 3), gs_ref, wi_ref, plane)
            part_ref[plane * 128 : (plane + 1) * 128, :] = part

    for_parity(position()[0], body)


def main_kernel(
    scale,
    cross_ref,
    cot_ref,
    edge_ref,
    select_ref,
    xs_ref,
    part_ref,
    half_act_ref,
    xu_ref,
    pre_ref,
    term_ref,
    spread_ref,
    wi_ref,
    wf_ref,
    wg_ref,
    far_act_ref,
    far_gi_ref,
    far_skip_ref,
    keep_ref,
    send_ref,
    xc_ref,
    gs_ref,
    gw_ref,
    gj_ref,
    act_ref,
    gi_ref,
    skip_ref,
    sems,
):
    core, quad = position()
    skip_copy = pltpu.make_async_copy(skip_ref, far_skip_ref, sems.at[2])
    gi_copy = pltpu.make_async_copy(gi_ref, far_gi_ref, sems.at[3])

    def copies_of(odd):
        ready, late = (slice(0, 1024), slice(1024, 2048)) if odd else (slice(1024, 2048), slice(0, 1024))
        return (
            pltpu.make_async_copy(half_act_ref, far_act_ref.at[:, ready], sems.at[0]),
            pltpu.make_async_copy(act_ref, far_act_ref.at[:, late], sems.at[1]),
        )

    def first(odd):
        ready_copy, late_copy = copies_of(odd)
        ready_copy.start()
        place_skip(cross_ref[...], select_ref[...], xc_ref, 0)
        shift = shift_columns()
        for j in (2, 3) if odd else (0, 1):
            start = 4 * odd
            planes = [e for e in range(j, j + 3) if start <= e < start + 2]
            taps = slice((planes[0] - j) * 192, (planes[-1] - j + 1) * 192)
            rows = slice((planes[0] - start) * 192, (planes[-1] - start + 1) * 192)
            z = mm(wf_ref[:, taps], xc_ref[rows, :])
            at = (j % 2) * 64
            pre = pre_ref[at : at + 64, :] + row_taps(z, 64)
            inner = j in (1, 2)
            cot = cot_ref[:, (j - 1) * 1024 : j * 1024] if inner else edge_cot(edge_ref)
            act, grad = gated(pre, cot)
            place_grad(grad, shift, gs_ref, (j % 2) * 192)
            if inner:
                act_ref[...] = act
                late_copy.start()
        for plane in range(2):
            at = slice(plane * 128, (plane + 1) * 128)
            gj_ref[at, :] = part_ref[at, :] + input_grad((2, 3) if odd else (0, 1), gs_ref, wi_ref, plane)

    for_parity(core, first)

    lower = lax.broadcasted_iota(jnp.int32, (64, W), 1) < 64
    ups = []
    skips = []
    for j in range(2):
        grad = gj_ref[j * 128 : (j + 1) * 128, :]
        ups.append(grad[:64].astype(BF16))
        skips.append(grad[64:])
    for h in range(8):
        first = skips[0][:, h * W : (h + 1) * W]
        second = skips[1][:, h * W : (h + 1) * W]
        skip_ref[2 * h] = jnp.where(lower, first, pltpu.roll(second, 64, 1)).astype(BF16)
        skip_ref[2 * h + 1] = jnp.where(lower, pltpu.roll(first, 64, 1), second).astype(BF16)

    skip_copy.start()
    tiles = []
    for h in range(4):
        tiles.append(
            jnp.concatenate(
                [ups[i][:, (2 * h + j) * W : (2 * h + j + 1) * W] for i in range(2) for j in range(2)],
                axis=0,
            )
        )
    grad_up = lax.dot_general(
        jnp.concatenate(tiles, axis=1), spread_ref[...], NT, preferred_element_type=F32
    )
    grad_up = grad_up * scale
    for ij in range(4):
        for k in range(2):
            at = (27 + 2 * ij + k) * 64
            gw_ref[at : at + 64, :] = grad_up[ij * 64 : (ij + 1) * 64, k * W : (k + 1) * W]
    gw_ref[35 * 64 :, :] = jnp.zeros((64, W), F32)

    def part_lanes(row, col):
        return ((row >> 7) == ((col >> 6) & 1)) & ((row & 127) == 2 * (col & 63) + (col >> 7))

    apart = one_hot((256, 256), part_lanes)
    halves = [
        mm(jnp.concatenate([tiles[2 * t], tiles[2 * t + 1]], axis=1), apart).astype(BF16) for t in range(2)
    ]
    operand = jnp.concatenate(
        [jnp.concatenate([half[:, k * W : (k + 1) * W] for half in halves], axis=1) for k in range(2)],
        axis=0,
    )
    gi_ref[...] = mm(wg_ref[...], operand).astype(BF16)
    gi_copy.start()

    def second(odd):
        j = 2 if odd else 1

        def skip_rows(e, tap):
            start = 4 * odd
            if start <= e < start + 2:
                ref, at = (xc_ref, (e - start) * 192 + tap * 64)
            else:
                ref, at = (xs_ref, (e - (0 if odd else 2)) * 192 + tap * 64)
            return ref[at : at + 64, :]

        at = (j % 2) * 192 + 64
        grad = gs_ref[at : at + 64, :]
        total = weight_term(grad, xu_ref, skip_rows, j) + term_ref[...]
        total = (total * scale).T
        for a in range(3):
            for b in range(3):
                for tap in range(3):
                    at = (9 * a + 3 * b + tap) * 64
                    column = (3 * a + tap) * W
                    gw_ref[at : at + 64, :] = total[b * 64 : (b + 1) * 64, column : column + W]
        for done in copies_of(odd):
            done.wait()

    for_parity(core, second)

    for k in range(4):
        row = jnp.bitwise_xor(quad, k) * 288
        mine = pl.multiple_of(core * 1152 + row, 32)
        other = pl.multiple_of((1 - core) * 1152 + row, 32)
        keep_ref[k * 288 : (k + 1) * 288, :] = gw_ref[pl.ds(mine, 288), :]
        send_ref[k * 288 : (k + 1) * 288, :] = gw_ref[pl.ds(other, 288), :].astype(BF16)
    for done in (skip_copy, gi_copy):
        done.wait()


def finish_kernel(mine, value_ref, *refs):
    conv_ref, up_ref, stage_ref, sems = refs[-4:]
    core, quad = position()
    side = core if mine else 1 - core

    def each(act):
        for k in range(4):
            piece = 4 * side + jnp.bitwise_xor(quad, k)
            rows = slice(k * 9, k * 9 + 9)

            @pl.when(piece < 6)
            def _():
                dst = conv_ref.at[pl.ds(piece * 9, 9)]
                act(k, pltpu.make_async_copy(stage_ref.at[rows], dst, sems.at[k]))

            @pl.when(piece == 6)
            def _():
                act(k, pltpu.make_async_copy(stage_ref.at[rows], up_ref.at[0:9], sems.at[k]))

            @pl.when(piece == 7)
            def _():
                src = stage_ref.at[k * 9 : k * 9 + 7]
                act(k, pltpu.make_async_copy(src, up_ref.at[9:16], sems.at[k]))

    for k in range(4):
        rows = slice(k * 288, (k + 1) * 288)
        stage_ref[k * 9 : k * 9 + 9] = value_ref[rows, :].astype(F32).reshape(9, 32, 128)
    each(lambda k, copy: copy.start())
    each(lambda k, copy: copy.wait())


def room(mebibytes):
    return pltpu.CompilerParams(vmem_limit_bytes=mebibytes << 20)


VMEM = pl.BlockSpec(memory_space=pltpu.VMEM)
FAR = pl.BlockSpec(memory_space=pl.ANY)


def far(value):
    return pltpu.with_memory_space_constraint(value, pltpu.HBM)


def near(value):
    return pltpu.with_memory_space_constraint(value, pltpu.VMEM)


def like(shape, dtype=BF16):
    return jax.ShapeDtypeStruct(shape, dtype)


def inside(shape, dtype=BF16):
    return pltpu.VMEM(shape, dtype)


def outside(shape, dtype=BF16):
    return pltpu.HBM(shape, dtype)


def reduce_weights(keep, send, back, finish_others, n):
    def swap(value, bit):
        return lax.ppermute(value, AXIS, [(i, i ^ bit) for i in range(n)])

    summed = keep + swap(send, 1).astype(F32)
    rounded = summed.astype(BF16)
    total = summed[:288]
    for k in (1, 2, 3):
        total = total + swap(rounded[k * 288 : (k + 1) * 288], 2 * k).astype(F32)
    total, back = lax.optimization_barrier((total, back))
    bit = 8
    while bit < n:
        own = total.astype(BF16)
        total = own.astype(F32) + swap(own, bit).astype(F32)
        bit *= 2
    own = total.astype(BF16)
    pieces = [own] + [swap(own, 2 * k) for k in (1, 2, 3)]
    pieces, others = lax.optimization_barrier((pieces, finish_others(back)))
    mine = jnp.concatenate(pieces, axis=0)
    other = swap(mine, 1)
    sums = ()
    for first, value in ((True, mine), (False, other)):
        sums = pl.pallas_call(
            functools.partial(finish_kernel, first),
            out_shape=(outside((54, 32, 128), F32), outside((16, 32, 128), F32)),
            in_specs=[VMEM] + [FAR] * len(sums),
            out_specs=(FAR, FAR),
            scratch_shapes=[pltpu.VMEM((36, 32, 128), F32), pltpu.SemaphoreType.DMA((4,))],
            input_output_aliases={} if first else {1: 0, 2: 1},
            compiler_params=room(6),
            cost_estimate=pl.CostEstimate(flops=1200000000, bytes_accessed=1000000, transcendentals=0),
            name="finish",
        )(near(value), *sums)
    conv, up = sums
    return conv.reshape(27, 64, 128), up.reshape(8, 64, 128), others


def local(coarse_input, skip, cotangent, w_up, w_conv):
    n = lax.axis_size(AXIS)
    cells = cotangent.shape[2]
    planes = cotangent.shape[1]
    positions = skip.shape[2]
    core_pairs = [(i, i ^ 1) for i in range(n)]
    cross_pairs = [(i, i + 1 if i % 2 else i - 1) for i in range(1, n - 1)]
    me = lax.axis_index(AXIS)
    core = me & 1

    sent = skip.reshape(64, n, 2 * positions).transpose(1, 0, 2)
    held = lax.all_to_all(sent, AXIS, split_axis=0, concat_axis=0, tiled=True)
    if positions != 64:
        held = held.reshape(n, 64, 2, positions).transpose(1, 2, 0, 3).reshape(64, 2, 16, 64)
        held = held.transpose(2, 0, 1, 3).reshape(16, 64, 128)

    coarse = coarse_input.reshape(128, 256)
    flat = lax.optimization_barrier(cotangent.reshape(64, 2048))

    def edge(plane):
        halves = [lax.dynamic_slice_in_dim(flat, 1024 * plane + 512 * i, 512, 1) for i in range(2)]
        return jnp.concatenate([coarse, jnp.concatenate(halves, axis=0)], axis=1)

    edge_core = lax.ppermute(edge(1 - core), AXIS, core_pairs)
    edge_cross = lax.ppermute(edge(core), AXIS, cross_pairs)
    xu, spread, wf_up, wf_skip, wi, wg, pick_skip = pl.pallas_call(
        prepare_kernel,
        out_shape=(
            inside((384, 1024)),
            outside((256, 512)),
            outside((192, 576)),
            outside((192, 576)),
            outside((384, 576)),
            outside((128, 512)),
            inside((256, 768)),
        ),
        in_specs=[VMEM] * 3,
        out_specs=(VMEM,) * 7,
        compiler_params=room(8),
        cost_estimate=pl.CostEstimate(flops=1840000000, bytes_accessed=1000000, transcendentals=0),
        name="prepare",
    )(coarse, w_up, w_conv)
    held, wf_up = lax.optimization_barrier((held, wf_up))
    held_core = lax.ppermute(held, AXIS, core_pairs)
    held_cross = lax.ppermute(held, AXIS, cross_pairs)
    held, held_core, held_cross = [v.reshape(8, 2, 64, 128) for v in (held, held_core, held_cross)]
    xu, pre_up = pl.pallas_call(
        edge_kernel,
        out_shape=(inside((1152, 1024)), inside((256, 1024), F32)),
        in_specs=[VMEM] * 4 + [FAR],
        out_specs=(VMEM,) * 2,
        scratch_shapes=[pltpu.VMEM((192, 576), BF16), pltpu.SemaphoreType.DMA((2,))],
        compiler_params=room(16),
        cost_estimate=pl.CostEstimate(flops=3000000000, bytes_accessed=1000000, transcendentals=0),
        name="edges",
    )(near(edge_core), near(edge_cross), w_up, near(xu), far(wf_up))
    xs, pre, part, half_act, term, wf_skip, spread, wi, wg = pl.pallas_call(
        inner_kernel,
        out_shape=(
            inside((768, 1024)),
            inside((128, 1024), F32),
            inside((256, 1024), F32),
            inside((64, 1024)),
            inside((1152, 192), F32),
            inside((192, 576)),
            inside((256, 512)),
            inside((384, 576)),
            inside((128, 512)),
        ),
        in_specs=[VMEM] * 7 + [FAR] * 4,
        out_specs=(VMEM,) * 9,
        scratch_shapes=[pltpu.VMEM((384, 1024), BF16), pltpu.SemaphoreType.DMA((4,))],
        compiler_params=room(20),
        cost_estimate=pl.CostEstimate(flops=4000000000, bytes_accessed=1000000, transcendentals=0),
        name="inner",
    )(
        *(near(v) for v in (edge_core, held, held_core, flat, pick_skip, xu, pre_up)),
        *(far(v) for v in (wf_skip, spread, wi, wg)),
    )

    scale = 1.0 / math.sqrt(n * planes * cells)
    act, gi, skip_part, keep, send = pl.pallas_call(
        functools.partial(main_kernel, scale),
        out_shape=(
            outside((64, 2048)),
            outside((128, 256)),
            outside((16, 64, 128)),
            inside((1152, 128), F32),
            inside((1152, 128)),
        ),
        in_specs=[VMEM] * 14,
        out_specs=(FAR,) * 3 + (VMEM,) * 2,
        scratch_shapes=[
            pltpu.VMEM((384, 1024), BF16),
            pltpu.VMEM((384, 1024), BF16),
            pltpu.VMEM((2304, 128), F32),
            pltpu.VMEM((256, 1024), F32),
            pltpu.VMEM((64, 1024), BF16),
            pltpu.VMEM((128, 256), BF16),
            pltpu.VMEM((16, 64, 128), BF16),
            pltpu.SemaphoreType.DMA((4,)),
        ],
        compiler_params=room(24),
        cost_estimate=pl.CostEstimate(flops=8280000000, bytes_accessed=1000000, transcendentals=0),
        name="section",
    )(
        *(
            near(v)
            for v in (
                held_cross,
                flat,
                edge_cross,
                pick_skip,
                xs,
                part,
                half_act,
                xu,
                pre,
                term,
                spread,
                wi,
                wf_skip,
                wg,
            )
        ),
    )
    if positions != 64:
        skip_part = skip_part.reshape(16, 64, 2, 64).transpose(1, 2, 0, 3)
        skip_part = skip_part.reshape(64, 2, n, positions).transpose(2, 0, 1, 3)
        skip_part = skip_part.reshape(n, 64, 2 * positions)
    back = lax.all_to_all(skip_part, AXIS, split_axis=0, concat_axis=0, tiled=True)

    def others(back):
        return (
            act.reshape(64, planes, cells),
            gi.reshape(128, 1, 256),
            back.transpose(1, 0, 2).reshape(64, 2 * n, positions),
        )

    grad_w_conv, grad_w_up, rest = reduce_weights(keep, send, back, others, n)
    return (*rest, grad_w_up, grad_w_conv)


def solution(mesh):
    spec = jax.sharding.PartitionSpec
    in_specs = (
        spec("groups", "space", None),
        spec("groups", None, "space"),
        spec("groups", "space", None),
        spec(),
        spec(),
    )
    out_specs = (
        spec("groups", "space", None),
        spec("groups", "space", None),
        spec("groups", None, "space"),
        spec("groups", None, None),
        spec("groups", None, None),
    )
    return jax.shard_map(local, mesh=mesh, in_specs=in_specs, out_specs=out_specs, check_vma=False)
```

```python
import functools
import math

import jax
import jax.numpy as jnp
from jax import lax
from jax.experimental import pallas as pl
from jax.experimental.pallas import tpu as pltpu

W = 128
AXIS = "space"
BF16 = jnp.bfloat16
F32 = jnp.float32
NT = (((1,), (1,)), ((), ()))


def mm(a, b):
    return jnp.dot(a, b, preferred_element_type=F32)


def one_hot(shape, cond):
    rows = lax.broadcasted_iota(jnp.int32, shape, 0)
    cols = lax.broadcasted_iota(jnp.int32, shape, 1)
    return jnp.where(cond(rows, cols), 1.0, 0.0).astype(BF16)


def row_taps(z, channels):
    zero = jnp.zeros((channels, W), F32)
    low = jnp.concatenate([zero, z[:channels, :-W]], axis=1)
    high = jnp.concatenate([z[2 * channels :, W:], zero], axis=1)
    return z[channels : 2 * channels] + low + high


def row_taps_back(z, channels):
    zero = jnp.zeros((channels, W), F32)
    low = jnp.concatenate([z[:channels, W:], zero], axis=1)
    high = jnp.concatenate([zero, z[2 * channels :, :-W]], axis=1)
    return z[channels : 2 * channels] + low + high


def spread_columns():
    def pick(lane_in, col):
        tap, k, parity, lane = (col >> 9, (col >> 8) & 1, (col >> 7) & 1, col & 127)
        return ((lane_in >> 6) == parity) & (2 * (lane_in & 63) + k == lane + tap - 1)

    return one_hot((128, 1536), pick)


def skip_columns():
    def pick(row, col):
        out = jnp.where(col >= 384, 1, 0)
        rest = col - 384 * out
        tap, lane = (rest >> 7, rest & 127)
        return (((row >> 6) & 1) == out) & ((row >> 7) * 64 + (row & 63) == lane + tap - 1)

    return one_hot((256, 768), pick)


def place_skip(value, select, xs_ref, base):
    joined = jnp.concatenate([value[:, 0].reshape(512, 128), value[:, 1].reshape(512, 128)], axis=1)
    placed = mm(joined, select).astype(BF16)
    for parity in range(2):
        for tap in range(3):
            at = base + parity * 192 + tap * 64
            for h in range(8):
                xs_ref[at : at + 64, h * W : (h + 1) * W] = placed[
                    h * 64 : (h + 1) * 64, (3 * parity + tap) * W : (3 * parity + tap + 1) * W
                ]


def shift_columns():
    return one_hot((128, 256), lambda row, col: row == (col & 127) + 1 - 2 * (col >> 7))


def gated(pre, cot):
    gate = 1.0 / (1.0 + jnp.exp(-pre))
    grad = (cot.astype(F32) * gate * (1.0 + pre * (1.0 - gate))).astype(BF16)
    return (pre * gate).astype(BF16), grad


def place_grad(grad, shift, gs_ref, base):
    gs_ref[base + 64 : base + 128, :] = grad
    tall = jnp.concatenate([grad[:, h * W : (h + 1) * W] for h in range(8)], axis=0)
    moved = mm(tall, shift).astype(BF16)
    for side in range(2):
        at = base + side * 128
        for h in range(8):
            gs_ref[at : at + 64, h * W : (h + 1) * W] = moved[
                h * 64 : (h + 1) * 64, side * W : side * W + W
            ]


def weight_term(grad, xu_ref, skip_rows, first):
    zero = jnp.zeros((64, W), BF16)
    low = jnp.concatenate([grad[:, W:], zero], axis=1)
    high = jnp.concatenate([zero, grad[:, :-W]], axis=1)
    pieces = []
    for e in range(first, first + 3):
        for tap in range(3):
            at = e * 192 + tap * 64
            pieces += [xu_ref[at : at + 64, :], skip_rows(e, tap)]
    rows = jnp.concatenate([low, grad, high], axis=0)
    return lax.dot_general(jnp.concatenate(pieces, axis=0), rows, NT, preferred_element_type=F32)


def input_grad(held, gs_ref, wi_ref, plane):
    ours = [j for j in range(plane, plane + 3) if j in held]
    taps = slice((ours[0] - plane) * 192, (ours[-1] - plane + 1) * 192)
    rows = slice((ours[0] - held[0]) * 192, (ours[-1] - held[0] + 1) * 192)
    return row_taps_back(mm(wi_ref[:, taps], gs_ref[rows, :]), 128)


def edge_cot(edge_ref):
    return jnp.concatenate([edge_ref[:64, 256:], edge_ref[64:, 256:]], axis=1)


def position():
    me = lax.axis_index(AXIS)
    return me & 1, (me >> 1) & 3


def for_parity(core, body):
    @pl.when(core == 0)
    def _():
        body(0)

    @pl.when(core == 1)
    def _():
        body(1)


def up_weights(wup_ref):
    return jnp.concatenate(
        [jnp.concatenate([wup_ref[2 * ij], wup_ref[2 * ij + 1]], axis=1) for ij in range(4)], axis=0
    )


def upsample(coarse, weights, select, xu_ref, base, spread_ref=None):
    spread = [mm(coarse[:, 128 * t : 128 * t + 128], select).astype(BF16) for t in range(2)]
    for tap in range(3):
        columns = []
        for h in range(4):
            at = 512 * tap + 128 * (h & 1)
            piece = spread[h >> 1]
            columns.append(jnp.concatenate([piece[:, at : at + 128], piece[:, at + 256 : at + 384]], axis=0))
        operand = jnp.concatenate(columns, axis=1)
        if spread_ref is not None and tap == 1:
            spread_ref[...] = operand
        up = mm(weights, operand).astype(BF16)
        for i in range(2):
            for j in range(2):
                at = base + i * 192 + tap * 64
                for h in range(4):
                    xu_ref[at : at + 64, (2 * h + j) * W : (2 * h + j + 1) * W] = up[
                        (2 * i + j) * 64 : (2 * i + j + 1) * 64, h * W : (h + 1) * W
                    ]


def prepare_kernel(
    own_ref, wup_ref, wc_ref, xu_ref, spread_ref, wfu_ref, wfs_ref, wi_ref, wg_ref, skip_ref
):
    select = spread_columns()
    skip_ref[...] = skip_columns()
    upsample(own_ref[...], up_weights(wup_ref), select, xu_ref, 0, spread_ref)
    rows = []
    for b in range(3):
        taps = [wc_ref[9 * a + 3 * b + c] for a in range(3) for c in range(3)]
        rows.append(jnp.concatenate(taps + [jnp.zeros((64, 128), BF16)], axis=1))
    full = jnp.concatenate(rows, axis=0)
    for half, ref in enumerate((wfu_ref, wfs_ref)):
        select = one_hot((256, 128), lambda row, col: row == (col & 63) + 64 * half + 128 * (col >> 6))
        for m in range(5):
            part = mm(full[:, 256 * m : 256 * m + 256], select).astype(BF16)
            if m < 4:
                ref[:, 128 * m : 128 * m + 128] = part
            else:
                ref[:, 512:] = part[:, :64]
    for b in range(3):
        taps = [wc_ref[9 * (2 - jj) + 3 * b + c] for jj in range(3) for c in range(3)]
        wi_ref[b * 128 : (b + 1) * 128, :] = jnp.concatenate(taps, axis=0).T
    wg_ref[...] = jnp.concatenate([wup_ref[2 * ij + k] for k in range(2) for ij in range(4)], axis=0).T


def edge_kernel(
    core_ref, cross_ref, wup_ref, own_ref, far_wfu_ref, xu_ref, pre_ref, wfu_ref, sems
):
    pairs = ((far_wfu_ref, wfu_ref), (own_ref, xu_ref.at[384:768]))
    copies = [pltpu.make_async_copy(src, dst, sems.at[i]) for i, (src, dst) in enumerate(pairs)]
    for copy in copies:
        copy.start()
    weights = up_weights(wup_ref)
    select = spread_columns()
    even = position()[0] == 0
    near, other = (core_ref[:, :256], cross_ref[:, :256])
    upsample(jnp.where(even, other, near), weights, select, xu_ref, 0)
    upsample(jnp.where(even, near, other), weights, select, xu_ref, 768)
    for copy in copies:
        copy.wait()
    for j in range(4):
        z = mm(wfu_ref[...], xu_ref[j * 192 : j * 192 + 576, :])
        pre_ref[j * 64 : (j + 1) * 64, :] = row_taps(z, 64)


def inner_kernel(
    edge_ref,
    held_ref,
    held_core_ref,
    cot_ref,
    skip_ref,
    xu_ref,
    pre_up_ref,
    far_wfs_ref,
    far_spread_ref,
    far_wi_ref,
    far_wg_ref,
    xs_ref,
    pre_ref,
    part_ref,
    act_ref,
    term_ref,
    wfs_ref,
    spread_ref,
    wi_ref,
    wg_ref,
    gs_ref,
    sems,
):
    pairs = (
        (far_wfs_ref, wfs_ref),
        (far_spread_ref, spread_ref),
        (far_wi_ref, wi_ref),
        (far_wg_ref, wg_ref),
    )
    copies = [pltpu.make_async_copy(src, dst, sems.at[i]) for i, (src, dst) in enumerate(pairs)]
    for copy in copies:
        copy.start()

    def body(odd):
        base = 0 if odd else 2
        place_skip(held_ref[...], skip_ref[...], xs_ref, 384 * odd)
        place_skip(held_core_ref[...], skip_ref[...], xs_ref, 384 * (1 - odd))
        for copy in copies:
            copy.wait()
        shift = shift_columns()
        for j in range(4):
            planes = [e for e in range(j, j + 3) if base <= e < base + 4]
            taps = slice((planes[0] - j) * 192, (planes[-1] - j + 1) * 192)
            rows = slice((planes[0] - base) * 192, (planes[-1] - base + 1) * 192)
            pre = pre_up_ref[j * 64 : (j + 1) * 64, :] + row_taps(mm(wfs_ref[:, taps], xs_ref[rows, :]), 64)
            if (j >= 2) == bool(odd):
                at = (j % 2) * 64
                pre_ref[at : at + 64, :] = pre
                continue
            inner = j in (1, 2)
            cot = cot_ref[:, (j - 1) * 1024 : j * 1024] if inner else edge_cot(edge_ref)
            act, grad = gated(pre, cot)
            place_grad(grad, shift, gs_ref, (j % 2) * 192)
            if inner:
                act_ref[...] = act

                def skip_rows(e, tap):
                    at = (e - base) * 192 + tap * 64
                    return xs_ref[at : at + 64, :]

                term_ref[...] = weight_term(grad, xu_ref, skip_rows, j)

        for plane in range(2):
            part = input_grad((0, 1) if odd else (2, 3), gs_ref, wi_ref, plane)
            part_ref[plane * 128 : (plane + 1) * 128, :] = part

    for_parity(position()[0], body)


def main_kernel(
    scale,
    cross_ref,
    cot_ref,
    edge_ref,
    select_ref,
    xs_ref,
    part_ref,
    half_act_ref,
    xu_ref,
    pre_ref,
    term_ref,
    spread_ref,
    wi_ref,
    wf_ref,
    wg_ref,
    far_act_ref,
    far_gi_ref,
    far_skip_ref,
    keep_ref,
    send_ref,
    xc_ref,
    gs_ref,
    gw_ref,
    gj_ref,
    act_ref,
    gi_ref,
    skip_ref,
    sems,
):
    core, quad = position()
    skip_copy = pltpu.make_async_copy(skip_ref, far_skip_ref, sems.at[2])
    gi_copy = pltpu.make_async_copy(gi_ref, far_gi_ref, sems.at[3])

    def copies_of(odd):
        ready, late = (slice(0, 1024), slice(1024, 2048)) if odd else (slice(1024, 2048), slice(0, 1024))
        return (
            pltpu.make_async_copy(half_act_ref, far_act_ref.at[:, ready], sems.at[0]),
            pltpu.make_async_copy(act_ref, far_act_ref.at[:, late], sems.at[1]),
        )

    def first(odd):
        ready_copy, late_copy = copies_of(odd)
        ready_copy.start()
        place_skip(cross_ref[...], select_ref[...], xc_ref, 0)
        shift = shift_columns()
        for j in (2, 3) if odd else (0, 1):
            start = 4 * odd
            planes = [e for e in range(j, j + 3) if start <= e < start + 2]
            taps = slice((planes[0] - j) * 192, (planes[-1] - j + 1) * 192)
            rows = slice((planes[0] - start) * 192, (planes[-1] - start + 1) * 192)
            z = mm(wf_ref[:, taps], xc_ref[rows, :])
            at = (j % 2) * 64
            pre = pre_ref[at : at + 64, :] + row_taps(z, 64)
            inner = j in (1, 2)
            cot = cot_ref[:, (j - 1) * 1024 : j * 1024] if inner else edge_cot(edge_ref)
            act, grad = gated(pre, cot)
            place_grad(grad, shift, gs_ref, (j % 2) * 192)
            if inner:
                act_ref[...] = act
                late_copy.start()
        for plane in range(2):
            at = slice(plane * 128, (plane + 1) * 128)
            gj_ref[at, :] = part_ref[at, :] + input_grad((2, 3) if odd else (0, 1), gs_ref, wi_ref, plane)

    for_parity(core, first)

    lower = lax.broadcasted_iota(jnp.int32, (64, W), 1) < 64
    ups = []
    skips = []
    for j in range(2):
        grad = gj_ref[j * 128 : (j + 1) * 128, :]
        ups.append(grad[:64].astype(BF16))
        skips.append(grad[64:])
    for h in range(8):
        first = skips[0][:, h * W : (h + 1) * W]
        second = skips[1][:, h * W : (h + 1) * W]
        skip_ref[2 * h] = jnp.where(lower, first, pltpu.roll(second, 64, 1)).astype(BF16)
        skip_ref[2 * h + 1] = jnp.where(lower, pltpu.roll(first, 64, 1), second).astype(BF16)

    skip_copy.start()
    tiles = []
    for h in range(4):
        tiles.append(
            jnp.concatenate(
                [ups[i][:, (2 * h + j) * W : (2 * h + j + 1) * W] for i in range(2) for j in range(2)],
                axis=0,
            )
        )
    grad_up = lax.dot_general(
        jnp.concatenate(tiles, axis=1), spread_ref[...], NT, preferred_element_type=F32
    )
    grad_up = grad_up * scale
    for ij in range(4):
        for k in range(2):
            at = (27 + 2 * ij + k) * 64
            gw_ref[at : at + 64, :] = grad_up[ij * 64 : (ij + 1) * 64, k * W : (k + 1) * W]
    gw_ref[35 * 64 :, :] = jnp.zeros((64, W), F32)

    def part_lanes(row, col):
        return ((row >> 7) == ((col >> 6) & 1)) & ((row & 127) == 2 * (col & 63) + (col >> 7))

    apart = one_hot((256, 256), part_lanes)
    halves = [
        mm(jnp.concatenate([tiles[2 * t], tiles[2 * t + 1]], axis=1), apart).astype(BF16) for t in range(2)
    ]
    operand = jnp.concatenate(
        [jnp.concatenate([half[:, k * W : (k + 1) * W] for half in halves], axis=1) for k in range(2)],
        axis=0,
    )
    gi_ref[...] = mm(wg_ref[...], operand).astype(BF16)
    gi_copy.start()

    def second(odd):
        j = 2 if odd else 1

        def skip_rows(e, tap):
            start = 4 * odd
            if start <= e < start + 2:
                ref, at = (xc_ref, (e - start) * 192 + tap * 64)
            else:
                ref, at = (xs_ref, (e - (0 if odd else 2)) * 192 + tap * 64)
            return ref[at : at + 64, :]

        at = (j % 2) * 192 + 64
        grad = gs_ref[at : at + 64, :]
        total = weight_term(grad, xu_ref, skip_rows, j) + term_ref[...]
        total = (total * scale).T
        for a in range(3):
            for b in range(3):
                for tap in range(3):
                    at = (9 * a + 3 * b + tap) * 64
                    column = (3 * a + tap) * W
                    gw_ref[at : at + 64, :] = total[b * 64 : (b + 1) * 64, column : column + W]
        for done in copies_of(odd):
            done.wait()

    for_parity(core, second)

    for k in range(4):
        row = jnp.bitwise_xor(quad, k) * 288
        mine = pl.multiple_of(core * 1152 + row, 32)
        other = pl.multiple_of((1 - core) * 1152 + row, 32)
        keep_ref[k * 288 : (k + 1) * 288, :] = gw_ref[pl.ds(mine, 288), :]
        send_ref[k * 288 : (k + 1) * 288, :] = gw_ref[pl.ds(other, 288), :].astype(BF16)
    for done in (skip_copy, gi_copy):
        done.wait()


def finish_kernel(mine, value_ref, *refs):
    conv_ref, up_ref, stage_ref, sems = refs[-4:]
    core, quad = position()
    side = core if mine else 1 - core

    def each(act):
        for k in range(4):
            piece = 4 * side + jnp.bitwise_xor(quad, k)
            rows = slice(k * 9, k * 9 + 9)

            @pl.when(piece < 6)
            def _():
                dst = conv_ref.at[pl.ds(piece * 9, 9)]
                act(k, pltpu.make_async_copy(stage_ref.at[rows], dst, sems.at[k]))

            @pl.when(piece == 6)
            def _():
                act(k, pltpu.make_async_copy(stage_ref.at[rows], up_ref.at[0:9], sems.at[k]))

            @pl.when(piece == 7)
            def _():
                src = stage_ref.at[k * 9 : k * 9 + 7]
                act(k, pltpu.make_async_copy(src, up_ref.at[9:16], sems.at[k]))

    for k in range(4):
        rows = slice(k * 288, (k + 1) * 288)
        stage_ref[k * 9 : k * 9 + 9] = value_ref[rows, :].astype(F32).reshape(9, 32, 128)
    each(lambda k, copy: copy.start())
    each(lambda k, copy: copy.wait())


def room(mebibytes):
    return pltpu.CompilerParams(vmem_limit_bytes=mebibytes << 20)


VMEM = pl.BlockSpec(memory_space=pltpu.VMEM)
FAR = pl.BlockSpec(memory_space=pl.ANY)


def far(value):
    return pltpu.with_memory_space_constraint(value, pltpu.HBM)


def near(value):
    return pltpu.with_memory_space_constraint(value, pltpu.VMEM)


def like(shape, dtype=BF16):
    return jax.ShapeDtypeStruct(shape, dtype)


def inside(shape, dtype=BF16):
    return pltpu.VMEM(shape, dtype)


def outside(shape, dtype=BF16):
    return pltpu.HBM(shape, dtype)


def reduce_weights(keep, send, back, finish_others, n):
    def swap(value, bit):
        return lax.ppermute(value, AXIS, [(i, i ^ bit) for i in range(n)])

    summed = keep + swap(send, 1).astype(F32)
    rounded = summed.astype(BF16)
    total = summed[:288]
    for k in (1, 3, 2):
        total = total + swap(rounded[k * 288 : (k + 1) * 288], 2 * k).astype(F32)
    total, back = lax.optimization_barrier((total, back))
    bit = 8
    while bit < n:
        own = total.astype(BF16)
        total = own.astype(F32) + swap(own, bit).astype(F32)
        bit *= 2
    own = total.astype(BF16)
    gathered = {k: swap(own, 2 * k) for k in (1, 3, 2)}
    arrived = [gathered[k] for k in (1, 2, 3)]
    arrived, own, others = lax.optimization_barrier((arrived, own, finish_others(back)))
    gathered = dict(zip((1, 2, 3), arrived))
    mine = jnp.concatenate([own] + [gathered[k] for k in (1, 2, 3)], axis=0)
    other = swap(mine, 1)
    sums = ()
    for first, value in ((True, mine), (False, other)):
        sums = pl.pallas_call(
            functools.partial(finish_kernel, first),
            out_shape=(outside((54, 32, 128), F32), outside((16, 32, 128), F32)),
            in_specs=[VMEM] + [FAR] * len(sums),
            out_specs=(FAR, FAR),
            scratch_shapes=[pltpu.VMEM((36, 32, 128), F32), pltpu.SemaphoreType.DMA((4,))],
            input_output_aliases={} if first else {1: 0, 2: 1},
            compiler_params=room(6),
            cost_estimate=pl.CostEstimate(flops=1200000000, bytes_accessed=1000000, transcendentals=0),
            name="finish",
        )(near(value), *sums)
    conv, up = sums
    return conv.reshape(27, 64, 128), up.reshape(8, 64, 128), others


def local(coarse_input, skip, cotangent, w_up, w_conv):
    n = lax.axis_size(AXIS)
    cells = cotangent.shape[2]
    planes = cotangent.shape[1]
    positions = skip.shape[2]
    core_pairs = [(i, i ^ 1) for i in range(n)]
    cross_pairs = [(i, i + 1 if i % 2 else i - 1) for i in range(1, n - 1)]
    me = lax.axis_index(AXIS)
    core = me & 1

    sent = skip.reshape(64, n, 2 * positions).transpose(1, 0, 2)
    held = lax.all_to_all(sent, AXIS, split_axis=0, concat_axis=0, tiled=True)
    if positions != 64:
        held = held.reshape(n, 64, 2, positions).transpose(1, 2, 0, 3).reshape(64, 2, 16, 64)
        held = held.transpose(2, 0, 1, 3).reshape(16, 64, 128)

    coarse = coarse_input.reshape(128, 256)
    flat = lax.optimization_barrier(cotangent.reshape(64, 2048))

    def edge(plane):
        halves = [lax.dynamic_slice_in_dim(flat, 1024 * plane + 512 * i, 512, 1) for i in range(2)]
        return jnp.concatenate([coarse, jnp.concatenate(halves, axis=0)], axis=1)

    edge_core = lax.ppermute(edge(1 - core), AXIS, core_pairs)
    edge_cross = lax.ppermute(edge(core), AXIS, cross_pairs)
    xu, spread, wf_up, wf_skip, wi, wg, pick_skip = pl.pallas_call(
        prepare_kernel,
        out_shape=(
            inside((384, 1024)),
            outside((256, 512)),
            outside((192, 576)),
            outside((192, 576)),
            outside((384, 576)),
            outside((128, 512)),
            inside((256, 768)),
        ),
        in_specs=[VMEM] * 3,
        out_specs=(VMEM,) * 7,
        compiler_params=room(8),
        cost_estimate=pl.CostEstimate(flops=1840000000, bytes_accessed=1000000, transcendentals=0),
        name="prepare",
    )(coarse, w_up, w_conv)
    held, wf_up = lax.optimization_barrier((held, wf_up))
    held_cross = lax.ppermute(held, AXIS, cross_pairs)
    later, edge_core, edge_cross = lax.optimization_barrier((held, edge_core, edge_cross))
    held_core = lax.ppermute(later, AXIS, core_pairs)
    held, held_core, held_cross = [v.reshape(8, 2, 64, 128) for v in (held, held_core, held_cross)]
    xu, pre_up = pl.pallas_call(
        edge_kernel,
        out_shape=(inside((1152, 1024)), inside((256, 1024), F32)),
        in_specs=[VMEM] * 4 + [FAR],
        out_specs=(VMEM,) * 2,
        scratch_shapes=[pltpu.VMEM((192, 576), BF16), pltpu.SemaphoreType.DMA((2,))],
        compiler_params=room(16),
        cost_estimate=pl.CostEstimate(flops=3000000000, bytes_accessed=1000000, transcendentals=0),
        name="edges",
    )(near(edge_core), near(edge_cross), w_up, near(xu), far(wf_up))
    xs, pre, part, half_act, term, wf_skip, spread, wi, wg = pl.pallas_call(
        inner_kernel,
        out_shape=(
            inside((768, 1024)),
            inside((128, 1024), F32),
            inside((256, 1024), F32),
            inside((64, 1024)),
            inside((1152, 192), F32),
            inside((192, 576)),
            inside((256, 512)),
            inside((384, 576)),
            inside((128, 512)),
        ),
        in_specs=[VMEM] * 7 + [FAR] * 4,
        out_specs=(VMEM,) * 9,
        scratch_shapes=[pltpu.VMEM((384, 1024), BF16), pltpu.SemaphoreType.DMA((4,))],
        compiler_params=room(20),
        cost_estimate=pl.CostEstimate(flops=4000000000, bytes_accessed=1000000, transcendentals=0),
        name="inner",
    )(
        *(near(v) for v in (edge_core, held, held_core, flat, pick_skip, xu, pre_up)),
        *(far(v) for v in (wf_skip, spread, wi, wg)),
    )

    scale = 1.0 / math.sqrt(n * planes * cells)
    act, gi, skip_part, keep, send = pl.pallas_call(
        functools.partial(main_kernel, scale),
        out_shape=(
            outside((64, 2048)),
            outside((128, 256)),
            outside((16, 64, 128)),
            inside((1152, 128), F32),
            inside((1152, 128)),
        ),
        in_specs=[VMEM] * 14,
        out_specs=(FAR,) * 3 + (VMEM,) * 2,
        scratch_shapes=[
            pltpu.VMEM((384, 1024), BF16),
            pltpu.VMEM((384, 1024), BF16),
            pltpu.VMEM((2304, 128), F32),
            pltpu.VMEM((256, 1024), F32),
            pltpu.VMEM((64, 1024), BF16),
            pltpu.VMEM((128, 256), BF16),
            pltpu.VMEM((16, 64, 128), BF16),
            pltpu.SemaphoreType.DMA((4,)),
        ],
        compiler_params=room(24),
        cost_estimate=pl.CostEstimate(flops=8280000000, bytes_accessed=1000000, transcendentals=0),
        name="section",
    )(
        *(
            near(v)
            for v in (
                held_cross,
                flat,
                edge_cross,
                pick_skip,
                xs,
                part,
                half_act,
                xu,
                pre,
                term,
                spread,
                wi,
                wf_skip,
                wg,
            )
        ),
    )
    if positions != 64:
        skip_part = skip_part.reshape(16, 64, 2, 64).transpose(1, 2, 0, 3)
        skip_part = skip_part.reshape(64, 2, n, positions).transpose(2, 0, 1, 3)
        skip_part = skip_part.reshape(n, 64, 2 * positions)
    back = lax.all_to_all(skip_part, AXIS, split_axis=0, concat_axis=0, tiled=True)

    def others(back):
        return (
            act.reshape(64, planes, cells),
            gi.reshape(128, 1, 256),
            back.transpose(1, 0, 2).reshape(64, 2 * n, positions),
        )

    grad_w_conv, grad_w_up, rest = reduce_weights(keep, send, back, others, n)
    return (*rest, grad_w_up, grad_w_conv)


def solution(mesh):
    spec = jax.sharding.PartitionSpec
    in_specs = (
        spec("groups", "space", None),
        spec("groups", None, "space"),
        spec("groups", "space", None),
        spec(),
        spec(),
    )
    out_specs = (
        spec("groups", "space", None),
        spec("groups", "space", None),
        spec("groups", None, "space"),
        spec("groups", None, None),
        spec("groups", None, None),
    )
    return jax.shard_map(local, mesh=mesh, in_specs=in_specs, out_specs=out_specs, check_vma=False)
```

```python
import functools
import math

import jax
import jax.numpy as jnp
from jax import lax
from jax.experimental import pallas as pl
from jax.experimental.pallas import tpu as pltpu

W = 128
AXIS = "space"
BF16 = jnp.bfloat16
F32 = jnp.float32
NT = (((1,), (1,)), ((), ()))


def mm(a, b):
    return jnp.dot(a, b, preferred_element_type=F32)


def one_hot(shape, cond):
    rows = lax.broadcasted_iota(jnp.int32, shape, 0)
    cols = lax.broadcasted_iota(jnp.int32, shape, 1)
    return jnp.where(cond(rows, cols), 1.0, 0.0).astype(BF16)


def row_taps(z, channels):
    zero = jnp.zeros((channels, W), F32)
    low = jnp.concatenate([zero, z[:channels, :-W]], axis=1)
    high = jnp.concatenate([z[2 * channels :, W:], zero], axis=1)
    return z[channels : 2 * channels] + low + high


def row_taps_back(z, channels):
    zero = jnp.zeros((channels, W), F32)
    low = jnp.concatenate([z[:channels, W:], zero], axis=1)
    high = jnp.concatenate([zero, z[2 * channels :, :-W]], axis=1)
    return z[channels : 2 * channels] + low + high


def spread_columns():
    def pick(lane_in, col):
        tap, k, parity, lane = (col >> 9, (col >> 8) & 1, (col >> 7) & 1, col & 127)
        return ((lane_in >> 6) == parity) & (2 * (lane_in & 63) + k == lane + tap - 1)

    return one_hot((128, 1536), pick)


def skip_columns():
    def pick(row, col):
        out = jnp.where(col >= 384, 1, 0)
        rest = col - 384 * out
        tap, lane = (rest >> 7, rest & 127)
        return (((row >> 6) & 1) == out) & ((row >> 7) * 64 + (row & 63) == lane + tap - 1)

    return one_hot((256, 768), pick)


def place_skip(value, select, xs_ref, base):
    joined = jnp.concatenate([value[:, 0].reshape(512, 128), value[:, 1].reshape(512, 128)], axis=1)
    placed = mm(joined, select).astype(BF16)
    for parity in range(2):
        for tap in range(3):
            at = base + parity * 192 + tap * 64
            for h in range(8):
                xs_ref[at : at + 64, h * W : (h + 1) * W] = placed[
                    h * 64 : (h + 1) * 64, (3 * parity + tap) * W : (3 * parity + tap + 1) * W
                ]


def shift_columns():
    return one_hot((128, 256), lambda row, col: row == (col & 127) + 1 - 2 * (col >> 7))


def gated(pre, cot):
    gate = 1.0 / (1.0 + jnp.exp(-pre))
    grad = (cot.astype(F32) * gate * (1.0 + pre * (1.0 - gate))).astype(BF16)
    return (pre * gate).astype(BF16), grad


def place_grad(grad, shift, gs_ref, base):
    gs_ref[base + 64 : base + 128, :] = grad
    tall = jnp.concatenate([grad[:, h * W : (h + 1) * W] for h in range(8)], axis=0)
    moved = mm(tall, shift).astype(BF16)
    for side in range(2):
        at = base + side * 128
        for h in range(8):
            gs_ref[at : at + 64, h * W : (h + 1) * W] = moved[
                h * 64 : (h + 1) * 64, side * W : side * W + W
            ]


def weight_term(grad, xu_ref, skip_rows, first):
    zero = jnp.zeros((64, W), BF16)
    low = jnp.concatenate([grad[:, W:], zero], axis=1)
    high = jnp.concatenate([zero, grad[:, :-W]], axis=1)
    pieces = []
    for e in range(first, first + 3):
        for tap in range(3):
            at = e * 192 + tap * 64
            pieces += [xu_ref[at : at + 64, :], skip_rows(e, tap)]
    rows = jnp.concatenate([low, grad, high], axis=0)
    return lax.dot_general(jnp.concatenate(pieces, axis=0), rows, NT, preferred_element_type=F32)


def input_grad(held, gs_ref, wi_ref, plane):
    ours = [j for j in range(plane, plane + 3) if j in held]
    taps = slice((ours[0] - plane) * 192, (ours[-1] - plane + 1) * 192)
    rows = slice((ours[0] - held[0]) * 192, (ours[-1] - held[0] + 1) * 192)
    return row_taps_back(mm(wi_ref[:, taps], gs_ref[rows, :]), 128)


def edge_cot(edge_ref):
    return jnp.concatenate([edge_ref[:64, 256:], edge_ref[64:, 256:]], axis=1)


def position():
    me = lax.axis_index(AXIS)
    return me & 1, (me >> 1) & 3


def for_parity(core, body):
    @pl.when(core == 0)
    def _():
        body(0)

    @pl.when(core == 1)
    def _():
        body(1)


def up_weights(wup_ref):
    return jnp.concatenate(
        [jnp.concatenate([wup_ref[2 * ij], wup_ref[2 * ij + 1]], axis=1) for ij in range(4)], axis=0
    )


def upsample(coarse, weights, select, xu_ref, base, spread_ref=None):
    spread = [mm(coarse[:, 128 * t : 128 * t + 128], select).astype(BF16) for t in range(2)]
    for tap in range(3):
        columns = []
        for h in range(4):
            at = 512 * tap + 128 * (h & 1)
            piece = spread[h >> 1]
            columns.append(jnp.concatenate([piece[:, at : at + 128], piece[:, at + 256 : at + 384]], axis=0))
        operand = jnp.concatenate(columns, axis=1)
        if spread_ref is not None and tap == 1:
            spread_ref[...] = operand
        up = mm(weights, operand).astype(BF16)
        for i in range(2):
            for j in range(2):
                at = base + i * 192 + tap * 64
                for h in range(4):
                    xu_ref[at : at + 64, (2 * h + j) * W : (2 * h + j + 1) * W] = up[
                        (2 * i + j) * 64 : (2 * i + j + 1) * 64, h * W : (h + 1) * W
                    ]


def prepare_kernel(
    own_ref, wup_ref, wc_ref, xu_ref, spread_ref, wfu_ref, wfs_ref, wi_ref, wg_ref, skip_ref
):
    select = spread_columns()
    skip_ref[...] = skip_columns()
    upsample(own_ref[...], up_weights(wup_ref), select, xu_ref, 0, spread_ref)
    rows = []
    for b in range(3):
        taps = [wc_ref[9 * a + 3 * b + c] for a in range(3) for c in range(3)]
        rows.append(jnp.concatenate(taps + [jnp.zeros((64, 128), BF16)], axis=1))
    full = jnp.concatenate(rows, axis=0)
    for half, ref in enumerate((wfu_ref, wfs_ref)):
        select = one_hot((256, 128), lambda row, col: row == (col & 63) + 64 * half + 128 * (col >> 6))
        for m in range(5):
            part = mm(full[:, 256 * m : 256 * m + 256], select).astype(BF16)
            if m < 4:
                ref[:, 128 * m : 128 * m + 128] = part
            else:
                ref[:, 512:] = part[:, :64]
    for b in range(3):
        taps = [wc_ref[9 * (2 - jj) + 3 * b + c] for jj in range(3) for c in range(3)]
        wi_ref[b * 128 : (b + 1) * 128, :] = jnp.concatenate(taps, axis=0).T
    wg_ref[...] = jnp.concatenate([wup_ref[2 * ij + k] for k in range(2) for ij in range(4)], axis=0).T


def edge_kernel(
    core_ref, cross_ref, wup_ref, own_ref, far_wfu_ref, xu_ref, pre_ref, wfu_ref, sems
):
    pairs = ((far_wfu_ref, wfu_ref), (own_ref, xu_ref.at[384:768]))
    copies = [pltpu.make_async_copy(src, dst, sems.at[i]) for i, (src, dst) in enumerate(pairs)]
    for copy in copies:
        copy.start()
    weights = up_weights(wup_ref)
    select = spread_columns()
    even = position()[0] == 0
    near, other = (core_ref[:, :256], cross_ref[:, :256])
    upsample(jnp.where(even, other, near), weights, select, xu_ref, 0)
    upsample(jnp.where(even, near, other), weights, select, xu_ref, 768)
    for copy in copies:
        copy.wait()
    for j in range(4):
        z = mm(wfu_ref[...], xu_ref[j * 192 : j * 192 + 576, :])
        pre_ref[j * 64 : (j + 1) * 64, :] = row_taps(z, 64)


def inner_kernel(
    edge_ref,
    held_ref,
    held_core_ref,
    cot_ref,
    skip_ref,
    xu_ref,
    pre_up_ref,
    far_wfs_ref,
    far_spread_ref,
    far_wi_ref,
    far_wg_ref,
    xs_ref,
    pre_ref,
    part_ref,
    act_ref,
    term_ref,
    wfs_ref,
    spread_ref,
    wi_ref,
    wg_ref,
    gs_ref,
    sems,
):
    pairs = (
        (far_wfs_ref, wfs_ref),
        (far_spread_ref, spread_ref),
        (far_wi_ref, wi_ref),
        (far_wg_ref, wg_ref),
    )
    copies = [pltpu.make_async_copy(src, dst, sems.at[i]) for i, (src, dst) in enumerate(pairs)]
    for copy in copies:
        copy.start()

    def body(odd):
        base = 0 if odd else 2
        place_skip(held_ref[...], skip_ref[...], xs_ref, 384 * odd)
        place_skip(held_core_ref[...], skip_ref[...], xs_ref, 384 * (1 - odd))
        copies[0].wait()
        shift = shift_columns()
        for j in range(4):
            planes = [e for e in range(j, j + 3) if base <= e < base + 4]
            taps = slice((planes[0] - j) * 192, (planes[-1] - j + 1) * 192)
            rows = slice((planes[0] - base) * 192, (planes[-1] - base + 1) * 192)
            pre = pre_up_ref[j * 64 : (j + 1) * 64, :] + row_taps(mm(wfs_ref[:, taps], xs_ref[rows, :]), 64)
            if (j >= 2) == bool(odd):
                at = (j % 2) * 64
                pre_ref[at : at + 64, :] = pre
                continue
            inner = j in (1, 2)
            cot = cot_ref[:, (j - 1) * 1024 : j * 1024] if inner else edge_cot(edge_ref)
            act, grad = gated(pre, cot)
            place_grad(grad, shift, gs_ref, (j % 2) * 192)
            if inner:
                act_ref[...] = act

                def skip_rows(e, tap):
                    at = (e - base) * 192 + tap * 64
                    return xs_ref[at : at + 64, :]

                term_ref[...] = weight_term(grad, xu_ref, skip_rows, j)

        for copy in copies[1:]:
            copy.wait()
        for plane in range(2):
            part = input_grad((0, 1) if odd else (2, 3), gs_ref, wi_ref, plane)
            part_ref[plane * 128 : (plane + 1) * 128, :] = part

    for_parity(position()[0], body)


def main_kernel(
    scale,
    cross_ref,
    cot_ref,
    edge_ref,
    select_ref,
    xs_ref,
    part_ref,
    half_act_ref,
    xu_ref,
    pre_ref,
    term_ref,
    spread_ref,
    wi_ref,
    wf_ref,
    wg_ref,
    far_act_ref,
    far_gi_ref,
    far_skip_ref,
    keep_ref,
    send_ref,
    xc_ref,
    gs_ref,
    gw_ref,
    gj_ref,
    act_ref,
    gi_ref,
    skip_ref,
    sems,
):
    core, quad = position()
    skip_copy = pltpu.make_async_copy(skip_ref, far_skip_ref, sems.at[2])
    gi_copy = pltpu.make_async_copy(gi_ref, far_gi_ref, sems.at[3])

    def copies_of(odd):
        ready, late = (slice(0, 1024), slice(1024, 2048)) if odd else (slice(1024, 2048), slice(0, 1024))
        return (
            pltpu.make_async_copy(half_act_ref, far_act_ref.at[:, ready], sems.at[0]),
            pltpu.make_async_copy(act_ref, far_act_ref.at[:, late], sems.at[1]),
        )

    def first(odd):
        ready_copy, late_copy = copies_of(odd)
        ready_copy.start()
        place_skip(cross_ref[...], select_ref[...], xc_ref, 0)
        shift = shift_columns()
        for j in (2, 3) if odd else (0, 1):
            start = 4 * odd
            planes = [e for e in range(j, j + 3) if start <= e < start + 2]
            taps = slice((planes[0] - j) * 192, (planes[-1] - j + 1) * 192)
            rows = slice((planes[0] - start) * 192, (planes[-1] - start + 1) * 192)
            z = mm(wf_ref[:, taps], xc_ref[rows, :])
            at = (j % 2) * 64
            pre = pre_ref[at : at + 64, :] + row_taps(z, 64)
            inner = j in (1, 2)
            cot = cot_ref[:, (j - 1) * 1024 : j * 1024] if inner else edge_cot(edge_ref)
            act, grad = gated(pre, cot)
            place_grad(grad, shift, gs_ref, (j % 2) * 192)
            if inner:
                act_ref[...] = act
                late_copy.start()
        for plane in range(2):
            at = slice(plane * 128, (plane + 1) * 128)
            gj_ref[at, :] = part_ref[at, :] + input_grad((2, 3) if odd else (0, 1), gs_ref, wi_ref, plane)

    for_parity(core, first)

    lower = lax.broadcasted_iota(jnp.int32, (64, W), 1) < 64
    ups = []
    skips = []
    for j in range(2):
        grad = gj_ref[j * 128 : (j + 1) * 128, :]
        ups.append(grad[:64].astype(BF16))
        skips.append(grad[64:])
    for h in range(8):
        first = skips[0][:, h * W : (h + 1) * W]
        second = skips[1][:, h * W : (h + 1) * W]
        skip_ref[2 * h] = jnp.where(lower, first, pltpu.roll(second, 64, 1)).astype(BF16)
        skip_ref[2 * h + 1] = jnp.where(lower, pltpu.roll(first, 64, 1), second).astype(BF16)

    skip_copy.start()
    tiles = []
    for h in range(4):
        tiles.append(
            jnp.concatenate(
                [ups[i][:, (2 * h + j) * W : (2 * h + j + 1) * W] for i in range(2) for j in range(2)],
                axis=0,
            )
        )
    grad_up = lax.dot_general(
        jnp.concatenate(tiles, axis=1), spread_ref[...], NT, preferred_element_type=F32
    )
    grad_up = grad_up * scale
    for ij in range(4):
        for k in range(2):
            at = (27 + 2 * ij + k) * 64
            gw_ref[at : at + 64, :] = grad_up[ij * 64 : (ij + 1) * 64, k * W : (k + 1) * W]
    gw_ref[35 * 64 :, :] = jnp.zeros((64, W), F32)

    def part_lanes(row, col):
        return ((row >> 7) == ((col >> 6) & 1)) & ((row & 127) == 2 * (col & 63) + (col >> 7))

    apart = one_hot((256, 256), part_lanes)
    halves = [
        mm(jnp.concatenate([tiles[2 * t], tiles[2 * t + 1]], axis=1), apart).astype(BF16) for t in range(2)
    ]
    operand = jnp.concatenate(
        [jnp.concatenate([half[:, k * W : (k + 1) * W] for half in halves], axis=1) for k in range(2)],
        axis=0,
    )
    gi_ref[...] = mm(wg_ref[...], operand).astype(BF16)
    gi_copy.start()

    def second(odd):
        j = 2 if odd else 1

        def skip_rows(e, tap):
            start = 4 * odd
            if start <= e < start + 2:
                ref, at = (xc_ref, (e - start) * 192 + tap * 64)
            else:
                ref, at = (xs_ref, (e - (0 if odd else 2)) * 192 + tap * 64)
            return ref[at : at + 64, :]

        at = (j % 2) * 192 + 64
        grad = gs_ref[at : at + 64, :]
        total = weight_term(grad, xu_ref, skip_rows, j) + term_ref[...]
        total = (total * scale).T
        for a in range(3):
            for b in range(3):
                for tap in range(3):
                    at = (9 * a + 3 * b + tap) * 64
                    column = (3 * a + tap) * W
                    gw_ref[at : at + 64, :] = total[b * 64 : (b + 1) * 64, column : column + W]
        for done in copies_of(odd):
            done.wait()

    for_parity(core, second)

    for k in range(4):
        row = jnp.bitwise_xor(quad, k) * 288
        mine = pl.multiple_of(core * 1152 + row, 32)
        other = pl.multiple_of((1 - core) * 1152 + row, 32)
        keep_ref[k * 288 : (k + 1) * 288, :] = gw_ref[pl.ds(mine, 288), :]
        send_ref[k * 288 : (k + 1) * 288, :] = gw_ref[pl.ds(other, 288), :].astype(BF16)
    for done in (skip_copy, gi_copy):
        done.wait()


def finish_kernel(mine, value_ref, *refs):
    conv_ref, up_ref, stage_ref, sems = refs[-4:]
    core, quad = position()
    side = core if mine else 1 - core

    def each(act):
        for k in range(4):
            piece = 4 * side + jnp.bitwise_xor(quad, k)
            rows = slice(k * 9, k * 9 + 9)

            @pl.when(piece < 6)
            def _():
                dst = conv_ref.at[pl.ds(piece * 9, 9)]
                act(k, pltpu.make_async_copy(stage_ref.at[rows], dst, sems.at[k]))

            @pl.when(piece == 6)
            def _():
                act(k, pltpu.make_async_copy(stage_ref.at[rows], up_ref.at[0:9], sems.at[k]))

            @pl.when(piece == 7)
            def _():
                src = stage_ref.at[k * 9 : k * 9 + 7]
                act(k, pltpu.make_async_copy(src, up_ref.at[9:16], sems.at[k]))

    for k in range(4):
        rows = slice(k * 288, (k + 1) * 288)
        stage_ref[k * 9 : k * 9 + 9] = value_ref[rows, :].astype(F32).reshape(9, 32, 128)
    each(lambda k, copy: copy.start())
    each(lambda k, copy: copy.wait())


def room(mebibytes):
    return pltpu.CompilerParams(vmem_limit_bytes=mebibytes << 20)


VMEM = pl.BlockSpec(memory_space=pltpu.VMEM)
FAR = pl.BlockSpec(memory_space=pl.ANY)


def far(value):
    return pltpu.with_memory_space_constraint(value, pltpu.HBM)


def near(value):
    return pltpu.with_memory_space_constraint(value, pltpu.VMEM)


def like(shape, dtype=BF16):
    return jax.ShapeDtypeStruct(shape, dtype)


def inside(shape, dtype=BF16):
    return pltpu.VMEM(shape, dtype)


def outside(shape, dtype=BF16):
    return pltpu.HBM(shape, dtype)


def reduce_weights(keep, send, back, finish_others, n):
    def swap(value, bit):
        return lax.ppermute(value, AXIS, [(i, i ^ bit) for i in range(n)])

    summed = keep + swap(send, 1).astype(F32)
    rounded = summed.astype(BF16)
    total = summed[:288]
    for k in (3, 2, 1):
        total = total + swap(rounded[k * 288 : (k + 1) * 288], 2 * k).astype(F32)
    total, back = lax.optimization_barrier((total, back))
    bit = 8
    while bit < n:
        own = total.astype(BF16)
        total = own.astype(F32) + swap(own, bit).astype(F32)
        bit *= 2
    own = total.astype(BF16)
    gathered = {k: swap(own, 2 * k) for k in (1, 3, 2)}
    arrived = [gathered[k] for k in (1, 3, 2)]
    arrived, own, others = lax.optimization_barrier((arrived, own, finish_others(back)))
    gathered = dict(zip((1, 3, 2), arrived))
    mine = jnp.concatenate([own] + [gathered[k] for k in (1, 2, 3)], axis=0)
    other = swap(mine, 1)
    sums = ()
    for first, value in ((True, mine), (False, other)):
        sums = pl.pallas_call(
            functools.partial(finish_kernel, first),
            out_shape=(outside((54, 32, 128), F32), outside((16, 32, 128), F32)),
            in_specs=[VMEM] + [FAR] * len(sums),
            out_specs=(FAR, FAR),
            scratch_shapes=[pltpu.VMEM((36, 32, 128), F32), pltpu.SemaphoreType.DMA((4,))],
            input_output_aliases={} if first else {1: 0, 2: 1},
            compiler_params=room(6),
            cost_estimate=pl.CostEstimate(flops=1200000000, bytes_accessed=1000000, transcendentals=0),
            name="finish",
        )(near(value), *sums)
    conv, up = sums
    return conv.reshape(27, 64, 128), up.reshape(8, 64, 128), others


def local(coarse_input, skip, cotangent, w_up, w_conv):
    n = lax.axis_size(AXIS)
    cells = cotangent.shape[2]
    planes = cotangent.shape[1]
    positions = skip.shape[2]
    core_pairs = [(i, i ^ 1) for i in range(n)]
    cross_pairs = [(i, i + 1 if i % 2 else i - 1) for i in range(1, n - 1)]
    me = lax.axis_index(AXIS)
    core = me & 1

    sent = skip.reshape(64, n, 2 * positions).transpose(1, 0, 2)
    held = lax.all_to_all(sent, AXIS, split_axis=0, concat_axis=0, tiled=True)
    if positions != 64:
        held = held.reshape(n, 64, 2, positions).transpose(1, 2, 0, 3).reshape(64, 2, 16, 64)
        held = held.transpose(2, 0, 1, 3).reshape(16, 64, 128)

    coarse = coarse_input.reshape(128, 256)
    flat = lax.optimization_barrier(cotangent.reshape(64, 2048))

    def edge(plane):
        halves = [lax.dynamic_slice_in_dim(flat, 1024 * plane + 512 * i, 512, 1) for i in range(2)]
        return jnp.concatenate([coarse, jnp.concatenate(halves, axis=0)], axis=1)

    edge_core = lax.ppermute(edge(1 - core), AXIS, core_pairs)
    edge_cross = lax.ppermute(edge(core), AXIS, cross_pairs)
    xu, spread, wf_up, wf_skip, wi, wg, pick_skip = pl.pallas_call(
        prepare_kernel,
        out_shape=(
            inside((384, 1024)),
            outside((256, 512)),
            outside((192, 576)),
            outside((192, 576)),
            outside((384, 576)),
            outside((128, 512)),
            inside((256, 768)),
        ),
        in_specs=[VMEM] * 3,
        out_specs=(VMEM,) * 7,
        compiler_params=room(8),
        cost_estimate=pl.CostEstimate(flops=1840000000, bytes_accessed=1000000, transcendentals=0),
        name="prepare",
    )(coarse, w_up, w_conv)
    held, wf_up = lax.optimization_barrier((held, wf_up))
    held_cross = lax.ppermute(held, AXIS, cross_pairs)
    later, edge_core, edge_cross = lax.optimization_barrier((held, edge_core, edge_cross))
    held_core = lax.ppermute(later, AXIS, core_pairs)
    held, held_core, held_cross = [v.reshape(8, 2, 64, 128) for v in (held, held_core, held_cross)]
    xu, pre_up = pl.pallas_call(
        edge_kernel,
        out_shape=(inside((1152, 1024)), inside((256, 1024), F32)),
        in_specs=[VMEM] * 4 + [FAR],
        out_specs=(VMEM,) * 2,
        scratch_shapes=[pltpu.VMEM((192, 576), BF16), pltpu.SemaphoreType.DMA((2,))],
        compiler_params=room(16),
        cost_estimate=pl.CostEstimate(flops=3000000000, bytes_accessed=1000000, transcendentals=0),
        name="edges",
    )(near(edge_core), near(edge_cross), w_up, near(xu), far(wf_up))
    xs, pre, part, half_act, term, wf_skip, spread, wi, wg = pl.pallas_call(
        inner_kernel,
        out_shape=(
            inside((768, 1024)),
            inside((128, 1024), F32),
            inside((256, 1024), F32),
            inside((64, 1024)),
            inside((1152, 192), F32),
            inside((192, 576)),
            inside((256, 512)),
            inside((384, 576)),
            inside((128, 512)),
        ),
        in_specs=[VMEM] * 7 + [FAR] * 4,
        out_specs=(VMEM,) * 9,
        scratch_shapes=[pltpu.VMEM((384, 1024), BF16), pltpu.SemaphoreType.DMA((4,))],
        compiler_params=room(20),
        cost_estimate=pl.CostEstimate(flops=4000000000, bytes_accessed=1000000, transcendentals=0),
        name="inner",
    )(
        *(near(v) for v in (edge_core, held, held_core, flat, pick_skip, xu, pre_up)),
        *(far(v) for v in (wf_skip, spread, wi, wg)),
    )

    scale = 1.0 / math.sqrt(n * planes * cells)
    act, gi, skip_part, keep, send = pl.pallas_call(
        functools.partial(main_kernel, scale),
        out_shape=(
            outside((64, 2048)),
            outside((128, 256)),
            outside((16, 64, 128)),
            inside((1152, 128), F32),
            inside((1152, 128)),
        ),
        in_specs=[VMEM] * 14,
        out_specs=(FAR,) * 3 + (VMEM,) * 2,
        scratch_shapes=[
            pltpu.VMEM((384, 1024), BF16),
            pltpu.VMEM((384, 1024), BF16),
            pltpu.VMEM((2304, 128), F32),
            pltpu.VMEM((256, 1024), F32),
            pltpu.VMEM((64, 1024), BF16),
            pltpu.VMEM((128, 256), BF16),
            pltpu.VMEM((16, 64, 128), BF16),
            pltpu.SemaphoreType.DMA((4,)),
        ],
        compiler_params=room(24),
        cost_estimate=pl.CostEstimate(flops=8280000000, bytes_accessed=1000000, transcendentals=0),
        name="section",
    )(
        *(
            near(v)
            for v in (
                held_cross,
                flat,
                edge_cross,
                pick_skip,
                xs,
                part,
                half_act,
                xu,
                pre,
                term,
                spread,
                wi,
                wf_skip,
                wg,
            )
        ),
    )
    if positions != 64:
        skip_part = skip_part.reshape(16, 64, 2, 64).transpose(1, 2, 0, 3)
        skip_part = skip_part.reshape(64, 2, n, positions).transpose(2, 0, 1, 3)
        skip_part = skip_part.reshape(n, 64, 2 * positions)
    back = lax.all_to_all(skip_part, AXIS, split_axis=0, concat_axis=0, tiled=True)

    def others(back):
        return (
            act.reshape(64, planes, cells),
            gi.reshape(128, 1, 256),
            back.transpose(1, 0, 2).reshape(64, 2 * n, positions),
        )

    grad_w_conv, grad_w_up, rest = reduce_weights(keep, send, back, others, n)
    return (*rest, grad_w_up, grad_w_conv)


def solution(mesh):
    spec = jax.sharding.PartitionSpec
    in_specs = (
        spec("groups", "space", None),
        spec("groups", None, "space"),
        spec("groups", "space", None),
        spec(),
        spec(),
    )
    out_specs = (
        spec("groups", "space", None),
        spec("groups", "space", None),
        spec("groups", None, "space"),
        spec("groups", None, None),
        spec("groups", None, None),
    )
    return jax.shard_map(local, mesh=mesh, in_specs=in_specs, out_specs=out_specs, check_vma=False)
```
